256 devices in a mesh: gx: 32 (over z_hi, x, core), gy: 8 (over z_lo, y).
Axes of the slice: x: 4, y: 4, z: 8 (z_hi: 4, z_lo: 2; z = z_hi * 2 + z_lo), core: 2. Of those that a mesh axis runs over, the one named last changes fastest.
Arguments:
- checkpoint: float32 [19, 256, 2048], P(None, 'gx', 'gy'), as said below
- cotangent: float32 [19, 256, 2048], P(None, 'gx', 'gy'), may hold values from -6 to 6
- blade_area: float32 [1536], replicated, may hold values from 0.5 to 2
- hub_tile: int32 [16], replicated, may hold values from 0 to 255
- point_side: int32 [1536], replicated, may hold values from 0 to 8
- point_local: int32 [1536], replicated, may hold values from 0 to 2047
Outputs:
- grad_checkpoint: float32 [19, 256, 2048], P(None, 'gx', 'gy')
- grad_area: float32 [1536], replicated
The draws below stay inside these ranges and needn't reach their ends.
Inputs may be any that keep to these rules, and one draw needn't show every extreme that they name: `hub_tile`: tile ids count every tile of the slab. `point_side`: every actuator point lies in its hub tile or one of the eight tiles around it. `checkpoint`: populations are positive and near a local equilibrium with density near one and streamwise velocity near 0.08.
All inputs are finite; a program needn't handle non-finite values.
Results may differ from the reference program's by a relative error of at most 0.0003.
Values sent between devices are 32-bit elements; how exact they have to be, the bound alone decides.
No kernel may reach another device: no remote copies, remote signals or barrier semaphores. Data moves between devices by JAX's collectives and lax.ppermute only.
A program may use at most 128 MiB of HBM per device.

```python
import math
import jax
import jax.numpy as jnp
import numpy as np
from jax import lax

CX = 8
CY = 16
NZ = 16
STEPS = 4
NTURB = 16
PTS = 96
NX = 256
NY = 128
NPTS = 1536
N_GX = 32
N_GY = 8


def draw_lattice():
    axis_part = [(1, 0, 0), (-1, 0, 0), (0, 1, 0), (0, -1, 0), (0, 0, 1), (0, 0, -1)]
    edge_part = [(1, 1, 0), (-1, -1, 0), (1, -1, 0), (-1, 1, 0), (1, 0, 1), (-1, 0, -1), (1, 0, -1), (-1, 0, 1), (0, 1, 1), (0, -1, -1), (0, 1, -1), (0, -1, 1)]
    vectors = np.array([(0, 0, 0)] + axis_part + edge_part) * 1.0
    weights = np.array([1.0 / 3.0] + [1.0 / 18.0] * 6 + [1.0 / 36.0] * 12)
    return (jnp.asarray(vectors, jnp.float32), jnp.asarray(weights, jnp.float32))


def draw_checkpoint(key, part):
    vectors, weights = draw_lattice()
    keys = jax.random.split(key, 5)
    shape = (NX, NY * NZ)
    noises = [jnp.clip(jax.random.normal(keys[column], shape, jnp.float32), -3.0, 3.0) for column in range(4)]
    baseline = 0.08
    perturb = 0.1 * jnp.clip(jax.random.normal(keys[4], (19,) + shape, jnp.float32), -2.0, 2.0)
    density = 1.0 + 0.04 * noises[0]
    velocity_x = baseline + 0.03 * noises[1]
    velocity_y = 0.03 * noises[2]
    velocity_z = 0.02 * noises[3]
    project = vectors[:, 0, None, None] * velocity_x[None] + vectors[:, 1, None, None] * velocity_y[None] + vectors[:, 2, None, None] * velocity_z[None]
    speed_sq = velocity_x * velocity_x + velocity_y * velocity_y + velocity_z * velocity_z
    equil = weights[:, None, None] * density[None] * (1.0 + 3.0 * project + 4.5 * project * project - 1.5 * speed_sq[None])
    return (equil * (1.0 + perturb)).astype(jnp.float32)


def place_ends(entries, stream_key, smallest, high):
    place = [jax.random.randint(jax.random.fold_in(stream_key, axis), (), 0, length) for axis, length in enumerate(entries.shape)]
    longest = entries.shape.index(max(entries.shape))
    neighbour = place[:longest] + [(place[longest] + 1) % entries.shape[longest]] + place[longest + 1:]
    return entries.at[tuple(place)].set(smallest).at[tuple(neighbour)].set(high)


def shard_levels(rng, shape, cuts, smallest, high):
    gain = 1.0
    for dim, blocks in cuts:
        draws = jax.random.uniform(jax.random.fold_in(jax.random.fold_in(rng, 6), dim), (blocks,), jnp.float32, smallest / len(cuts), high / len(cuts))
        gain = gain * jnp.repeat(jnp.exp(draws), shape[dim] // blocks).reshape((-1,) + (1,) * (len(shape) - 1 - dim))
    return gain


def bell_draw(stream_key, shape, scale, bound, cuts=(), held_as=jnp.bfloat16):
    values = jax.random.normal(stream_key, shape, jnp.float32) * scale
    if len(cuts) > 0:
        values = shard_levels(stream_key, shape, cuts, -0.22, 0.18) * values
    return jnp.clip(values, min=-bound, max=bound).astype(held_as)


def setup_inputs(seed: int = 0) -> dict:
    key_list = jax.random.split(jax.random.key(seed), 7)
    checkpoint = draw_checkpoint(jax.random.fold_in(key_list[6], 71), 0)
    cotangent = bell_draw(key_list[1], (19, NX, NY * NZ), 1.0, 6.0, ((1, 32), (2, 8)), jnp.float32)
    blade_area = jnp.clip(jnp.exp(jax.random.uniform(key_list[2], (NPTS,), jnp.float32, math.log(0.5), math.log(2.0))), 0.5, 2.0)
    hub_tile = place_ends(jax.random.randint(key_list[3], (NTURB,), 0, N_GX * N_GY), jax.random.fold_in(key_list[3], 1), 0, (N_GX * N_GY) - 1).astype(jnp.int32)
    point_side = place_ends(jax.random.randint(key_list[4], (NPTS,), 0, 9), jax.random.fold_in(key_list[4], 1), 0, 8).astype(jnp.int32)
    point_local = place_ends(jax.random.randint(key_list[5], (NPTS,), 0, CX * CY * NZ), jax.random.fold_in(key_list[5], 1), 0, (CX * CY * NZ) - 1).astype(jnp.int32)
    return {"checkpoint": checkpoint, "cotangent": cotangent, "blade_area": blade_area, "hub_tile": hub_tile, "point_side": point_side, "point_local": point_local}


TAU_ZERO = 0.52
SMAGORINSKY = 0.17 * 0.17
TINY = 1e-10
THRUST = 4.0
GHOST_RATES = np.array([1.05, 1.15, 1.25, 1.35, 1.45, 1.55, 1.65, 1.75, 1.85])

def lattice():
    axis_part = [(1, 0, 0), (-1, 0, 0), (0, 1, 0), (0, -1, 0), (0, 0, 1), (0, 0, -1)]
    edge_part = [(1, 1, 0), (-1, -1, 0), (1, -1, 0), (-1, 1, 0), (1, 0, 1), (-1, 0, -1), (1, 0, -1), (-1, 0, 1), (0, 1, 1), (0, -1, -1), (0, 1, -1), (0, -1, 1)]
    vectors = np.array([(0, 0, 0)] + axis_part + edge_part) * 1.0
    weights = np.array([1.0 / 3.0] + [1.0 / 18.0] * 6 + [1.0 / 36.0] * 12)
    opposite = np.array([int(np.argmin(np.abs(vectors + vectors[column]).sum(1))) for column in range(19)])
    return (vectors, weights, opposite)

def orthonormal(monomials, weights):
    rows = []
    for entry in monomials:
        vector = entry * 1.0
        for sweep in range(2):
            for other in rows:
                vector = vector - np.sum(weights * vector * other) * other
        vector = vector / np.sqrt(np.sum(weights * vector * vector))
        rows.append(vector)
    return np.stack(rows, 0)

def tables():
    vectors, weights, opposite = lattice()
    along_x, along_y, along_z = (vectors[:, 0], vectors[:, 1], vectors[:, 2])
    monomials = [np.ones(19), along_x, along_y, along_z, along_x * along_x, along_y * along_y, along_z * along_z, along_x * along_y, along_x * along_z, along_y * along_z, along_x * along_y * along_y, along_x * along_z * along_z, along_y * along_x * along_x, along_y * along_z * along_z, along_z * along_x * along_x, along_z * along_y * along_y, along_x * along_x * along_y * along_y, along_x * along_x * along_z * along_z, along_y * along_y * along_z * along_z]
    basis = orthonormal(monomials, weights)
    second = weights[:, None] * basis[4:10].T
    ghost = weights[:, None] * basis[10:].T * GHOST_RATES[None, :]
    stress = np.stack([along_x * along_x, along_y * along_y, along_z * along_z, along_x * along_y, along_x * along_z, along_y * along_z], 0)
    push = 3.0 * weights * along_x
    return {'vectors': vectors, 'weights': weights, 'opposite': opposite, 'high': jnp.asarray(basis[4:], jnp.float32), 'second': jnp.asarray(second, jnp.float32), 'ghost': jnp.asarray(ghost, jnp.float32), 'stress': jnp.asarray(stress, jnp.float32), 'push': jnp.asarray(push, jnp.float32), 'velt': jnp.asarray(vectors.T, jnp.float32), 'wvec': jnp.asarray(weights, jnp.float32), 'vecs': jnp.asarray(vectors, jnp.float32)}

def streamwise_velocity(flat, table):
    density = lax.optimization_barrier(jnp.sum(flat, 0))
    momentum = jnp.dot(table['velt'], flat, precision=lax.Precision.HIGHEST)
    return momentum[0] / density

def collide(flat, force, table):
    density = lax.optimization_barrier(jnp.sum(flat, 0))
    momentum = jnp.dot(table['velt'], flat, precision=lax.Precision.HIGHEST)
    velocity = momentum / density[None, :]
    project = jnp.dot(table['vecs'], velocity, precision=lax.Precision.HIGHEST)
    speed_sq = lax.optimization_barrier(jnp.sum(velocity * velocity, 0))
    equil = table['wvec'][:, None] * density[None, :] * (1.0 + 3.0 * project + 4.5 * project * project - 1.5 * speed_sq[None, :])
    noneq = flat - equil
    stress = jnp.dot(table['stress'], noneq, precision=lax.Precision.HIGHEST)
    square = lax.optimization_barrier(jnp.sum(stress[:3] * stress[:3], 0)) + 2.0 * lax.optimization_barrier(jnp.sum(stress[3:] * stress[3:], 0))
    relax_time = 0.5 * (TAU_ZERO + jnp.sqrt(TAU_ZERO * TAU_ZERO + 18.0 * SMAGORINSKY * jnp.sqrt(square + TINY) / density))
    moments = jnp.dot(table['high'], noneq, precision=lax.Precision.HIGHEST)
    relaxed = jnp.dot(table['second'], moments[:6] / relax_time[None, :], precision=lax.Precision.HIGHEST)
    relaxed = relaxed + jnp.dot(table['ghost'], moments[6:], precision=lax.Precision.HIGHEST)
    return flat - relaxed + table['push'][:, None] * force[None, :]

def wall_mask(vectors, depth):
    keep = np.ones((19, depth))
    for column in range(19):
        if vectors[column, 2] > 0.5:
            keep[column, 0] = 0.0
        if vectors[column, 2] < -0.5:
            keep[column, depth - 1] = 0.0
    return keep

def reference(checkpoint, cotangent, blade_area, hub_tile, point_side, point_local):
    table = tables()
    vectors = table['vectors']
    opposite = table['opposite']
    keep = jnp.asarray(wall_mask(vectors, NZ), jnp.float32)[:, None, None, :]
    turbine = jnp.arange(NTURB * PTS, dtype=jnp.int32) // PTS
    hub_x = hub_tile // N_GY
    hub_y = hub_tile % N_GY
    tile_x = (hub_x[turbine] + point_side // 3 - 1) % N_GX
    tile_y = (hub_y[turbine] + point_side % 3 - 1) % N_GY
    local_x = point_local // (CY * NZ)
    local_y = point_local // NZ % CY
    local_z = point_local % NZ
    cell = (((tile_x * CX + local_x) * NY + tile_y * CY + local_y) * NZ + local_z).astype(jnp.int32)

    def advance(state, area):
        field = state.reshape(19, NX, NY, NZ)
        pulled = jnp.stack([jnp.roll(field[column], (int(vectors[column, 0]), int(vectors[column, 1]), int(vectors[column, 2])), (0, 1, 2)) for column in range(19)], 0)
        read = pulled * keep + (1.0 - keep) * field[opposite]
        flat = read.reshape(19, NX * NY * NZ)
        sampled = streamwise_velocity(flat, table)[cell]
        numer = lax.optimization_barrier(jnp.sum((area * sampled).reshape(NTURB, PTS), 1))
        rotor = numer / lax.optimization_barrier(jnp.sum(area.reshape(NTURB, PTS), 1))
        thrust = -THRUST * area * rotor[turbine] * sampled
        force = jnp.zeros((NX * NY * NZ,), jnp.float32).at[cell].add(thrust)
        return collide(flat, force, table).reshape(19, NX, NY * NZ)

    def run(state, area):
        for counter in range(STEPS):
            state = jax.checkpoint(advance)(state, area)
        return state
    final, pullback = jax.vjp(run, checkpoint, blade_area)
    grads = pullback(cotangent)
    return (grads[0], grads[1])
```

```python
import functools

import jax
import jax.numpy as jnp
import numpy as np
from jax import lax
from jax.experimental import pallas as pl
from jax.experimental.pallas import tpu as pltpu
from jax.sharding import PartitionSpec as P

NZ = 16
CX = 8
CY = 16
STEPS = 4
NTURB = 16
PTS = 96
MARGIN = 8
RX = CX + 2 * MARGIN
RY = CY + 2 * MARGIN
LANES = RY * NZ
OWN_ROWS = slice(MARGIN, MARGIN + CX)
OWN_LANE = MARGIN * NZ
OWN_SPAN = CY * NZ

TAU_ZERO = 0.52
SMAGORINSKY = 0.17 * 0.17
TINY = 1e-10
THRUST = 4.0
GHOST_RATES = np.array([1.05, 1.15, 1.25, 1.35, 1.45, 1.55, 1.65, 1.75, 1.85])
W_REST, W_AXIS, W_EDGE = 1.0 / 3.0, 1.0 / 18.0, 1.0 / 36.0

VECTORS = np.array(
    [(0, 0, 0), (1, 0, 0), (-1, 0, 0), (0, 1, 0), (0, -1, 0), (0, 0, 1), (0, 0, -1)]
    + [(1, 1, 0), (-1, -1, 0), (1, -1, 0), (-1, 1, 0), (1, 0, 1), (-1, 0, -1)]
    + [(1, 0, -1), (-1, 0, 1), (0, 1, 1), (0, -1, -1), (0, 1, -1), (0, -1, 1)]
)
OPPOSITE = [0] + [i + 1 if i % 2 else i - 1 for i in range(1, 19)]


def basis():
    c = VECTORS * 1.0
    weights = np.array([W_REST] + [W_AXIS] * 6 + [W_EDGE] * 12)
    x, y, z = c[:, 0], c[:, 1], c[:, 2]
    monomials = [np.ones(19), x, y, z, x * x, y * y, z * z, x * y, x * z, y * z]
    monomials += [x * y * y, x * z * z, y * x * x, y * z * z, z * x * x, z * y * y]
    monomials += [x * x * y * y, x * x * z * z, y * y * z * z]
    rows = []
    for entry in monomials:
        vector = entry * 1.0
        for sweep in range(2):
            for other in rows:
                vector = vector - np.sum(weights * vector * other) * other
        rows.append(vector / np.sqrt(np.sum(weights * vector * vector)))
    return np.stack(rows, 0)


def ghost_tables():
    rows = basis()
    odd = []
    for first, members in ((10, (1, 7, 11)), (12, (3, 7, 15)), (14, (5, 11, 15))):
        h = rows[first : first + 2][:, list(members)]
        rates = GHOST_RATES[first - 10 : first - 8]
        odd.append(np.diag([W_AXIS, W_EDGE, W_EDGE]) @ h.T @ np.diag(rates) @ h)
    even = rows[16:19][:, [0, 1, 3, 5, 7, 11, 15]]
    return odd, even, GHOST_RATES[6:9]


ODD, EVEN, EVEN_RATES = ghost_tables()
CLASS_W = [W_REST] + [W_AXIS] * 3 + [W_EDGE] * 3


def combine(coefs, values):
    total = None
    for coef, value in zip(coefs, values):
        coef = float(coef)
        if abs(coef) < 1e-12:
            continue
        term = value if coef == 1.0 else value * coef
        total = term if total is None else total + term
    return total


def split_parity(s):
    e = [s[i] + s[i + 1] for i in range(1, 19, 2)]
    o = [s[i] - s[i + 1] for i in range(1, 19, 2)]
    even = [s[0], e[0], e[1], e[2], e[3] + e[4], e[5] + e[6], e[7] + e[8]]
    cross = [e[3] - e[4], e[5] - e[6], e[7] - e[8]]
    odd_x = [o[0], o[3] + o[4], o[5] + o[6]]
    odd_y = [o[1], o[3] - o[4], o[7] + o[8]]
    odd_z = [o[2], o[5] - o[6], o[7] - o[8]]
    return even, cross, odd_x, odd_y, odd_z


def merge_parity(s, even, cross, odd_x, odd_y, odd_z):
    out = [s[0] + even[0]]
    for axis, odd in enumerate((odd_x, odd_y, odd_z)):
        out += [s[1 + 2 * axis] + (even[1 + axis] + odd[0])]
        out += [s[2 + 2 * axis] + (even[1 + axis] - odd[0])]
    pairs = ((odd_x[1], odd_y[1]), (odd_x[2], odd_z[1]), (odd_y[2], odd_z[2]))
    for family in range(3):
        first, second = pairs[family]
        base = 7 + 4 * family
        for sign, offset in ((1, 0), (-1, 2)):
            level = even[4 + family] + cross[family] if sign > 0 else even[4 + family] - cross[family]
            swing = first + second if sign > 0 else first - second
            out += [s[base + offset] + (level + swing), s[base + offset + 1] + (level - swing)]
    return out


def ghost_even(even, transpose):
    if transpose:
        even = [value * w for value, w in zip(even, CLASS_W)]
    m = [combine(EVEN[k], even) * float(EVEN_RATES[k]) for k in range(3)]
    out = [combine(EVEN[:, j], m) for j in range(7)]
    if not transpose:
        out = [value * w for value, w in zip(out, CLASS_W)]
    return out


def ghost_odd(index, odd, transpose):
    matrix = ODD[index].T if transpose else ODD[index]
    return [combine(matrix[j], odd) for j in range(3)]


def local_state(even, cross, odds):
    rho = ((even[0] + even[1]) + (even[2] + even[3])) + ((even[4] + even[5]) + even[6])
    inverse = 1.0 / rho
    mom = [(odd[0] + odd[1]) + odd[2] for odd in odds]
    u = [m * inverse for m in mom]
    third = rho * (1.0 / 3.0)
    edges = ((even[4], even[5]), (even[4], even[6]), (even[5], even[6]))
    stress = [
        ((even[1 + a] + edges[a][0]) + edges[a][1]) - third - mom[a] * u[a] for a in range(3)
    ]
    stress += [cross[0] - mom[0] * u[1], cross[1] - mom[0] * u[2], cross[2] - mom[1] * u[2]]
    square = stress[0] * stress[0] + stress[1] * stress[1] + stress[2] * stress[2]
    square = square + 2.0 * (
        stress[3] * stress[3] + stress[4] * stress[4] + stress[5] * stress[5]
    )
    norm = jnp.sqrt(square + TINY)
    root = jnp.sqrt(TAU_ZERO * TAU_ZERO + (18.0 * SMAGORINSKY) * norm * inverse)
    tau = 0.5 * (TAU_ZERO + root)
    return inverse, u, stress, norm, root, tau


def collide(s, force):
    even, cross, odd_x, odd_y, odd_z = split_parity(s)
    inverse, u, stress, norm, root, tau = local_state(even, cross, (odd_x, odd_y, odd_z))
    scale = 4.5 / tau
    k = [value * scale for value in stress]
    trace = (k[0] + k[1] + k[2]) * (1.0 / 3.0)
    relax = [-trace, k[0] - trace, k[1] - trace, k[2] - trace]
    relax += [k[0] + relax[2], k[0] + relax[3], k[1] + relax[3]]
    ghost = ghost_even(even, False)
    even_out = [-(relax[j] * CLASS_W[j] + ghost[j]) for j in range(7)]
    cross_out = [k[3 + j] * (-2.0 * W_EDGE) for j in range(3)]
    gx = ghost_odd(0, odd_x, False)
    ox = [force * (1.0 / 6.0) - gx[0], force * (1.0 / 12.0) - gx[1], force * (1.0 / 12.0) - gx[2]]
    oy = [-value for value in ghost_odd(1, odd_y, False)]
    oz = [-value for value in ghost_odd(2, odd_z, False)]
    return merge_parity(s, even_out, cross_out, ox, oy, oz)


def collide_adjoint(s, a, speed_bar):
    even, cross, odd_x, odd_y, odd_z = split_parity(s)
    inverse, u, stress, norm, root, tau = local_state(even, cross, (odd_x, odd_y, odd_z))
    ev, cr, ax, ay, az = split_parity(a)
    weighted = [value * w for value, w in zip(ev, CLASS_W)]
    total = ((weighted[0] + weighted[1]) + (weighted[2] + weighted[3])) + (
        (weighted[4] + weighted[5]) + weighted[6]
    )
    third = total * (1.0 / 3.0)
    edges = ((4, 5), (4, 6), (5, 6))
    beta = [
        (weighted[1 + i] + weighted[edges[i][0]] + weighted[edges[i][1]] - third) * -4.5
        for i in range(3)
    ]
    beta += [value * (-9.0 * W_EDGE) for value in cr]
    inv_tau = 1.0 / tau
    dot = (beta[0] * stress[0] + beta[1] * stress[1] + beta[2] * stress[2]) + (
        beta[3] * stress[3] + beta[4] * stress[4] + beta[5] * stress[5]
    )
    tau_bar = -dot * inv_tau * inv_tau
    common = tau_bar * (4.5 * SMAGORINSKY) * inverse / root
    factor = common / norm
    p_bar = [beta[i] * inv_tau + stress[i] * factor for i in range(3)]
    twice = factor + factor
    p_bar += [beta[i] * inv_tau + stress[i] * twice for i in range(3, 6)]
    sp = speed_bar * inverse
    px, py, pz, pxy, pxz, pyz = p_bar
    tx = pxy * u[1] + pxz * u[2]
    ty = pyz * u[2]
    mx = sp - (2.0 * px * u[0] + tx)
    my = -(2.0 * py * u[1] + pxy * u[0] + ty)
    mz = -(2.0 * pz * u[2] + pxz * u[0] + pyz * u[1])
    rho_bar = -common * norm * inverse - (px + py + pz) * (1.0 / 3.0)
    rho_bar = rho_bar + (px * u[0] + tx) * u[0] + (py * u[1] + ty) * u[1] + pz * u[2] * u[2]
    rho_bar = rho_bar - sp * u[0]
    ghost = ghost_even(ev, True)
    level = [rho_bar, rho_bar + px, rho_bar + py, rho_bar + pz]
    level += [level[1] + py, level[1] + pz, level[2] + pz]
    even_out = [level[j] - ghost[j] for j in range(7)]
    gx, gy, gz = (ghost_odd(i, odd, True) for i, odd in enumerate((ax, ay, az)))
    ox = [mx - value for value in gx]
    oy = [my - value for value in gy]
    oz = [mz - value for value in gz]
    return merge_parity(a, even_out, p_bar[3:], ox, oy, oz)


def chunks(body):
    def step(index, carry):
        lane = pl.multiple_of(index * 128, 128)
        for row in range(0, RX, 8):
            body(pl.ds(row, 8), pl.ds(lane, 128))
        return carry

    lax.fori_loop(0, LANES // 128, step, 0)


def shifted(value, cx, cy, cz):
    lane = (NZ * cy + cz) % LANES
    if lane:
        value = pltpu.roll(value, lane, 1)
    if cx % RX:
        value = pltpu.roll(value, cx % RX, 0)
    return value


def height():
    return lax.broadcasted_iota(jnp.int32, (RX, LANES), 1) & (NZ - 1)


def stream(field, out):
    z = height()
    for i in range(19):
        cx, cy, cz = (int(v) for v in VECTORS[i])
        value = shifted(field[i], cx, cy, cz)
        if cz:
            value = jnp.where(z == (0 if cz > 0 else NZ - 1), field[OPPOSITE[i]], value)
        out[i] = value


def stream_adjoint(field, out):
    z = height()
    for i in range(19):
        cx, cy, cz = (int(v) for v in VECTORS[i])
        value = field[i]
        if cz:
            value = jnp.where(z == (0 if cz > 0 else NZ - 1), 0.0, value)
        value = shifted(value, -cx, -cy, -cz)
        if cz:
            value = value + jnp.where(z == (NZ - 1 if cz > 0 else 0), field[OPPOSITE[i]], 0.0)
        out[i] = value


def speeds(s_ref, v_ref):
    def one(rows, lanes):
        s = [s_ref[i, rows, lanes] for i in range(19)]
        even, cross, odd_x, odd_y, odd_z = split_parity(s)
        rho = ((even[0] + even[1]) + (even[2] + even[3])) + ((even[4] + even[5]) + even[6])
        v_ref[rows, lanes] = ((odd_x[0] + odd_x[1]) + odd_x[2]) / rho

    chunks(one)


def push_back(a):
    odd = (a[7] - a[8]) + (a[9] - a[10]) + (a[11] - a[12]) + (a[13] - a[14])
    return (a[1] - a[2]) * (1.0 / 6.0) + odd * (1.0 / 12.0)


def turbine_sums(area_ref, field_ref, sums_ref, out_ref, base):
    parts = [field_ref[OWN_ROWS, OWN_LANE + j : OWN_LANE + j + 128] for j in range(0, OWN_SPAN, 128)]
    for t in range(NTURB):
        total = None
        for j, part in enumerate(parts):
            lane = OWN_LANE + 128 * j
            term = area_ref[t, OWN_ROWS, lane : lane + 128] * part
            total = term if total is None else total + term
        sums_ref[t : t + 1, :] = jnp.sum(total, axis=0, keepdims=True)
    row = jnp.sum(sums_ref[...], axis=1, keepdims=True)
    out_ref[base : base + NTURB, :] = jnp.broadcast_to(row, (NTURB, 128))


def weighted_area(area_ref, weight_ref, rows, lanes):
    total = None
    for t in range(NTURB):
        term = area_ref[t, rows, lanes] * weight_ref[t : t + 1, :]
        total = term if total is None else total + term
    return total


def area_kernel(x_ref, yz_ref, area_ref, out_ref):
    rows = lax.broadcasted_iota(jnp.int32, (RX, PTS), 0)
    columns = lax.broadcasted_iota(jnp.int32, (LANES, PTS), 0)
    for t in range(NTURB):
        area = area_ref[t : t + 1, :]
        spread = jnp.where(rows == x_ref[t : t + 1, :], area, 0.0)
        high = spread.astype(jnp.bfloat16)
        rest = spread - high.astype(jnp.float32)
        middle = rest.astype(jnp.bfloat16)
        low = (rest - middle.astype(jnp.float32)).astype(jnp.bfloat16)
        hot = jnp.where(columns == yz_ref[t : t + 1, :], 1.0, 0.0).astype(jnp.bfloat16)
        left = jnp.concatenate([high, middle, low], axis=0)
        product = lax.dot_general(
            left, hot, (((1,), (1,)), ((), ())), preferred_element_type=jnp.float32
        )
        out_ref[t] = product[:RX] + product[RX : 2 * RX] + product[2 * RX :]


def first_kernel(field_ref, area_ref, s_ref, v_ref, sum_ref, sums):
    stream(field_ref, s_ref)
    speeds(s_ref, v_ref)
    turbine_sums(area_ref, v_ref, sums, sum_ref, 0)


def forward_kernel(last, s_ref, v_ref, area_ref, rotor_ref, *rest):
    if last:
        cot_ref, next_ref, vn_ref, sum_ref, field, drag, sums = rest
    else:
        next_ref, vn_ref, sum_ref, field, sums = rest

    def one(rows, lanes):
        s = [s_ref[i, rows, lanes] for i in range(19)]
        force = weighted_area(area_ref, rotor_ref, rows, lanes) * v_ref[rows, lanes] * -THRUST
        for i, value in enumerate(collide(s, force)):
            field[i, rows, lanes] = value

    chunks(one)
    stream(field, next_ref)
    speeds(next_ref, vn_ref)
    turbine_sums(area_ref, vn_ref, sums, sum_ref, 0)
    if last:

        def other(rows, lanes):
            a = [cot_ref[i, rows, lanes] for i in range(19)]
            drag[rows, lanes] = push_back(a) * vn_ref[rows, lanes] * -THRUST

        chunks(other)
        turbine_sums(area_ref, drag, sums, sum_ref, NTURB)


def adjoint_field(s_ref, a_ref, area_ref, rotor_ref, bar_ref, field):
    def one(rows, lanes):
        s = [s_ref[i, rows, lanes] for i in range(19)]
        a = [a_ref[i, rows, lanes] for i in range(19)]
        speed_bar = weighted_area(area_ref, rotor_ref, rows, lanes) * push_back(a) * -THRUST
        speed_bar = speed_bar + weighted_area(area_ref, bar_ref, rows, lanes)
        for i, value in enumerate(collide_adjoint(s, a, speed_bar)):
            field[i, rows, lanes] = value

    chunks(one)


def backward_kernel(s_ref, a_ref, area_ref, rotor_ref, bar_ref, v_ref, out_ref, drag_ref, sum_ref, field, sums):
    adjoint_field(s_ref, a_ref, area_ref, rotor_ref, bar_ref, field)
    stream_adjoint(field, out_ref)

    def other(rows, lanes):
        a = [out_ref[i, rows, lanes] for i in range(19)]
        drag_ref[rows, lanes] = push_back(a) * v_ref[rows, lanes] * -THRUST

    chunks(other)
    turbine_sums(area_ref, drag_ref, sums, sum_ref, 0)


def last_kernel(s_ref, a_ref, area_ref, rotor_ref, bar_ref, out_ref, field, result):
    adjoint_field(s_ref, a_ref, area_ref, rotor_ref, bar_ref, field)
    stream_adjoint(field, result)
    for i in range(19):
        out_ref[i] = result[i, OWN_ROWS, OWN_LANE : OWN_LANE + OWN_SPAN]


def gather_kernel(x_ref, yz_ref, cot_ref, q1, q2, q3, v1, v2, v3, v4, u1, u2, u3, u4, n2, n3, n4, inv, out_ref):
    own = (OWN_ROWS, slice(OWN_LANE, OWN_LANE + OWN_SPAN))
    v = [ref[own] for ref in (v1, v2, v3, v4)]
    q = [ref[own] for ref in (q1, q2, q3)]
    a = [cot_ref[(i,) + own] for i in range(19)]
    q.append(push_back(a) * v[3] * -THRUST)
    rows = lax.broadcasted_iota(jnp.int32, (CX, PTS), 0) + MARGIN
    columns = lax.broadcasted_iota(jnp.int32, (OWN_SPAN, PTS), 0) + OWN_LANE

    def wide(ref, t):
        return jnp.concatenate([ref[t : t + 1, :]] * (OWN_SPAN // 128), axis=1)

    for t in range(NTURB):
        u = [wide(ref, t) for ref in (u1, u2, u3, u4)]
        n = [None] + [wide(ref, t) for ref in (n2, n3, n4)]
        known = u[0] * q[0]
        for k in range(1, 4):
            known = known + u[k] * q[k] + n[k] * (v[k] - u[k])
        fields = [known, q[0], (v[0] - u[0]) * wide(inv, t)]
        stack = jnp.concatenate(fields, axis=0)
        high = stack.astype(jnp.bfloat16)
        rest = stack - high.astype(jnp.float32)
        middle = rest.astype(jnp.bfloat16)
        low = (rest - middle.astype(jnp.float32)).astype(jnp.bfloat16)
        hot = jnp.where(columns == yz_ref[t : t + 1, :], 1.0, 0.0).astype(jnp.bfloat16)
        product = sum(
            jnp.dot(part, hot, preferred_element_type=jnp.float32) for part in (low, middle, high)
        )
        mine = rows == x_ref[t : t + 1, :]
        for j in range(3):
            picked = jnp.where(mine, product[CX * j : CX * (j + 1)], 0.0)
            out_ref[j * NTURB + t : j * NTURB + t + 1, 0:PTS] = jnp.sum(picked, axis=0, keepdims=True)
    out_ref[:, PTS:128] = jnp.zeros((3 * NTURB, 128 - PTS), jnp.float32)


def call(kernel, outs, scratch, *args):
    vmem = pl.BlockSpec(memory_space=pltpu.VMEM)
    return pl.pallas_call(
        kernel,
        out_shape=[jax.ShapeDtypeStruct(shape, jnp.float32) for shape in outs],
        in_specs=[vmem] * len(args),
        out_specs=[vmem] * len(outs),
        scratch_shapes=[pltpu.VMEM(shape, jnp.float32) for shape in scratch],
        compiler_params=pltpu.CompilerParams(vmem_limit_bytes=32 * 1024 * 1024),
    )(*args)


def shift(value, axis, step):
    size = lax.axis_size(axis)
    return lax.ppermute(value, axis, [(i, (i + step) % size) for i in range(size)])


def window(value):
    for axis in ("gx", "gy"):
        left, right = shift(value, axis, 1), shift(value, axis, -1)
        low, high = left + value, value + right
        value = low + right + shift(low, axis, 2) + shift(high, axis, -2)
    return value


def spread(value):
    for axis, step in (("gy", 1), ("gy", 3), ("gx", 1), ("gx", 3), ("gx", 9), ("gx", 3)):
        other = [shift(value, axis, step), shift(value, axis, -step)]
        for part in other:
            value = jnp.where(value != 0.0, value, part)
    return value


def region(value):
    before, after = shift(value, "gx", 1), shift(value, "gx", -1)
    value = jnp.concatenate([before, value, after], axis=1)
    edge = MARGIN * NZ
    span = value.shape[2]
    before = shift(value[:, :, span - edge :], "gy", 1)
    after = shift(value[:, :, :edge], "gy", -1)
    return jnp.concatenate([before, value, after], axis=2)


def body(checkpoint, cotangent, blade_area, hub_tile, point_side, point_local):
    count_x, count_y = lax.axis_size("gx"), lax.axis_size("gy")
    index_x, index_y = lax.axis_index("gx"), lax.axis_index("gy")
    area = blade_area.reshape(NTURB, PTS)
    side = point_side.reshape(NTURB, PTS)
    local = point_local.reshape(NTURB, PTS)
    hub = hub_tile.reshape(NTURB, 1)
    cell_x = (hub // count_y + side // 3 - 1 - index_x) * CX + local // (CY * NZ) + MARGIN
    cell_y = (hub % count_y + side % 3 - 1 - index_y) * CY + local // NZ % CY + MARGIN
    cell_x = cell_x % (count_x * CX)
    cell_y = cell_y % (count_y * CY)
    inside = (cell_x < RX) & (cell_y < RY)
    cell_x = jnp.where(inside, cell_x, -1)
    cell_yz = jnp.where(inside, cell_y * NZ + local % NZ, -1)
    mine_y = (cell_y >= MARGIN) & (cell_y < MARGIN + CY)
    inverse = jnp.broadcast_to(1.0 / jnp.sum(area, 1, keepdims=True), (NTURB, 128))

    full = (19, RX, LANES)
    flat = (RX, LANES)
    row = (NTURB, 128)
    both = region(jnp.concatenate([checkpoint, cotangent], 0))
    field, cot = both[:19], both[19:]
    (spots,) = call(area_kernel, [(NTURB,) + flat], [], cell_x, cell_yz, area)

    s, v, rotor = [None] * 5, [None] * 5, [None] * 5
    s[1], v[1], sums = call(first_kernel, [full, flat, row], [row], field, spots)
    for k in (1, 2, 3):
        rotor[k] = window(sums) * inverse
        last = k == 3
        outs = [full, flat, (2 * NTURB, 128) if last else row]
        s[k + 1], v[k + 1], sums = call(
            functools.partial(forward_kernel, last),
            outs,
            [full] + ([flat] if last else []) + [row],
            *([s[k], v[k], spots, rotor[k]] + ([cot] if last else [])),
        )
    sums = window(sums)
    rotor[4] = sums[:NTURB] * inverse
    sums = sums[NTURB:]
    adjoint = cot
    bar, drag = [None] * 5, [None] * 5
    for k in (4, 3, 2):
        bar[k] = (window(sums) if k < 4 else sums) * inverse
        adjoint, drag[k - 1], sums = call(
            backward_kernel,
            [full, flat, row],
            [full, row],
            *(s[k], adjoint, spots, rotor[k], bar[k], v[k - 1]),
        )
    (points,) = call(
        gather_kernel,
        [(3 * NTURB, 128)],
        [],
        *([cell_x, jnp.where(mine_y, cell_yz, -1), cot] + drag[1:4] + v[1:] + rotor[1:] + bar[2:] + [inverse]),
    )
    points = spread(points)[:, :PTS]
    known, swing, slope = points[:NTURB], points[NTURB : 2 * NTURB], points[2 * NTURB :]
    total = jnp.sum(area * swing, 1, keepdims=True)
    grad_area = (known + total * slope).reshape(-1)
    bar[1] = total * inverse
    (grad,) = call(
        last_kernel,
        [(19, CX, CY * NZ)],
        [full, full],
        *(s[1], adjoint, spots, rotor[1], bar[1]),
    )
    return grad, grad_area


def solution(mesh):
    return jax.shard_map(
        body,
        mesh=mesh,
        in_specs=(P(None, "gx", "gy"), P(None, "gx", "gy"), P(), P(), P(), P()),
        out_specs=(P(None, "gx", "gy"), P()),
        check_vma=False,
    )
```

```python
import functools

import jax
import jax.numpy as jnp
import numpy as np
from jax import lax
from jax.experimental import pallas as pl
from jax.experimental.pallas import tpu as pltpu
from jax.sharding import PartitionSpec as P

NZ = 16
CX = 8
CY = 16
STEPS = 4
NTURB = 16
PTS = 96
MARGIN = 8
RX = CX + 2 * MARGIN
RY = CY + 2 * MARGIN
LANES = RY * NZ
OWN_ROWS = slice(MARGIN, MARGIN + CX)
OWN_LANE = MARGIN * NZ
OWN_SPAN = CY * NZ

TAU_ZERO = 0.52
SMAGORINSKY = 0.17 * 0.17
TINY = 1e-10
THRUST = 4.0
GHOST_RATES = np.array([1.05, 1.15, 1.25, 1.35, 1.45, 1.55, 1.65, 1.75, 1.85])
W_REST, W_AXIS, W_EDGE = 1.0 / 3.0, 1.0 / 18.0, 1.0 / 36.0

VECTORS = np.array(
    [(0, 0, 0), (1, 0, 0), (-1, 0, 0), (0, 1, 0), (0, -1, 0), (0, 0, 1), (0, 0, -1)]
    + [(1, 1, 0), (-1, -1, 0), (1, -1, 0), (-1, 1, 0), (1, 0, 1), (-1, 0, -1)]
    + [(1, 0, -1), (-1, 0, 1), (0, 1, 1), (0, -1, -1), (0, 1, -1), (0, -1, 1)]
)
OPPOSITE = [0] + [i + 1 if i % 2 else i - 1 for i in range(1, 19)]


def basis():
    c = VECTORS * 1.0
    weights = np.array([W_REST] + [W_AXIS] * 6 + [W_EDGE] * 12)
    x, y, z = c[:, 0], c[:, 1], c[:, 2]
    monomials = [np.ones(19), x, y, z, x * x, y * y, z * z, x * y, x * z, y * z]
    monomials += [x * y * y, x * z * z, y * x * x, y * z * z, z * x * x, z * y * y]
    monomials += [x * x * y * y, x * x * z * z, y * y * z * z]
    rows = []
    for entry in monomials:
        vector = entry * 1.0
        for sweep in range(2):
            for other in rows:
                vector = vector - np.sum(weights * vector * other) * other
        rows.append(vector / np.sqrt(np.sum(weights * vector * vector)))
    return np.stack(rows, 0)


def ghost_tables():
    rows = basis()
    odd = []
    for first, members in ((10, (1, 7, 11)), (12, (3, 7, 15)), (14, (5, 11, 15))):
        h = rows[first : first + 2][:, list(members)]
        rates = GHOST_RATES[first - 10 : first - 8]
        odd.append(np.diag([W_AXIS, W_EDGE, W_EDGE]) @ h.T @ np.diag(rates) @ h)
    even = rows[16:19][:, [0, 1, 3, 5, 7, 11, 15]]
    return odd, even, GHOST_RATES[6:9]


ODD, EVEN, EVEN_RATES = ghost_tables()
CLASS_W = [W_REST] + [W_AXIS] * 3 + [W_EDGE] * 3


def combine(coefs, values):
    total = None
    for coef, value in zip(coefs, values):
        coef = float(coef)
        if abs(coef) < 1e-12:
            continue
        term = value if coef == 1.0 else value * coef
        total = term if total is None else total + term
    return total


def split_parity(s):
    e = [s[i] + s[i + 1] for i in range(1, 19, 2)]
    o = [s[i] - s[i + 1] for i in range(1, 19, 2)]
    even = [s[0], e[0], e[1], e[2], e[3] + e[4], e[5] + e[6], e[7] + e[8]]
    cross = [e[3] - e[4], e[5] - e[6], e[7] - e[8]]
    odd_x = [o[0], o[3] + o[4], o[5] + o[6]]
    odd_y = [o[1], o[3] - o[4], o[7] + o[8]]
    odd_z = [o[2], o[5] - o[6], o[7] - o[8]]
    return even, cross, odd_x, odd_y, odd_z


def merge_parity(s, even, cross, odd_x, odd_y, odd_z):
    out = [s[0] + even[0]]
    for axis, odd in enumerate((odd_x, odd_y, odd_z)):
        out += [s[1 + 2 * axis] + (even[1 + axis] + odd[0])]
        out += [s[2 + 2 * axis] + (even[1 + axis] - odd[0])]
    pairs = ((odd_x[1], odd_y[1]), (odd_x[2], odd_z[1]), (odd_y[2], odd_z[2]))
    for family in range(3):
        first, second = pairs[family]
        base = 7 + 4 * family
        for sign, offset in ((1, 0), (-1, 2)):
            level = even[4 + family] + cross[family] if sign > 0 else even[4 + family] - cross[family]
            swing = first + second if sign > 0 else first - second
            out += [s[base + offset] + (level + swing), s[base + offset + 1] + (level - swing)]
    return out


def ghost_even(even, transpose):
    if transpose:
        even = [value * w for value, w in zip(even, CLASS_W)]
    m = [combine(EVEN[k], even) * float(EVEN_RATES[k]) for k in range(3)]
    out = [combine(EVEN[:, j], m) for j in range(7)]
    if not transpose:
        out = [value * w for value, w in zip(out, CLASS_W)]
    return out


def ghost_odd(index, odd, transpose):
    matrix = ODD[index].T if transpose else ODD[index]
    return [combine(matrix[j], odd) for j in range(3)]


def local_state(even, cross, odds):
    rho = ((even[0] + even[1]) + (even[2] + even[3])) + ((even[4] + even[5]) + even[6])
    inverse = 1.0 / rho
    mom = [(odd[0] + odd[1]) + odd[2] for odd in odds]
    u = [m * inverse for m in mom]
    third = rho * (1.0 / 3.0)
    edges = ((even[4], even[5]), (even[4], even[6]), (even[5], even[6]))
    stress = [
        ((even[1 + a] + edges[a][0]) + edges[a][1]) - third - mom[a] * u[a] for a in range(3)
    ]
    stress += [cross[0] - mom[0] * u[1], cross[1] - mom[0] * u[2], cross[2] - mom[1] * u[2]]
    square = stress[0] * stress[0] + stress[1] * stress[1] + stress[2] * stress[2]
    square = square + 2.0 * (
        stress[3] * stress[3] + stress[4] * stress[4] + stress[5] * stress[5]
    )
    norm = jnp.sqrt(square + TINY)
    root = jnp.sqrt(TAU_ZERO * TAU_ZERO + (18.0 * SMAGORINSKY) * norm * inverse)
    tau = 0.5 * (TAU_ZERO + root)
    return inverse, u, stress, norm, root, tau


def collide(s, force):
    even, cross, odd_x, odd_y, odd_z = split_parity(s)
    inverse, u, stress, norm, root, tau = local_state(even, cross, (odd_x, odd_y, odd_z))
    scale = 4.5 / tau
    k = [value * scale for value in stress]
    trace = (k[0] + k[1] + k[2]) * (1.0 / 3.0)
    relax = [-trace, k[0] - trace, k[1] - trace, k[2] - trace]
    relax += [k[0] + relax[2], k[0] + relax[3], k[1] + relax[3]]
    ghost = ghost_even(even, False)
    even_out = [-(relax[j] * CLASS_W[j] + ghost[j]) for j in range(7)]
    cross_out = [k[3 + j] * (-2.0 * W_EDGE) for j in range(3)]
    gx = ghost_odd(0, odd_x, False)
    ox = [force * (1.0 / 6.0) - gx[0], force * (1.0 / 12.0) - gx[1], force * (1.0 / 12.0) - gx[2]]
    oy = [-value for value in ghost_odd(1, odd_y, False)]
    oz = [-value for value in ghost_odd(2, odd_z, False)]
    return merge_parity(s, even_out, cross_out, ox, oy, oz)


def collide_adjoint(s, a, speed_bar):
    even, cross, odd_x, odd_y, odd_z = split_parity(s)
    inverse, u, stress, norm, root, tau = local_state(even, cross, (odd_x, odd_y, odd_z))
    ev, cr, ax, ay, az = split_parity(a)
    weighted = [value * w for value, w in zip(ev, CLASS_W)]
    total = ((weighted[0] + weighted[1]) + (weighted[2] + weighted[3])) + (
        (weighted[4] + weighted[5]) + weighted[6]
    )
    third = total * (1.0 / 3.0)
    edges = ((4, 5), (4, 6), (5, 6))
    beta = [
        (weighted[1 + i] + weighted[edges[i][0]] + weighted[edges[i][1]] - third) * -4.5
        for i in range(3)
    ]
    beta += [value * (-9.0 * W_EDGE) for value in cr]
    inv_tau = 1.0 / tau
    dot = (beta[0] * stress[0] + beta[1] * stress[1] + beta[2] * stress[2]) + (
        beta[3] * stress[3] + beta[4] * stress[4] + beta[5] * stress[5]
    )
    tau_bar = -dot * inv_tau * inv_tau
    common = tau_bar * (4.5 * SMAGORINSKY) * inverse / root
    factor = common / norm
    p_bar = [beta[i] * inv_tau + stress[i] * factor for i in range(3)]
    twice = factor + factor
    p_bar += [beta[i] * inv_tau + stress[i] * twice for i in range(3, 6)]
    sp = speed_bar * inverse
    px, py, pz, pxy, pxz, pyz = p_bar
    tx = pxy * u[1] + pxz * u[2]
    ty = pyz * u[2]
    mx = sp - (2.0 * px * u[0] + tx)
    my = -(2.0 * py * u[1] + pxy * u[0] + ty)
    mz = -(2.0 * pz * u[2] + pxz * u[0] + pyz * u[1])
    rho_bar = -common * norm * inverse - (px + py + pz) * (1.0 / 3.0)
    rho_bar = rho_bar + (px * u[0] + tx) * u[0] + (py * u[1] + ty) * u[1] + pz * u[2] * u[2]
    rho_bar = rho_bar - sp * u[0]
    ghost = ghost_even(ev, True)
    level = [rho_bar, rho_bar + px, rho_bar + py, rho_bar + pz]
    level += [level[1] + py, level[1] + pz, level[2] + pz]
    even_out = [level[j] - ghost[j] for j in range(7)]
    gx, gy, gz = (ghost_odd(i, odd, True) for i, odd in enumerate((ax, ay, az)))
    ox = [mx - value for value in gx]
    oy = [my - value for value in gy]
    oz = [mz - value for value in gz]
    return merge_parity(a, even_out, p_bar[3:], ox, oy, oz)


def chunks(body):
    def step(index, carry):
        lane = pl.multiple_of(index * 128, 128)
        for row in range(0, RX, 8):
            body(pl.ds(row, 8), pl.ds(lane, 128))
        return carry

    lax.fori_loop(0, LANES // 128, step, 0)


def shifted(value, cx, cy, cz):
    lane = (NZ * cy + cz) % LANES
    if lane:
        value = pltpu.roll(value, lane, 1)
    if cx % RX:
        value = pltpu.roll(value, cx % RX, 0)
    return value


def height():
    return lax.broadcasted_iota(jnp.int32, (RX, LANES), 1) & (NZ - 1)


def stream(field, out):
    z = height()
    for i in range(19):
        cx, cy, cz = (int(v) for v in VECTORS[i])
        value = shifted(field[i], cx, cy, cz)
        if cz:
            value = jnp.where(z == (0 if cz > 0 else NZ - 1), field[OPPOSITE[i]], value)
        out[i] = value


def stream_adjoint(field, out):
    z = height()
    for i in range(19):
        cx, cy, cz = (int(v) for v in VECTORS[i])
        value = field[i]
        if cz:
            value = jnp.where(z == (0 if cz > 0 else NZ - 1), 0.0, value)
        value = shifted(value, -cx, -cy, -cz)
        if cz:
            value = value + jnp.where(z == (NZ - 1 if cz > 0 else 0), field[OPPOSITE[i]], 0.0)
        out[i] = value


def speeds(s_ref, v_ref):
    def one(rows, lanes):
        s = [s_ref[i, rows, lanes] for i in range(19)]
        even, cross, odd_x, odd_y, odd_z = split_parity(s)
        rho = ((even[0] + even[1]) + (even[2] + even[3])) + ((even[4] + even[5]) + even[6])
        v_ref[rows, lanes] = ((odd_x[0] + odd_x[1]) + odd_x[2]) / rho

    chunks(one)


def push_back(a):
    odd = (a[7] - a[8]) + (a[9] - a[10]) + (a[11] - a[12]) + (a[13] - a[14])
    return (a[1] - a[2]) * (1.0 / 6.0) + odd * (1.0 / 12.0)


def turbine_sums(area_ref, field_ref, sums_ref, out_ref, base):
    parts = [field_ref[OWN_ROWS, OWN_LANE + j : OWN_LANE + j + 128] for j in range(0, OWN_SPAN, 128)]
    for t in range(NTURB):
        total = None
        for j, part in enumerate(parts):
            lane = OWN_LANE + 128 * j
            term = area_ref[t, OWN_ROWS, lane : lane + 128] * part
            total = term if total is None else total + term
        sums_ref[t : t + 1, :] = jnp.sum(total, axis=0, keepdims=True)
    row = jnp.sum(sums_ref[...], axis=1, keepdims=True)
    out_ref[base : base + NTURB, :] = jnp.broadcast_to(row, (NTURB, 128))


def weighted_area(area_ref, weight_ref, rows, lanes):
    total = None
    for t in range(NTURB):
        term = area_ref[t, rows, lanes] * weight_ref[t : t + 1, :]
        total = term if total is None else total + term
    return total


def split_three(value):
    high = value.astype(jnp.bfloat16)
    rest = value - high.astype(jnp.float32)
    middle = rest.astype(jnp.bfloat16)
    return high, middle, (rest - middle.astype(jnp.float32)).astype(jnp.bfloat16)


def area_kernel(x_ref, yz_ref, area_ref, out_ref):
    rows = lax.broadcasted_iota(jnp.int32, (RX, PTS), 0)
    columns = lax.broadcasted_iota(jnp.int32, (LANES, PTS), 0)

    def one(t, carry):
        point = pl.ds(t, 1)
        spots = jnp.where(rows == x_ref[point, :], area_ref[point, :], 0.0)
        left = jnp.concatenate(split_three(spots), axis=0)
        hot = jnp.where(columns == yz_ref[point, :], 1.0, 0.0).astype(jnp.bfloat16)
        product = lax.dot_general(
            left, hot, (((1,), (1,)), ((), ())), preferred_element_type=jnp.float32
        )
        out_ref[t] = product[:RX] + product[RX : 2 * RX] + product[2 * RX :]
        return carry

    lax.fori_loop(0, NTURB, one, 0)


class Joined:
    def __init__(self, *parts):
        self.parts = parts

    def __getitem__(self, index):
        return jnp.concatenate([part[index] for part in self.parts], axis=0)


def first_kernel(before_ref, own_ref, after_ref, area_ref, s_ref, v_ref, cot_ref, sum_ref, sums):
    both = Joined(before_ref, own_ref, after_ref)
    stream(both, s_ref)
    speeds(s_ref, v_ref)
    turbine_sums(area_ref, v_ref, sums, sum_ref, 0)
    for i in range(19):
        cot_ref[i] = both[19 + i]


def forward_kernel(last, s_ref, v_ref, area_ref, rotor_ref, *rest):
    if last:
        cot_ref, next_ref, vn_ref, sum_ref, field, drag, sums = rest
    else:
        next_ref, vn_ref, sum_ref, field, sums = rest

    def one(rows, lanes):
        s = [s_ref[i, rows, lanes] for i in range(19)]
        force = weighted_area(area_ref, rotor_ref, rows, lanes) * v_ref[rows, lanes] * -THRUST
        for i, value in enumerate(collide(s, force)):
            field[i, rows, lanes] = value

    chunks(one)
    stream(field, next_ref)
    speeds(next_ref, vn_ref)
    turbine_sums(area_ref, vn_ref, sums, sum_ref, 0)
    if last:

        def other(rows, lanes):
            a = [cot_ref[i, rows, lanes] for i in range(19)]
            drag[rows, lanes] = push_back(a) * vn_ref[rows, lanes] * -THRUST

        chunks(other)
        turbine_sums(area_ref, drag, sums, sum_ref, NTURB)


def adjoint_field(s_ref, a_ref, area_ref, rotor_ref, bar_ref, field):
    def one(rows, lanes):
        s = [s_ref[i, rows, lanes] for i in range(19)]
        a = [a_ref[i, rows, lanes] for i in range(19)]
        speed_bar = weighted_area(area_ref, rotor_ref, rows, lanes) * push_back(a) * -THRUST
        speed_bar = speed_bar + weighted_area(area_ref, bar_ref, rows, lanes)
        for i, value in enumerate(collide_adjoint(s, a, speed_bar)):
            field[i, rows, lanes] = value

    chunks(one)


def backward_kernel(s_ref, a_ref, area_ref, rotor_ref, bar_ref, v_ref, out_ref, drag_ref, sum_ref, field, sums):
    adjoint_field(s_ref, a_ref, area_ref, rotor_ref, bar_ref, field)
    stream_adjoint(field, out_ref)

    def other(rows, lanes):
        a = [out_ref[i, rows, lanes] for i in range(19)]
        drag_ref[rows, lanes] = push_back(a) * v_ref[rows, lanes] * -THRUST

    chunks(other)
    turbine_sums(area_ref, drag_ref, sums, sum_ref, 0)


def last_kernel(s_ref, a_ref, area_ref, rotor_ref, bar_ref, out_ref, field, result):
    adjoint_field(s_ref, a_ref, area_ref, rotor_ref, bar_ref, field)
    stream_adjoint(field, result)
    for i in range(19):
        out_ref[i] = result[i, OWN_ROWS, OWN_LANE : OWN_LANE + OWN_SPAN]


def gather_kernel(x_ref, yz_ref, cot_ref, q1, q2, q3, v1, v2, v3, v4, u1, u2, u3, u4, n2, n3, n4, inv, out_ref):
    own = (OWN_ROWS, slice(OWN_LANE, OWN_LANE + OWN_SPAN))
    v = [ref[own] for ref in (v1, v2, v3, v4)]
    q = [ref[own] for ref in (q1, q2, q3)]
    a = [cot_ref[(i,) + own] for i in range(19)]
    q.append(push_back(a) * v[3] * -THRUST)
    rows = lax.broadcasted_iota(jnp.int32, (CX, PTS), 0) + MARGIN
    columns = lax.broadcasted_iota(jnp.int32, (OWN_SPAN, PTS), 0) + OWN_LANE

    def wide(ref, t):
        return jnp.concatenate([ref[pl.ds(t, 1), :]] * (OWN_SPAN // 128), axis=1)

    out_ref[...] = jnp.zeros_like(out_ref)

    def one(t, carry):
        u = [wide(ref, t) for ref in (u1, u2, u3, u4)]
        n = [None] + [wide(ref, t) for ref in (n2, n3, n4)]
        known = u[0] * q[0]
        for k in range(1, 4):
            known = known + u[k] * q[k] + n[k] * (v[k] - u[k])
        fields = [known, q[0], (v[0] - u[0]) * wide(inv, t)]
        left = jnp.concatenate(split_three(jnp.concatenate(fields, axis=0)), axis=0)
        hot = jnp.where(columns == yz_ref[pl.ds(t, 1), :], 1.0, 0.0).astype(jnp.bfloat16)
        product = jnp.dot(left, hot, preferred_element_type=jnp.float32)
        size = 3 * CX
        product = product[:size] + product[size : 2 * size] + product[2 * size :]
        mine = rows == x_ref[pl.ds(t, 1), :]
        for j in range(3):
            picked = jnp.where(mine, product[CX * j : CX * (j + 1)], 0.0)
            out_ref[pl.ds(j * NTURB + t, 1), 0:PTS] = jnp.sum(picked, axis=0, keepdims=True)
        return carry

    lax.fori_loop(0, NTURB, one, 0)


def call(kernel, outs, scratch, *args):
    vmem = pl.BlockSpec(memory_space=pltpu.VMEM)
    return pl.pallas_call(
        kernel,
        out_shape=[jax.ShapeDtypeStruct(shape, jnp.float32) for shape in outs],
        in_specs=[vmem] * len(args),
        out_specs=[vmem] * len(outs),
        scratch_shapes=[pltpu.VMEM(shape, jnp.float32) for shape in scratch],
        compiler_params=pltpu.CompilerParams(vmem_limit_bytes=32 * 1024 * 1024),
    )(*args)


def route(value, target):
    size_x, size_y = lax.axis_size("gx"), lax.axis_size("gy")
    pairs = []
    for i in range(size_x):
        for j in range(size_y):
            to = target(i, j)
            if to is not None:
                pairs.append((i * size_y + j, to[0] % size_x * size_y + to[1] % size_y))
    return lax.ppermute(value, ("gx", "gy"), pairs)


def swap(value):
    return route(value, lambda i, j: (i ^ 1, j))


def window(value):
    value = value + swap(value)
    left = route(value, lambda i, j: (i + 2, j))
    right = route(value, lambda i, j: (i - 2, j))
    far = route(value, lambda i, j: (i + (-4 if i % 2 else 4), j))
    value = (left + right) + (far + value)
    size = lax.axis_size("gy")
    copies = jnp.tile(value, (size, 1))
    copies = lax.all_to_all(copies, "gy", 0, 0, tiled=True)
    return jnp.sum(copies.reshape((size,) + value.shape), 0)


def merge(value, parts):
    for part in parts:
        value = jnp.where(value != 0.0, value, part)
    return value


def spread(value):
    size_x, size_y = lax.axis_size("gx"), lax.axis_size("gy")
    half = size_y // 2

    def across(first, second):
        def target(i, j):
            dy, dz = second if i % 2 else first
            return i, (j // half + dz) % 2 * half + (j % half + dy) % half

        return target

    def along(block, step, first, second):
        def target(i, j):
            move = second if i % 2 else first
            if move is None:
                return None
            return i // block * block + (i % block + move * step) % block, j

        return target

    value = merge(value, [swap(value)])
    turns = [((1, 0), (1, 1)), ((3, 0), (3, 1)), ((2, 0), (2, 1)), ((0, 1), (0, 1))]
    value = merge(value, [route(value, across(*turn)) for turn in turns])
    value = merge(value, [swap(value)])
    for block, step in ((8, 2), (size_x, 8)):
        turns = [(1, 2), (3, None)]
        value = merge(value, [route(value, along(block, step, *turn)) for turn in turns])
        value = merge(value, [swap(value)])
    return value


def shift(value, axis, step):
    size = lax.axis_size(axis)
    return lax.ppermute(value, axis, [(i, (i + step) % size) for i in range(size)])


def region(checkpoint, cotangent):
    edge = MARGIN * NZ
    span = checkpoint.shape[2]
    first = jnp.concatenate([checkpoint[:, :, :edge], cotangent[:, :, :edge]], axis=0)
    last = jnp.concatenate([checkpoint[:, :, span - edge :], cotangent[:, :, span - edge :]], axis=0)
    before, after = shift(last, "gy", 1), shift(first, "gy", -1)
    own = jnp.concatenate([checkpoint, cotangent], axis=0)
    own = jnp.concatenate([before, own, after], axis=2)
    return shift(own, "gx", 1), own, shift(own, "gx", -1)


def body(checkpoint, cotangent, blade_area, hub_tile, point_side, point_local):
    count_x, count_y = lax.axis_size("gx"), lax.axis_size("gy")
    index_x, index_y = lax.axis_index("gx"), lax.axis_index("gy")
    area = blade_area.reshape(NTURB, PTS)
    side = point_side.reshape(NTURB, PTS)
    local = point_local.reshape(NTURB, PTS)
    hub = hub_tile.reshape(NTURB, 1)
    cell_x = (hub // count_y + side // 3 - 1 - index_x) * CX + local // (CY * NZ) + MARGIN
    cell_y = (hub % count_y + side % 3 - 1 - index_y) * CY + local // NZ % CY + MARGIN
    cell_x = cell_x % (count_x * CX)
    cell_y = cell_y % (count_y * CY)
    inside = (cell_x < RX) & (cell_y < RY)
    cell_x = jnp.where(inside, cell_x, -1)
    cell_yz = jnp.where(inside, cell_y * NZ + local % NZ, -1)
    mine_y = (cell_y >= MARGIN) & (cell_y < MARGIN + CY)
    inverse = jnp.broadcast_to(1.0 / jnp.sum(area, 1, keepdims=True), (NTURB, 128))

    full = (19, RX, LANES)
    flat = (RX, LANES)
    row = (NTURB, 128)
    parts = region(checkpoint, cotangent)
    (spots,) = call(area_kernel, [(NTURB,) + flat], [], cell_x, cell_yz, area)

    s, v, rotor = [None] * 5, [None] * 5, [None] * 5
    s[1], v[1], cot, sums = call(first_kernel, [full, flat, full, row], [row], *parts, spots)
    for k in (1, 2, 3):
        rotor[k] = window(sums) * inverse
        last = k == 3
        outs = [full, flat, (2 * NTURB, 128) if last else row]
        s[k + 1], v[k + 1], sums = call(
            functools.partial(forward_kernel, last),
            outs,
            [full] + ([flat] if last else []) + [row],
            *([s[k], v[k], spots, rotor[k]] + ([cot] if last else [])),
        )
    sums = window(sums)
    rotor[4] = sums[:NTURB] * inverse
    sums = sums[NTURB:]
    adjoint = cot
    bar, drag = [None] * 5, [None] * 5
    for k in (4, 3, 2):
        bar[k] = (window(sums) if k < 4 else sums) * inverse
        adjoint, drag[k - 1], sums = call(
            backward_kernel,
            [full, flat, row],
            [full, row],
            *(s[k], adjoint, spots, rotor[k], bar[k], v[k - 1]),
        )
    (points,) = call(
        gather_kernel,
        [(3 * NTURB, 128)],
        [],
        *([cell_x, jnp.where(mine_y, cell_yz, -1), cot] + drag[1:4] + v[1:] + rotor[1:] + bar[2:] + [inverse]),
    )
    points = spread(points)[:, :PTS]
    known, swing, slope = points[:NTURB], points[NTURB : 2 * NTURB], points[2 * NTURB :]
    total = jnp.sum(area * swing, 1, keepdims=True)
    grad_area = (known + total * slope).reshape(-1)
    bar[1] = total * inverse
    (grad,) = call(
        last_kernel,
        [(19, CX, CY * NZ)],
        [full, full],
        *(s[1], adjoint, spots, rotor[1], bar[1]),
    )
    return grad, grad_area


def solution(mesh):
    return jax.shard_map(
        body,
        mesh=mesh,
        in_specs=(P(None, "gx", "gy"), P(None, "gx", "gy"), P(), P(), P(), P()),
        out_specs=(P(None, "gx", "gy"), P()),
        check_vma=False,
    )
```

```python
import functools

import jax
import jax.numpy as jnp
import numpy as np
from jax import lax
from jax.experimental import pallas as pl
from jax.experimental.pallas import tpu as pltpu
from jax.sharding import PartitionSpec as P

NZ = 16
CX = 8
CY = 16
STEPS = 4
NTURB = 16
PTS = 96
MARGIN = 8
RX = CX + 2 * MARGIN
RY = CY + 2 * MARGIN
LANES = RY * NZ
OWN_ROWS = slice(MARGIN, MARGIN + CX)
OWN_LANE = MARGIN * NZ
OWN_SPAN = CY * NZ

VMEM_LIMIT = 8 * 1024 * 1024

TAU_ZERO = 0.52
SMAGORINSKY = 0.17 * 0.17
TINY = 1e-10
THRUST = 4.0
GHOST_RATES = np.array([1.05, 1.15, 1.25, 1.35, 1.45, 1.55, 1.65, 1.75, 1.85])
W_REST, W_AXIS, W_EDGE = 1.0 / 3.0, 1.0 / 18.0, 1.0 / 36.0

VECTORS = np.array(
    [(0, 0, 0), (1, 0, 0), (-1, 0, 0), (0, 1, 0), (0, -1, 0), (0, 0, 1), (0, 0, -1)]
    + [(1, 1, 0), (-1, -1, 0), (1, -1, 0), (-1, 1, 0), (1, 0, 1), (-1, 0, -1)]
    + [(1, 0, -1), (-1, 0, 1), (0, 1, 1), (0, -1, -1), (0, 1, -1), (0, -1, 1)]
)
OPPOSITE = [0] + [i + 1 if i % 2 else i - 1 for i in range(1, 19)]


def basis():
    c = VECTORS * 1.0
    weights = np.array([W_REST] + [W_AXIS] * 6 + [W_EDGE] * 12)
    x, y, z = c[:, 0], c[:, 1], c[:, 2]
    monomials = [np.ones(19), x, y, z, x * x, y * y, z * z, x * y, x * z, y * z]
    monomials += [x * y * y, x * z * z, y * x * x, y * z * z, z * x * x, z * y * y]
    monomials += [x * x * y * y, x * x * z * z, y * y * z * z]
    rows = []
    for entry in monomials:
        vector = entry * 1.0
        for sweep in range(2):
            for other in rows:
                vector = vector - np.sum(weights * vector * other) * other
        rows.append(vector / np.sqrt(np.sum(weights * vector * vector)))
    return np.stack(rows, 0)


def ghost_tables():
    rows = basis()
    odd = []
    for first, members in ((10, (1, 7, 11)), (12, (3, 7, 15)), (14, (5, 11, 15))):
        h = rows[first : first + 2][:, list(members)]
        rates = GHOST_RATES[first - 10 : first - 8]
        odd.append(np.diag([W_AXIS, W_EDGE, W_EDGE]) @ h.T @ np.diag(rates) @ h)
    even = rows[16:19][:, [0, 1, 3, 5, 7, 11, 15]]
    return odd, even, GHOST_RATES[6:9]


ODD, EVEN, EVEN_RATES = ghost_tables()
CLASS_W = [W_REST] + [W_AXIS] * 3 + [W_EDGE] * 3


def combine(coefs, values):
    total = None
    for coef, value in zip(coefs, values):
        coef = float(coef)
        if abs(coef) < 1e-12:
            continue
        term = value if coef == 1.0 else value * coef
        total = term if total is None else total + term
    return total


def split_parity(s):
    e = [s[i] + s[i + 1] for i in range(1, 19, 2)]
    o = [s[i] - s[i + 1] for i in range(1, 19, 2)]
    even = [s[0], e[0], e[1], e[2], e[3] + e[4], e[5] + e[6], e[7] + e[8]]
    cross = [e[3] - e[4], e[5] - e[6], e[7] - e[8]]
    odd_x = [o[0], o[3] + o[4], o[5] + o[6]]
    odd_y = [o[1], o[3] - o[4], o[7] + o[8]]
    odd_z = [o[2], o[5] - o[6], o[7] - o[8]]
    return even, cross, odd_x, odd_y, odd_z


def merge_parity(s, even, cross, odd_x, odd_y, odd_z):
    out = [s[0] + even[0]]
    for axis, odd in enumerate((odd_x, odd_y, odd_z)):
        out += [s[1 + 2 * axis] + (even[1 + axis] + odd[0])]
        out += [s[2 + 2 * axis] + (even[1 + axis] - odd[0])]
    pairs = ((odd_x[1], odd_y[1]), (odd_x[2], odd_z[1]), (odd_y[2], odd_z[2]))
    for family in range(3):
        first, second = pairs[family]
        base = 7 + 4 * family
        for sign, offset in ((1, 0), (-1, 2)):
            level = even[4 + family] + cross[family] if sign > 0 else even[4 + family] - cross[family]
            swing = first + second if sign > 0 else first - second
            out += [s[base + offset] + (level + swing), s[base + offset + 1] + (level - swing)]
    return out


def ghost_even(even, transpose):
    if transpose:
        even = [value * w for value, w in zip(even, CLASS_W)]
    m = [combine(EVEN[k], even) * float(EVEN_RATES[k]) for k in range(3)]
    out = [combine(EVEN[:, j], m) for j in range(7)]
    if not transpose:
        out = [value * w for value, w in zip(out, CLASS_W)]
    return out


def ghost_odd(index, odd, transpose):
    matrix = ODD[index].T if transpose else ODD[index]
    return [combine(matrix[j], odd) for j in range(3)]


def local_state(even, cross, odds):
    rho = ((even[0] + even[1]) + (even[2] + even[3])) + ((even[4] + even[5]) + even[6])
    inverse = 1.0 / rho
    mom = [(odd[0] + odd[1]) + odd[2] for odd in odds]
    u = [m * inverse for m in mom]
    third = rho * (1.0 / 3.0)
    edges = ((even[4], even[5]), (even[4], even[6]), (even[5], even[6]))
    stress = [
        ((even[1 + a] + edges[a][0]) + edges[a][1]) - third - mom[a] * u[a] for a in range(3)
    ]
    stress += [cross[0] - mom[0] * u[1], cross[1] - mom[0] * u[2], cross[2] - mom[1] * u[2]]
    square = stress[0] * stress[0] + stress[1] * stress[1] + stress[2] * stress[2]
    square = square + 2.0 * (
        stress[3] * stress[3] + stress[4] * stress[4] + stress[5] * stress[5]
    )
    norm = jnp.sqrt(square + TINY)
    root = jnp.sqrt(TAU_ZERO * TAU_ZERO + (18.0 * SMAGORINSKY) * norm * inverse)
    tau = 0.5 * (TAU_ZERO + root)
    return inverse, u, stress, norm, root, tau


def collide(s, force):
    even, cross, odd_x, odd_y, odd_z = split_parity(s)
    inverse, u, stress, norm, root, tau = local_state(even, cross, (odd_x, odd_y, odd_z))
    scale = 4.5 / tau
    k = [value * scale for value in stress]
    trace = (k[0] + k[1] + k[2]) * (1.0 / 3.0)
    relax = [-trace, k[0] - trace, k[1] - trace, k[2] - trace]
    relax += [k[0] + relax[2], k[0] + relax[3], k[1] + relax[3]]
    ghost = ghost_even(even, False)
    even_out = [-(relax[j] * CLASS_W[j] + ghost[j]) for j in range(7)]
    cross_out = [k[3 + j] * (-2.0 * W_EDGE) for j in range(3)]
    gx = ghost_odd(0, odd_x, False)
    ox = [force * (1.0 / 6.0) - gx[0], force * (1.0 / 12.0) - gx[1], force * (1.0 / 12.0) - gx[2]]
    oy = [-value for value in ghost_odd(1, odd_y, False)]
    oz = [-value for value in ghost_odd(2, odd_z, False)]
    return merge_parity(s, even_out, cross_out, ox, oy, oz)


def collide_adjoint(s, a, speed_bar):
    even, cross, odd_x, odd_y, odd_z = split_parity(s)
    inverse, u, stress, norm, root, tau = local_state(even, cross, (odd_x, odd_y, odd_z))
    ev, cr, ax, ay, az = split_parity(a)
    weighted = [value * w for value, w in zip(ev, CLASS_W)]
    total = ((weighted[0] + weighted[1]) + (weighted[2] + weighted[3])) + (
        (weighted[4] + weighted[5]) + weighted[6]
    )
    third = total * (1.0 / 3.0)
    edges = ((4, 5), (4, 6), (5, 6))
    beta = [
        (weighted[1 + i] + weighted[edges[i][0]] + weighted[edges[i][1]] - third) * -4.5
        for i in range(3)
    ]
    beta += [value * (-9.0 * W_EDGE) for value in cr]
    inv_tau = 1.0 / tau
    dot = (beta[0] * stress[0] + beta[1] * stress[1] + beta[2] * stress[2]) + (
        beta[3] * stress[3] + beta[4] * stress[4] + beta[5] * stress[5]
    )
    tau_bar = -dot * inv_tau * inv_tau
    common = tau_bar * (4.5 * SMAGORINSKY) * inverse / root
    factor = common / norm
    p_bar = [beta[i] * inv_tau + stress[i] * factor for i in range(3)]
    twice = factor + factor
    p_bar += [beta[i] * inv_tau + stress[i] * twice for i in range(3, 6)]
    sp = speed_bar * inverse
    px, py, pz, pxy, pxz, pyz = p_bar
    tx = pxy * u[1] + pxz * u[2]
    ty = pyz * u[2]
    mx = sp - (2.0 * px * u[0] + tx)
    my = -(2.0 * py * u[1] + pxy * u[0] + ty)
    mz = -(2.0 * pz * u[2] + pxz * u[0] + pyz * u[1])
    rho_bar = -common * norm * inverse - (px + py + pz) * (1.0 / 3.0)
    rho_bar = rho_bar + (px * u[0] + tx) * u[0] + (py * u[1] + ty) * u[1] + pz * u[2] * u[2]
    rho_bar = rho_bar - sp * u[0]
    ghost = ghost_even(ev, True)
    level = [rho_bar, rho_bar + px, rho_bar + py, rho_bar + pz]
    level += [level[1] + py, level[1] + pz, level[2] + pz]
    even_out = [level[j] - ghost[j] for j in range(7)]
    gx, gy, gz = (ghost_odd(i, odd, True) for i, odd in enumerate((ax, ay, az)))
    ox = [mx - value for value in gx]
    oy = [my - value for value in gy]
    oz = [mz - value for value in gz]
    return merge_parity(a, even_out, p_bar[3:], ox, oy, oz)


def chunks(body):
    def step(index, carry):
        lane = pl.multiple_of(index * 128, 128)
        for row in range(0, RX, 8):
            body(pl.ds(row, 8), pl.ds(lane, 128))
        return carry

    lax.fori_loop(0, LANES // 128, step, 0)


def shifted(value, cx, cy, cz):
    lane = (NZ * cy + cz) % LANES
    if lane:
        value = pltpu.roll(value, lane, 1)
    if cx % RX:
        value = pltpu.roll(value, cx % RX, 0)
    return value


def height():
    return lax.broadcasted_iota(jnp.int32, (RX, LANES), 1) & (NZ - 1)


def stream(field, out):
    z = height()
    for i in range(19):
        cx, cy, cz = (int(v) for v in VECTORS[i])
        value = shifted(field[i], cx, cy, cz)
        if cz:
            value = jnp.where(z == (0 if cz > 0 else NZ - 1), field[OPPOSITE[i]], value)
        out[i] = value


def stream_adjoint(field, out):
    z = height()
    for i in range(19):
        cx, cy, cz = (int(v) for v in VECTORS[i])
        value = field[i]
        if cz:
            value = jnp.where(z == (0 if cz > 0 else NZ - 1), 0.0, value)
        value = shifted(value, -cx, -cy, -cz)
        if cz:
            value = value + jnp.where(z == (NZ - 1 if cz > 0 else 0), field[OPPOSITE[i]], 0.0)
        out[i] = value


def speeds(s_ref, v_ref):
    def one(rows, lanes):
        s = [s_ref[i, rows, lanes] for i in range(19)]
        even, cross, odd_x, odd_y, odd_z = split_parity(s)
        rho = ((even[0] + even[1]) + (even[2] + even[3])) + ((even[4] + even[5]) + even[6])
        v_ref[rows, lanes] = ((odd_x[0] + odd_x[1]) + odd_x[2]) / rho

    chunks(one)


def push_back(a):
    odd = (a[7] - a[8]) + (a[9] - a[10]) + (a[11] - a[12]) + (a[13] - a[14])
    return (a[1] - a[2]) * (1.0 / 6.0) + odd * (1.0 / 12.0)


def turbine_sums(area_ref, field_ref, sums_ref, base):
    parts = [field_ref[OWN_ROWS, OWN_LANE + j : OWN_LANE + j + 128] for j in range(0, OWN_SPAN, 128)]
    for t in range(NTURB):
        total = None
        for j, part in enumerate(parts):
            lane = OWN_LANE + 128 * j
            term = area_ref[t, OWN_ROWS, lane : lane + 128] * part
            total = term if total is None else total + term
        sums_ref[base + t : base + t + 1, :] = jnp.sum(total, axis=0, keepdims=True)


def publish(sums_ref, out_ref):
    ones = jnp.ones((8, 128), jnp.bfloat16)
    row = None
    for part in split_three(sums_ref[...]):
        term = lax.dot_general(
            ones, part, (((1,), (1,)), ((), ())), preferred_element_type=jnp.float32
        )
        row = term if row is None else row + term
    for j in range(0, out_ref.shape[0], 8):
        out_ref[j : j + 8, :] = row


def totals(got_ref, base):
    row = jnp.sum(got_ref[...], axis=0, keepdims=True)
    index = lax.broadcasted_iota(jnp.int32, (NTURB, 128), 0) + base
    lane = lax.broadcasted_iota(jnp.int32, (NTURB, 128), 1)
    picked = jnp.where(index == lane, jnp.broadcast_to(row, (NTURB, 128)), 0.0)
    return jnp.broadcast_to(jnp.sum(picked, axis=1, keepdims=True), (NTURB, 128))


def weighted_area(area_ref, weight_ref, rows, lanes):
    total = None
    for t in range(NTURB):
        term = area_ref[t, rows, lanes] * weight_ref[t : t + 1, :]
        total = term if total is None else total + term
    return total


def split_three(value):
    high = value.astype(jnp.bfloat16)
    rest = value - high.astype(jnp.float32)
    middle = rest.astype(jnp.bfloat16)
    return high, middle, (rest - middle.astype(jnp.float32)).astype(jnp.bfloat16)


def area_kernel(x_ref, yz_ref, area_ref, out_ref):
    rows = lax.broadcasted_iota(jnp.int32, (RX, PTS), 0)
    columns = lax.broadcasted_iota(jnp.int32, (LANES, PTS), 0)

    def one(t, carry):
        point = pl.ds(t, 1)
        spots = jnp.where(rows == x_ref[point, :], area_ref[point, :], 0.0)
        left = jnp.concatenate(split_three(spots), axis=0)
        hot = jnp.where(columns == yz_ref[point, :], 1.0, 0.0).astype(jnp.bfloat16)
        product = lax.dot_general(
            left, hot, (((1,), (1,)), ((), ())), preferred_element_type=jnp.float32
        )
        out_ref[t] = product[:RX] + product[RX : 2 * RX] + product[2 * RX :]
        return carry

    lax.fori_loop(0, NTURB, one, 0)


class Joined:
    def __init__(self, *parts):
        self.parts = parts

    def __getitem__(self, index):
        return jnp.concatenate([part[index] for part in self.parts], axis=0)


def first_kernel(before_ref, own_ref, after_ref, area_ref, s_ref, v_ref, cot_ref, out_ref, sums):
    both = Joined(before_ref, own_ref, after_ref)
    stream(both, s_ref)
    speeds(s_ref, v_ref)
    sums[...] = jnp.zeros_like(sums)
    turbine_sums(area_ref, v_ref, sums, 0)
    publish(sums, out_ref)
    for i in range(19):
        cot_ref[i] = both[19 + i]


def forward_kernel(last, s_ref, v_ref, area_ref, inv_ref, got_ref, *rest):
    if last:
        cot_ref, next_ref, vn_ref, rotor_ref, out_ref, field, sums, drag = rest
    else:
        next_ref, vn_ref, rotor_ref, out_ref, field, sums = rest
    rotor_ref[...] = totals(got_ref, 0) * inv_ref[...]

    def one(rows, lanes):
        s = [s_ref[i, rows, lanes] for i in range(19)]
        force = weighted_area(area_ref, rotor_ref, rows, lanes) * v_ref[rows, lanes] * -THRUST
        for i, value in enumerate(collide(s, force)):
            field[i, rows, lanes] = value

    chunks(one)
    stream(field, next_ref)
    speeds(next_ref, vn_ref)
    sums[...] = jnp.zeros_like(sums)
    turbine_sums(area_ref, vn_ref, sums, 0)
    if last:

        def other(rows, lanes):
            a = [cot_ref[i, rows, lanes] for i in range(19)]
            drag[rows, lanes] = push_back(a) * vn_ref[rows, lanes] * -THRUST

        chunks(other)
        turbine_sums(area_ref, drag, sums, NTURB)
    publish(sums, out_ref)


def adjoint_field(s_ref, a_ref, area_ref, rotor_ref, bar_ref, field):
    def one(rows, lanes):
        s = [s_ref[i, rows, lanes] for i in range(19)]
        a = [a_ref[i, rows, lanes] for i in range(19)]
        speed_bar = weighted_area(area_ref, rotor_ref, rows, lanes) * push_back(a) * -THRUST
        speed_bar = speed_bar + weighted_area(area_ref, bar_ref, rows, lanes)
        for i, value in enumerate(collide_adjoint(s, a, speed_bar)):
            field[i, rows, lanes] = value

    chunks(one)


def backward_kernel(first, s_ref, a_ref, area_ref, inv_ref, got_ref, v_ref, *rest):
    if first:
        out_ref, drag_ref, bar_ref, publish_ref, rotor_ref, field, sums = rest
        rotor_ref[...] = totals(got_ref, 0) * inv_ref[...]
    else:
        rotor_ref, out_ref, drag_ref, bar_ref, publish_ref, field, sums = rest
    bar_ref[...] = totals(got_ref, NTURB if first else 0) * inv_ref[...]
    adjoint_field(s_ref, a_ref, area_ref, rotor_ref, bar_ref, field)
    stream_adjoint(field, out_ref)

    def other(rows, lanes):
        a = [out_ref[i, rows, lanes] for i in range(19)]
        drag_ref[rows, lanes] = push_back(a) * v_ref[rows, lanes] * -THRUST

    chunks(other)
    sums[...] = jnp.zeros_like(sums)
    turbine_sums(area_ref, drag_ref, sums, 0)
    publish(sums, publish_ref)


def last_kernel(s_ref, a_ref, area_ref, rotor_ref, bar_ref, out_ref, field, result):
    adjoint_field(s_ref, a_ref, area_ref, rotor_ref, bar_ref, field)
    stream_adjoint(field, result)
    for i in range(19):
        out_ref[i] = result[i, OWN_ROWS, OWN_LANE : OWN_LANE + OWN_SPAN]


def gather_kernel(x_ref, yz_ref, cot_ref, q1, q2, q3, v1, v2, v3, v4, u1, u2, u3, u4, n2, n3, n4, inv, out_ref):
    own = (OWN_ROWS, slice(OWN_LANE, OWN_LANE + OWN_SPAN))
    v = [ref[own] for ref in (v1, v2, v3, v4)]
    q = [ref[own] for ref in (q1, q2, q3)]
    a = [cot_ref[(i,) + own] for i in range(19)]
    q.append(push_back(a) * v[3] * -THRUST)
    rows = lax.broadcasted_iota(jnp.int32, (CX, PTS), 0) + MARGIN
    columns = lax.broadcasted_iota(jnp.int32, (OWN_SPAN, PTS), 0) + OWN_LANE

    def wide(ref, t):
        return jnp.concatenate([ref[pl.ds(t, 1), :]] * (OWN_SPAN // 128), axis=1)

    out_ref[...] = jnp.zeros_like(out_ref)

    def one(t, carry):
        u = [wide(ref, t) for ref in (u1, u2, u3, u4)]
        n = [None] + [wide(ref, t) for ref in (n2, n3, n4)]
        known = u[0] * q[0]
        for k in range(1, 4):
            known = known + u[k] * q[k] + n[k] * (v[k] - u[k])
        fields = [known, q[0], (v[0] - u[0]) * wide(inv, t)]
        left = jnp.concatenate(split_three(jnp.concatenate(fields, axis=0)), axis=0)
        hot = jnp.where(columns == yz_ref[pl.ds(t, 1), :], 1.0, 0.0).astype(jnp.bfloat16)
        product = jnp.dot(left, hot, preferred_element_type=jnp.float32)
        size = 3 * CX
        product = product[:size] + product[size : 2 * size] + product[2 * size :]
        mine = rows == x_ref[pl.ds(t, 1), :]
        for j in range(3):
            picked = jnp.where(mine, product[CX * j : CX * (j + 1)], 0.0)
            out_ref[pl.ds(j * NTURB + t, 1), 0:PTS] = jnp.sum(picked, axis=0, keepdims=True)
        return carry

    lax.fori_loop(0, NTURB, one, 0)


def call(kernel, outs, scratch, *args):
    vmem = pl.BlockSpec(memory_space=pltpu.VMEM)
    return pl.pallas_call(
        kernel,
        out_shape=[jax.ShapeDtypeStruct(shape, jnp.float32) for shape in outs],
        in_specs=[vmem] * len(args),
        out_specs=[vmem] * len(outs),
        scratch_shapes=[pltpu.VMEM(shape, jnp.float32) for shape in scratch],
        compiler_params=pltpu.CompilerParams(vmem_limit_bytes=VMEM_LIMIT),
    )(*args)


def route(value, target):
    size_x, size_y = lax.axis_size("gx"), lax.axis_size("gy")
    pairs = []
    for i in range(size_x):
        for j in range(size_y):
            to = target(i, j)
            if to is not None:
                pairs.append((i * size_y + j, to[0] % size_x * size_y + to[1] % size_y))
    return lax.ppermute(value, ("gx", "gy"), pairs)


def swap(value):
    return route(value, lambda i, j: (i ^ 1, j))


def exchange(rows):
    return lax.all_to_all(rows, ("gx", "gy"), 0, 0, tiled=True)


def merge(value, parts):
    for part in parts:
        value = jnp.where(value != 0.0, value, part)
    return value


def spread(value):
    size_x, size_y = lax.axis_size("gx"), lax.axis_size("gy")
    half = size_y // 2

    def across(first, second):
        def target(i, j):
            dy, dz = second if i % 2 else first
            return i, (j // half + dz) % 2 * half + (j % half + dy) % half

        return target

    def along(block, step, first, second):
        def target(i, j):
            move = second if i % 2 else first
            if move is None:
                return None
            return i // block * block + (i % block + move * step) % block, j

        return target

    value = merge(value, [swap(value)])
    turns = [((1, 0), (1, 1)), ((3, 0), (3, 1)), ((2, 0), (2, 1)), ((0, 1), (0, 1))]
    value = merge(value, [route(value, across(*turn)) for turn in turns])
    value = merge(value, [swap(value)])
    for block, step in ((8, 2), (size_x, 8)):
        turns = [(1, 2), (3, None)]
        value = merge(value, [route(value, along(block, step, *turn)) for turn in turns])
        value = merge(value, [swap(value)])
    return value


def shift(value, axis, step):
    size = lax.axis_size(axis)
    return lax.ppermute(value, axis, [(i, (i + step) % size) for i in range(size)])


def region(checkpoint, cotangent):
    edge = MARGIN * NZ
    span = checkpoint.shape[2]
    first = jnp.concatenate([checkpoint[:, :, :edge], cotangent[:, :, :edge]], axis=0)
    last = jnp.concatenate([checkpoint[:, :, span - edge :], cotangent[:, :, span - edge :]], axis=0)
    before, after = shift(last, "gy", 1), shift(first, "gy", -1)
    own = jnp.concatenate([checkpoint, cotangent], axis=0)
    own = jnp.concatenate([before, own, after], axis=2)
    return shift(own, "gx", 1), own, shift(own, "gx", -1)


def body(checkpoint, cotangent, blade_area, hub_tile, point_side, point_local):
    count_x, count_y = lax.axis_size("gx"), lax.axis_size("gy")
    index_x, index_y = lax.axis_index("gx"), lax.axis_index("gy")
    area = blade_area.reshape(NTURB, PTS)
    side = point_side.reshape(NTURB, PTS)
    local = point_local.reshape(NTURB, PTS)
    hub = hub_tile.reshape(NTURB, 1)
    cell_x = (hub // count_y + side // 3 - 1 - index_x) * CX + local // (CY * NZ) + MARGIN
    cell_y = (hub % count_y + side % 3 - 1 - index_y) * CY + local // NZ % CY + MARGIN
    cell_x = cell_x % (count_x * CX)
    cell_y = cell_y % (count_y * CY)
    inside = (cell_x < RX) & (cell_y < RY)
    cell_x = jnp.where(inside, cell_x, -1)
    cell_yz = jnp.where(inside, cell_y * NZ + local % NZ, -1)
    mine_y = (cell_y >= MARGIN) & (cell_y < MARGIN + CY)
    inverse = jnp.broadcast_to(1.0 / jnp.sum(area, 1, keepdims=True), (NTURB, 128))

    full = (19, RX, LANES)
    flat = (RX, LANES)
    row = (NTURB, 128)
    parts = region(checkpoint, cotangent)
    (spots,) = call(area_kernel, [(NTURB,) + flat], [], cell_x, cell_yz, area)

    s, v, rotor = [None] * 5, [None] * 5, [None] * 5
    table = (128, 128)
    every = (count_x * count_y, 128)
    s[1], v[1], cot, sums = call(first_kernel, [full, flat, full, every], [table], *parts, spots)
    for k in (1, 2, 3):
        last = k == 3
        s[k + 1], v[k + 1], rotor[k], sums = call(
            functools.partial(forward_kernel, last),
            [full, flat, row, every],
            [full, table] + ([flat] if last else []),
            *([s[k], v[k], spots, inverse, exchange(sums)] + ([cot] if last else [])),
        )
    adjoint = cot
    bar, drag = [None] * 5, [None] * 5
    for k in (4, 3, 2):
        first = k == 4
        args = [s[k], adjoint, spots, inverse, exchange(sums), v[k - 1]]
        outs = call(
            functools.partial(backward_kernel, first),
            [full, flat, row, every] + ([row] if first else []),
            [full, table],
            *(args + ([] if first else [rotor[k]])),
        )
        adjoint, drag[k - 1], bar[k], sums = outs[:4]
        if first:
            rotor[4] = outs[4]
    (points,) = call(
        gather_kernel,
        [(3 * NTURB, 128)],
        [],
        *([cell_x, jnp.where(mine_y, cell_yz, -1), cot] + drag[1:4] + v[1:] + rotor[1:] + bar[2:] + [inverse]),
    )
    points = spread(points)[:, :PTS]
    known, swing, slope = points[:NTURB], points[NTURB : 2 * NTURB], points[2 * NTURB :]
    total = jnp.sum(area * swing, 1, keepdims=True)
    grad_area = (known + total * slope).reshape(-1)
    bar[1] = total * inverse
    (grad,) = call(
        last_kernel,
        [(19, CX, CY * NZ)],
        [full, full],
        *(s[1], adjoint, spots, rotor[1], bar[1]),
    )
    return grad, grad_area


def solution(mesh):
    return jax.shard_map(
        body,
        mesh=mesh,
        in_specs=(P(None, "gx", "gy"), P(None, "gx", "gy"), P(), P(), P(), P()),
        out_specs=(P(None, "gx", "gy"), P()),
        check_vma=False,
    )
```

```python
import functools

import jax
import jax.numpy as jnp
import numpy as np
from jax import lax
from jax.experimental import pallas as pl
from jax.experimental.pallas import tpu as pltpu
from jax.sharding import PartitionSpec as P

NZ = 16
CX = 8
CY = 16
STEPS = 4
NTURB = 16
PTS = 96
MARGIN = 8
RX = CX + 2 * MARGIN
RY = CY + 2 * MARGIN
LANES = RY * NZ
OWN_ROWS = slice(MARGIN, MARGIN + CX)
OWN_LANE = MARGIN * NZ
OWN_SPAN = CY * NZ

VMEM_LIMIT = 8 * 1024 * 1024

TAU_ZERO = 0.52
SMAGORINSKY = 0.17 * 0.17
TINY = 1e-10
THRUST = 4.0
GHOST_RATES = np.array([1.05, 1.15, 1.25, 1.35, 1.45, 1.55, 1.65, 1.75, 1.85])
W_REST, W_AXIS, W_EDGE = 1.0 / 3.0, 1.0 / 18.0, 1.0 / 36.0

VECTORS = np.array(
    [(0, 0, 0), (1, 0, 0), (-1, 0, 0), (0, 1, 0), (0, -1, 0), (0, 0, 1), (0, 0, -1)]
    + [(1, 1, 0), (-1, -1, 0), (1, -1, 0), (-1, 1, 0), (1, 0, 1), (-1, 0, -1)]
    + [(1, 0, -1), (-1, 0, 1), (0, 1, 1), (0, -1, -1), (0, 1, -1), (0, -1, 1)]
)
OPPOSITE = [0] + [i + 1 if i % 2 else i - 1 for i in range(1, 19)]


def basis():
    c = VECTORS * 1.0
    weights = np.array([W_REST] + [W_AXIS] * 6 + [W_EDGE] * 12)
    x, y, z = c[:, 0], c[:, 1], c[:, 2]
    monomials = [np.ones(19), x, y, z, x * x, y * y, z * z, x * y, x * z, y * z]
    monomials += [x * y * y, x * z * z, y * x * x, y * z * z, z * x * x, z * y * y]
    monomials += [x * x * y * y, x * x * z * z, y * y * z * z]
    rows = []
    for entry in monomials:
        vector = entry * 1.0
        for sweep in range(2):
            for other in rows:
                vector = vector - np.sum(weights * vector * other) * other
        rows.append(vector / np.sqrt(np.sum(weights * vector * vector)))
    return np.stack(rows, 0)


def ghost_tables():
    rows = basis()
    odd = []
    for first, members in ((10, (1, 7, 11)), (12, (3, 7, 15)), (14, (5, 11, 15))):
        h = rows[first : first + 2][:, list(members)]
        rates = GHOST_RATES[first - 10 : first - 8]
        odd.append(np.diag([W_AXIS, W_EDGE, W_EDGE]) @ h.T @ np.diag(rates) @ h)
    even = rows[16:19][:, [0, 1, 3, 5, 7, 11, 15]]
    return odd, even, GHOST_RATES[6:9]


ODD, EVEN, EVEN_RATES = ghost_tables()
CLASS_W = [W_REST] + [W_AXIS] * 3 + [W_EDGE] * 3


def combine(coefs, values):
    total = None
    for coef, value in zip(coefs, values):
        coef = float(coef)
        if abs(coef) < 1e-12:
            continue
        term = value if coef == 1.0 else value * coef
        total = term if total is None else total + term
    return total


def split_parity(s):
    e = [s[i] + s[i + 1] for i in range(1, 19, 2)]
    o = [s[i] - s[i + 1] for i in range(1, 19, 2)]
    even = [s[0], e[0], e[1], e[2], e[3] + e[4], e[5] + e[6], e[7] + e[8]]
    cross = [e[3] - e[4], e[5] - e[6], e[7] - e[8]]
    odd_x = [o[0], o[3] + o[4], o[5] + o[6]]
    odd_y = [o[1], o[3] - o[4], o[7] + o[8]]
    odd_z = [o[2], o[5] - o[6], o[7] - o[8]]
    return even, cross, odd_x, odd_y, odd_z


def merge_parity(s, even, cross, odd_x, odd_y, odd_z):
    out = [s[0] + even[0]]
    for axis, odd in enumerate((odd_x, odd_y, odd_z)):
        out += [s[1 + 2 * axis] + (even[1 + axis] + odd[0])]
        out += [s[2 + 2 * axis] + (even[1 + axis] - odd[0])]
    pairs = ((odd_x[1], odd_y[1]), (odd_x[2], odd_z[1]), (odd_y[2], odd_z[2]))
    for family in range(3):
        first, second = pairs[family]
        base = 7 + 4 * family
        for sign, offset in ((1, 0), (-1, 2)):
            level = even[4 + family] + cross[family] if sign > 0 else even[4 + family] - cross[family]
            swing = first + second if sign > 0 else first - second
            out += [s[base + offset] + (level + swing), s[base + offset + 1] + (level - swing)]
    return out


def ghost_even(even, transpose):
    if transpose:
        even = [value * w for value, w in zip(even, CLASS_W)]
    m = [combine(EVEN[k], even) * float(EVEN_RATES[k]) for k in range(3)]
    out = [combine(EVEN[:, j], m) for j in range(7)]
    if not transpose:
        out = [value * w for value, w in zip(out, CLASS_W)]
    return out


def ghost_odd(index, odd, transpose):
    matrix = ODD[index].T if transpose else ODD[index]
    return [combine(matrix[j], odd) for j in range(3)]


def local_state(even, cross, odds):
    rho = ((even[0] + even[1]) + (even[2] + even[3])) + ((even[4] + even[5]) + even[6])
    inverse = 1.0 / rho
    mom = [(odd[0] + odd[1]) + odd[2] for odd in odds]
    u = [m * inverse for m in mom]
    third = rho * (1.0 / 3.0)
    edges = ((even[4], even[5]), (even[4], even[6]), (even[5], even[6]))
    stress = [
        ((even[1 + a] + edges[a][0]) + edges[a][1]) - third - mom[a] * u[a] for a in range(3)
    ]
    stress += [cross[0] - mom[0] * u[1], cross[1] - mom[0] * u[2], cross[2] - mom[1] * u[2]]
    square = stress[0] * stress[0] + stress[1] * stress[1] + stress[2] * stress[2]
    square = square + 2.0 * (
        stress[3] * stress[3] + stress[4] * stress[4] + stress[5] * stress[5]
    )
    norm = jnp.sqrt(square + TINY)
    root = jnp.sqrt(TAU_ZERO * TAU_ZERO + (18.0 * SMAGORINSKY) * norm * inverse)
    tau = 0.5 * (TAU_ZERO + root)
    return inverse, u, stress, norm, root, tau


def collide(s, force):
    even, cross, odd_x, odd_y, odd_z = split_parity(s)
    inverse, u, stress, norm, root, tau = local_state(even, cross, (odd_x, odd_y, odd_z))
    scale = 4.5 / tau
    k = [value * scale for value in stress]
    trace = (k[0] + k[1] + k[2]) * (1.0 / 3.0)
    relax = [-trace, k[0] - trace, k[1] - trace, k[2] - trace]
    relax += [k[0] + relax[2], k[0] + relax[3], k[1] + relax[3]]
    ghost = ghost_even(even, False)
    even_out = [-(relax[j] * CLASS_W[j] + ghost[j]) for j in range(7)]
    cross_out = [k[3 + j] * (-2.0 * W_EDGE) for j in range(3)]
    gx = ghost_odd(0, odd_x, False)
    ox = [force * (1.0 / 6.0) - gx[0], force * (1.0 / 12.0) - gx[1], force * (1.0 / 12.0) - gx[2]]
    oy = [-value for value in ghost_odd(1, odd_y, False)]
    oz = [-value for value in ghost_odd(2, odd_z, False)]
    return merge_parity(s, even_out, cross_out, ox, oy, oz)


def collide_adjoint(s, a, speed_bar):
    even, cross, odd_x, odd_y, odd_z = split_parity(s)
    inverse, u, stress, norm, root, tau = local_state(even, cross, (odd_x, odd_y, odd_z))
    ev, cr, ax, ay, az = split_parity(a)
    weighted = [value * w for value, w in zip(ev, CLASS_W)]
    total = ((weighted[0] + weighted[1]) + (weighted[2] + weighted[3])) + (
        (weighted[4] + weighted[5]) + weighted[6]
    )
    third = total * (1.0 / 3.0)
    edges = ((4, 5), (4, 6), (5, 6))
    beta = [
        (weighted[1 + i] + weighted[edges[i][0]] + weighted[edges[i][1]] - third) * -4.5
        for i in range(3)
    ]
    beta += [value * (-9.0 * W_EDGE) for value in cr]
    inv_tau = 1.0 / tau
    dot = (beta[0] * stress[0] + beta[1] * stress[1] + beta[2] * stress[2]) + (
        beta[3] * stress[3] + beta[4] * stress[4] + beta[5] * stress[5]
    )
    tau_bar = -dot * inv_tau * inv_tau
    common = tau_bar * (4.5 * SMAGORINSKY) * inverse / root
    factor = common / norm
    p_bar = [beta[i] * inv_tau + stress[i] * factor for i in range(3)]
    twice = factor + factor
    p_bar += [beta[i] * inv_tau + stress[i] * twice for i in range(3, 6)]
    sp = speed_bar * inverse
    px, py, pz, pxy, pxz, pyz = p_bar
    tx = pxy * u[1] + pxz * u[2]
    ty = pyz * u[2]
    mx = sp - (2.0 * px * u[0] + tx)
    my = -(2.0 * py * u[1] + pxy * u[0] + ty)
    mz = -(2.0 * pz * u[2] + pxz * u[0] + pyz * u[1])
    rho_bar = -common * norm * inverse - (px + py + pz) * (1.0 / 3.0)
    rho_bar = rho_bar + (px * u[0] + tx) * u[0] + (py * u[1] + ty) * u[1] + pz * u[2] * u[2]
    rho_bar = rho_bar - sp * u[0]
    ghost = ghost_even(ev, True)
    level = [rho_bar, rho_bar + px, rho_bar + py, rho_bar + pz]
    level += [level[1] + py, level[1] + pz, level[2] + pz]
    even_out = [level[j] - ghost[j] for j in range(7)]
    gx, gy, gz = (ghost_odd(i, odd, True) for i, odd in enumerate((ax, ay, az)))
    ox = [mx - value for value in gx]
    oy = [my - value for value in gy]
    oz = [mz - value for value in gz]
    return merge_parity(a, even_out, p_bar[3:], ox, oy, oz)


def chunks(body):
    def step(index, carry):
        lane = pl.multiple_of(index * 128, 128)
        for row in range(0, RX, 8):
            body(pl.ds(row, 8), pl.ds(lane, 128))
        return carry

    lax.fori_loop(0, LANES // 128, step, 0)


def shifted(value, cx, cy, cz):
    lane = (NZ * cy + cz) % LANES
    if lane:
        value = pltpu.roll(value, lane, 1)
    if cx % RX:
        value = pltpu.roll(value, cx % RX, 0)
    return value


def height():
    return lax.broadcasted_iota(jnp.int32, (RX, LANES), 1) & (NZ - 1)


def stream(field, out):
    z = height()
    for i in range(19):
        cx, cy, cz = (int(v) for v in VECTORS[i])
        value = shifted(field[i], cx, cy, cz)
        if cz:
            value = jnp.where(z == (0 if cz > 0 else NZ - 1), field[OPPOSITE[i]], value)
        out[i] = value


def stream_adjoint(field, out):
    z = height()
    for i in range(19):
        cx, cy, cz = (int(v) for v in VECTORS[i])
        value = field[i]
        if cz:
            value = jnp.where(z == (0 if cz > 0 else NZ - 1), 0.0, value)
        value = shifted(value, -cx, -cy, -cz)
        if cz:
            value = value + jnp.where(z == (NZ - 1 if cz > 0 else 0), field[OPPOSITE[i]], 0.0)
        out[i] = value


def speeds(s_ref, v_ref):
    def one(rows, lanes):
        s = [s_ref[i, rows, lanes] for i in range(19)]
        even, cross, odd_x, odd_y, odd_z = split_parity(s)
        rho = ((even[0] + even[1]) + (even[2] + even[3])) + ((even[4] + even[5]) + even[6])
        v_ref[rows, lanes] = ((odd_x[0] + odd_x[1]) + odd_x[2]) / rho

    chunks(one)


def push_back(a):
    odd = (a[7] - a[8]) + (a[9] - a[10]) + (a[11] - a[12]) + (a[13] - a[14])
    return (a[1] - a[2]) * (1.0 / 6.0) + odd * (1.0 / 12.0)


def turbine_sums(area_ref, field_ref, sums_ref, base):
    parts = [field_ref[OWN_ROWS, OWN_LANE + j : OWN_LANE + j + 128] for j in range(0, OWN_SPAN, 128)]
    for t in range(NTURB):
        total = None
        for j, part in enumerate(parts):
            lane = OWN_LANE + 128 * j
            term = area_ref[t, OWN_ROWS, lane : lane + 128] * part
            total = term if total is None else total + term
        sums_ref[base + t : base + t + 1, :] = jnp.sum(total, axis=0, keepdims=True)


def publish(sums_ref, out_ref):
    ones = jnp.ones((8, 128), jnp.bfloat16)
    row = None
    for part in split_three(sums_ref[...]):
        term = lax.dot_general(
            ones, part, (((1,), (1,)), ((), ())), preferred_element_type=jnp.float32
        )
        row = term if row is None else row + term
    for j in range(0, out_ref.shape[0], 8):
        out_ref[j : j + 8, :] = row


def totals(got_ref, base):
    row = jnp.sum(got_ref[...], axis=0, keepdims=True)
    index = lax.broadcasted_iota(jnp.int32, (NTURB, 128), 0) + base
    lane = lax.broadcasted_iota(jnp.int32, (NTURB, 128), 1)
    picked = jnp.where(index == lane, jnp.broadcast_to(row, (NTURB, 128)), 0.0)
    return jnp.broadcast_to(jnp.sum(picked, axis=1, keepdims=True), (NTURB, 128))


def weighted_area(area_ref, weight_ref, rows, lanes):
    total = None
    for t in range(NTURB):
        term = area_ref[t, rows, lanes] * weight_ref[t : t + 1, :]
        total = term if total is None else total + term
    return total


def split_three(value):
    high = value.astype(jnp.bfloat16)
    rest = value - high.astype(jnp.float32)
    middle = rest.astype(jnp.bfloat16)
    return high, middle, (rest - middle.astype(jnp.float32)).astype(jnp.bfloat16)


def area_kernel(x_ref, yz_ref, area_ref, out_ref):
    rows = lax.broadcasted_iota(jnp.int32, (RX, PTS), 0)
    columns = lax.broadcasted_iota(jnp.int32, (LANES, PTS), 0)

    def one(t, carry):
        point = pl.ds(t, 1)
        spots = jnp.where(rows == x_ref[point, :], area_ref[point, :], 0.0)
        left = jnp.concatenate(split_three(spots), axis=0)
        hot = jnp.where(columns == yz_ref[point, :], 1.0, 0.0).astype(jnp.bfloat16)
        product = lax.dot_general(
            left, hot, (((1,), (1,)), ((), ())), preferred_element_type=jnp.float32
        )
        out_ref[t] = product[:RX] + product[RX : 2 * RX] + product[2 * RX :]
        return carry

    lax.fori_loop(0, NTURB, one, 0)


def pack_x_kernel(field_ref, cot_ref, next_ref, prev_ref):
    half = OWN_SPAN // 2
    top = lax.broadcasted_iota(jnp.int32, (CX, half), 0) < CX // 2
    for i in range(19):
        low, high = cot_ref[i, :, :half], cot_ref[i, :, half:]
        next_ref[i, :, :OWN_SPAN] = field_ref[i]
        prev_ref[i, :, :OWN_SPAN] = field_ref[i]
        next_ref[i, :, OWN_SPAN:] = jnp.where(top, pltpu.roll(low, CX // 2, 0), high)
        prev_ref[i, :, OWN_SPAN:] = jnp.where(top, low, pltpu.roll(high, CX // 2, 0))


def pack_y_kernel(field_ref, cot_ref, before_ref, after_ref, fields_ref, cots_ref, next_ref, prev_ref):
    half = OWN_SPAN // 2
    top = lax.broadcasted_iota(jnp.int32, (CX, half), 0) < CX // 2
    left = lax.broadcasted_iota(jnp.int32, (CX, half), 1) < half // 2
    for i in range(19):
        for j, part in enumerate((before_ref[i, :, :OWN_SPAN], field_ref[i], after_ref[i, :, :OWN_SPAN])):
            rows = slice(CX * j, CX * (j + 1))
            fields_ref[i, rows] = part
            prev_ref[i, rows] = part[:, :half]
            next_ref[i, rows] = part[:, half:]
        before, after = before_ref[i, :, OWN_SPAN:], after_ref[i, :, OWN_SPAN:]
        low = (pltpu.roll(before, CX // 2, 0), cot_ref[i, :, :half], after)
        high = (before, cot_ref[i, :, half:], pltpu.roll(after, CX // 2, 0))
        for j in range(3):
            rows = slice(CX * j, CX * (j + 1))
            cots_ref[i, rows, :half] = low[j]
            cots_ref[i, rows, half:] = high[j]
        outer = jnp.where(top, low[2], low[0])
        prev_ref[i, RX:] = jnp.where(left, low[1], pltpu.roll(outer, half // 2, 1))
        outer = jnp.where(top, high[2], high[0])
        next_ref[i, RX:] = jnp.where(left, pltpu.roll(high[1], half // 2, 1), outer)


class Joined:
    def __init__(self, before, here, after):
        self.parts = before, here, after

    def __getitem__(self, index):
        before, here, after = self.parts
        return jnp.concatenate([before[index, :RX], here[index], after[index, :RX]], axis=1)


def first_kernel(before_ref, fields_ref, after_ref, cots_ref, area_ref, s_ref, v_ref, cot_ref, out_ref, sums):
    stream(Joined(before_ref, fields_ref, after_ref), s_ref)
    speeds(s_ref, v_ref)
    sums[...] = jnp.zeros_like(sums)
    turbine_sums(area_ref, v_ref, sums, 0)
    publish(sums, out_ref)
    half = OWN_SPAN // 2
    for i in range(19):
        before, after = before_ref[i, RX:], after_ref[i, RX:]
        turned = pltpu.roll(before, half // 2, 1), pltpu.roll(after, half // 2, 1)
        for j in range(3):
            rows = slice(CX * j, CX * (j + 1))
            cot_ref[i, rows, :OWN_LANE] = turned[0] if j == 1 else before
            cot_ref[i, rows, OWN_LANE + OWN_SPAN :] = after if j == 1 else turned[1]
        cot_ref[i, :, OWN_LANE : OWN_LANE + OWN_SPAN] = cots_ref[i]


def forward_kernel(last, s_ref, v_ref, area_ref, inv_ref, got_ref, *rest):
    if last:
        cot_ref, next_ref, vn_ref, rotor_ref, out_ref, field, sums, drag = rest
    else:
        next_ref, vn_ref, rotor_ref, out_ref, field, sums = rest
    rotor_ref[...] = totals(got_ref, 0) * inv_ref[...]

    def one(rows, lanes):
        s = [s_ref[i, rows, lanes] for i in range(19)]
        force = weighted_area(area_ref, rotor_ref, rows, lanes) * v_ref[rows, lanes] * -THRUST
        for i, value in enumerate(collide(s, force)):
            field[i, rows, lanes] = value

    chunks(one)
    stream(field, next_ref)
    speeds(next_ref, vn_ref)
    sums[...] = jnp.zeros_like(sums)
    turbine_sums(area_ref, vn_ref, sums, 0)
    if last:

        def other(rows, lanes):
            a = [cot_ref[i, rows, lanes] for i in range(19)]
            drag[rows, lanes] = push_back(a) * vn_ref[rows, lanes] * -THRUST

        chunks(other)
        turbine_sums(area_ref, drag, sums, NTURB)
    publish(sums, out_ref)


def adjoint_field(s_ref, a_ref, area_ref, rotor_ref, bar_ref, field):
    def one(rows, lanes):
        s = [s_ref[i, rows, lanes] for i in range(19)]
        a = [a_ref[i, rows, lanes] for i in range(19)]
        speed_bar = weighted_area(area_ref, rotor_ref, rows, lanes) * push_back(a) * -THRUST
        speed_bar = speed_bar + weighted_area(area_ref, bar_ref, rows, lanes)
        for i, value in enumerate(collide_adjoint(s, a, speed_bar)):
            field[i, rows, lanes] = value

    chunks(one)


def backward_kernel(first, s_ref, a_ref, area_ref, inv_ref, got_ref, v_ref, *rest):
    if first:
        out_ref, drag_ref, bar_ref, publish_ref, rotor_ref, field, sums = rest
        rotor_ref[...] = totals(got_ref, 0) * inv_ref[...]
    else:
        rotor_ref, out_ref, drag_ref, bar_ref, publish_ref, field, sums = rest
    bar_ref[...] = totals(got_ref, NTURB if first else 0) * inv_ref[...]
    adjoint_field(s_ref, a_ref, area_ref, rotor_ref, bar_ref, field)
    stream_adjoint(field, out_ref)

    def other(rows, lanes):
        a = [out_ref[i, rows, lanes] for i in range(19)]
        drag_ref[rows, lanes] = push_back(a) * v_ref[rows, lanes] * -THRUST

    chunks(other)
    sums[...] = jnp.zeros_like(sums)
    turbine_sums(area_ref, drag_ref, sums, 0)
    publish(sums, publish_ref)


def last_kernel(s_ref, a_ref, area_ref, rotor_ref, bar_ref, out_ref, field, result):
    adjoint_field(s_ref, a_ref, area_ref, rotor_ref, bar_ref, field)
    stream_adjoint(field, result)
    for i in range(19):
        out_ref[i] = result[i, OWN_ROWS, OWN_LANE : OWN_LANE + OWN_SPAN]


def gather_kernel(x_ref, yz_ref, cot_ref, q1, q2, q3, v1, v2, v3, v4, u1, u2, u3, u4, n2, n3, n4, inv, out_ref):
    own = (OWN_ROWS, slice(OWN_LANE, OWN_LANE + OWN_SPAN))
    v = [ref[own] for ref in (v1, v2, v3, v4)]
    q = [ref[own] for ref in (q1, q2, q3)]
    a = [cot_ref[(i,) + own] for i in range(19)]
    q.append(push_back(a) * v[3] * -THRUST)
    rows = lax.broadcasted_iota(jnp.int32, (CX, PTS), 0) + MARGIN
    columns = lax.broadcasted_iota(jnp.int32, (OWN_SPAN, PTS), 0) + OWN_LANE

    def wide(ref, t):
        return jnp.concatenate([ref[pl.ds(t, 1), :]] * (OWN_SPAN // 128), axis=1)

    out_ref[...] = jnp.zeros_like(out_ref)

    def one(t, carry):
        u = [wide(ref, t) for ref in (u1, u2, u3, u4)]
        n = [None] + [wide(ref, t) for ref in (n2, n3, n4)]
        known = u[0] * q[0]
        for k in range(1, 4):
            known = known + u[k] * q[k] + n[k] * (v[k] - u[k])
        fields = [known, q[0], (v[0] - u[0]) * wide(inv, t)]
        left = jnp.concatenate(split_three(jnp.concatenate(fields, axis=0)), axis=0)
        hot = jnp.where(columns == yz_ref[pl.ds(t, 1), :], 1.0, 0.0).astype(jnp.bfloat16)
        product = jnp.dot(left, hot, preferred_element_type=jnp.float32)
        size = 3 * CX
        product = product[:size] + product[size : 2 * size] + product[2 * size :]
        mine = rows == x_ref[pl.ds(t, 1), :]
        for j in range(3):
            picked = jnp.where(mine, product[CX * j : CX * (j + 1)], 0.0)
            out_ref[pl.ds(j * NTURB + t, 1), 0:PTS] = jnp.sum(picked, axis=0, keepdims=True)
        return carry

    lax.fori_loop(0, NTURB, one, 0)


def call(kernel, outs, scratch, *args):
    vmem = pl.BlockSpec(memory_space=pltpu.VMEM)
    return pl.pallas_call(
        kernel,
        out_shape=[jax.ShapeDtypeStruct(shape, jnp.float32) for shape in outs],
        in_specs=[vmem] * len(args),
        out_specs=[vmem] * len(outs),
        scratch_shapes=[pltpu.VMEM(shape, jnp.float32) for shape in scratch],
        compiler_params=pltpu.CompilerParams(vmem_limit_bytes=VMEM_LIMIT),
    )(*args)


def route(value, target):
    size_x, size_y = lax.axis_size("gx"), lax.axis_size("gy")
    pairs = []
    for i in range(size_x):
        for j in range(size_y):
            to = target(i, j)
            if to is not None:
                pairs.append((i * size_y + j, to[0] % size_x * size_y + to[1] % size_y))
    return lax.ppermute(value, ("gx", "gy"), pairs)


def swap(value):
    return route(value, lambda i, j: (i ^ 1, j))


def exchange(rows):
    return lax.all_to_all(rows, ("gx", "gy"), 0, 0, tiled=True)


def merge(value, parts):
    for part in parts:
        value = jnp.where(value != 0.0, value, part)
    return value


def spread(value):
    size_x, size_y = lax.axis_size("gx"), lax.axis_size("gy")
    half = size_y // 2

    def across(first, second):
        def target(i, j):
            dy, dz = second if i % 2 else first
            return i, (j // half + dz) % 2 * half + (j % half + dy) % half

        return target

    def along(block, step, first, second):
        def target(i, j):
            move = second if i % 2 else first
            if move is None:
                return None
            return i // block * block + (i % block + move * step) % block, j

        return target

    value = merge(value, [swap(value)])
    turns = [((1, 0), (1, 1)), ((3, 0), (3, 1)), ((2, 0), (2, 1)), ((0, 1), (0, 1))]
    value = merge(value, [route(value, across(*turn)) for turn in turns])
    value = merge(value, [swap(value)])
    for block, step in ((8, 2), (size_x, 8)):
        turns = [(1, 2), (3, None)]
        value = merge(value, [route(value, along(block, step, *turn)) for turn in turns])
        value = merge(value, [swap(value)])
    return value


def shift(value, axis, step):
    size = lax.axis_size(axis)
    return lax.ppermute(value, axis, [(i, (i + step) % size) for i in range(size)])


def region(checkpoint, cotangent):
    wide = (19, CX, OWN_SPAN + OWN_SPAN // 2)
    right, left = call(pack_x_kernel, [wide] * 2, [], checkpoint, cotangent)
    before, after = shift(right, "gx", 1), shift(left, "gx", -1)
    stack, edge = (19, RX, OWN_SPAN), (19, RX + CX, OWN_SPAN // 2)
    fields, cots, right, left = call(
        pack_y_kernel, [stack, stack, edge, edge], [], checkpoint, cotangent, before, after
    )
    return shift(right, "gy", 1), fields, shift(left, "gy", -1), cots


def body(checkpoint, cotangent, blade_area, hub_tile, point_side, point_local):
    count_x, count_y = lax.axis_size("gx"), lax.axis_size("gy")
    index_x, index_y = lax.axis_index("gx"), lax.axis_index("gy")
    area = blade_area.reshape(NTURB, PTS)
    side = point_side.reshape(NTURB, PTS)
    local = point_local.reshape(NTURB, PTS)
    hub = hub_tile.reshape(NTURB, 1)
    cell_x = (hub // count_y + side // 3 - 1 - index_x) * CX + local // (CY * NZ) + MARGIN
    cell_y = (hub % count_y + side % 3 - 1 - index_y) * CY + local // NZ % CY + MARGIN
    cell_x = cell_x % (count_x * CX)
    cell_y = cell_y % (count_y * CY)
    inside = (cell_x < RX) & (cell_y < RY)
    cell_x = jnp.where(inside, cell_x, -1)
    cell_yz = jnp.where(inside, cell_y * NZ + local % NZ, -1)
    mine_y = (cell_y >= MARGIN) & (cell_y < MARGIN + CY)
    inverse = jnp.broadcast_to(1.0 / jnp.sum(area, 1, keepdims=True), (NTURB, 128))

    full = (19, RX, LANES)
    flat = (RX, LANES)
    row = (NTURB, 128)
    parts = region(checkpoint, cotangent)
    (spots,) = call(area_kernel, [(NTURB,) + flat], [], cell_x, cell_yz, area)

    s, v, rotor = [None] * 5, [None] * 5, [None] * 5
    table = (128, 128)
    every = (count_x * count_y, 128)
    s[1], v[1], cot, sums = call(first_kernel, [full, flat, full, every], [table], *parts, spots)
    for k in (1, 2, 3):
        last = k == 3
        s[k + 1], v[k + 1], rotor[k], sums = call(
            functools.partial(forward_kernel, last),
            [full, flat, row, every],
            [full, table] + ([flat] if last else []),
            *([s[k], v[k], spots, inverse, exchange(sums)] + ([cot] if last else [])),
        )
    adjoint = cot
    bar, drag = [None] * 5, [None] * 5
    for k in (4, 3, 2):
        first = k == 4
        args = [s[k], adjoint, spots, inverse, exchange(sums), v[k - 1]]
        outs = call(
            functools.partial(backward_kernel, first),
            [full, flat, row, every] + ([row] if first else []),
            [full, table],
            *(args + ([] if first else [rotor[k]])),
        )
        adjoint, drag[k - 1], bar[k], sums = outs[:4]
        if first:
            rotor[4] = outs[4]
    (points,) = call(
        gather_kernel,
        [(3 * NTURB, 128)],
        [],
        *([cell_x, jnp.where(mine_y, cell_yz, -1), cot] + drag[1:4] + v[1:] + rotor[1:] + bar[2:] + [inverse]),
    )
    points = spread(points)[:, :PTS]
    known, swing, slope = points[:NTURB], points[NTURB : 2 * NTURB], points[2 * NTURB :]
    total = jnp.sum(area * swing, 1, keepdims=True)
    grad_area = (known + total * slope).reshape(-1)
    bar[1] = total * inverse
    (grad,) = call(
        last_kernel,
        [(19, CX, CY * NZ)],
        [full, full],
        *(s[1], adjoint, spots, rotor[1], bar[1]),
    )
    return grad, grad_area


def solution(mesh):
    return jax.shard_map(
        body,
        mesh=mesh,
        in_specs=(P(None, "gx", "gy"), P(None, "gx", "gy"), P(), P(), P(), P()),
        out_specs=(P(None, "gx", "gy"), P()),
        check_vma=False,
    )
```

```python
import functools

import jax
import jax.numpy as jnp
import numpy as np
from jax import lax
from jax.experimental import pallas as pl
from jax.experimental.pallas import tpu as pltpu
from jax.sharding import PartitionSpec as P

NZ = 16
CX = 8
CY = 16
STEPS = 4
NTURB = 16
PTS = 96
MARGIN = 8
RX = CX + 2 * MARGIN
RY = CY + 2 * MARGIN
LANES = RY * NZ
OWN_ROWS = slice(MARGIN, MARGIN + CX)
OWN_LANE = MARGIN * NZ
OWN_SPAN = CY * NZ

VMEM_LIMIT = 8 * 1024 * 1024

TAU_ZERO = 0.52
SMAGORINSKY = 0.17 * 0.17
TINY = 1e-10
THRUST = 4.0
GHOST_RATES = np.array([1.05, 1.15, 1.25, 1.35, 1.45, 1.55, 1.65, 1.75, 1.85])
W_REST, W_AXIS, W_EDGE = 1.0 / 3.0, 1.0 / 18.0, 1.0 / 36.0

VECTORS = np.array(
    [(0, 0, 0), (1, 0, 0), (-1, 0, 0), (0, 1, 0), (0, -1, 0), (0, 0, 1), (0, 0, -1)]
    + [(1, 1, 0), (-1, -1, 0), (1, -1, 0), (-1, 1, 0), (1, 0, 1), (-1, 0, -1)]
    + [(1, 0, -1), (-1, 0, 1), (0, 1, 1), (0, -1, -1), (0, 1, -1), (0, -1, 1)]
)
OPPOSITE = [0] + [i + 1 if i % 2 else i - 1 for i in range(1, 19)]


def basis():
    c = VECTORS * 1.0
    weights = np.array([W_REST] + [W_AXIS] * 6 + [W_EDGE] * 12)
    x, y, z = c[:, 0], c[:, 1], c[:, 2]
    monomials = [np.ones(19), x, y, z, x * x, y * y, z * z, x * y, x * z, y * z]
    monomials += [x * y * y, x * z * z, y * x * x, y * z * z, z * x * x, z * y * y]
    monomials += [x * x * y * y, x * x * z * z, y * y * z * z]
    rows = []
    for entry in monomials:
        vector = entry * 1.0
        for sweep in range(2):
            for other in rows:
                vector = vector - np.sum(weights * vector * other) * other
        rows.append(vector / np.sqrt(np.sum(weights * vector * vector)))
    return np.stack(rows, 0)


def ghost_tables():
    rows = basis()
    odd = []
    for first, members in ((10, (1, 7, 11)), (12, (3, 7, 15)), (14, (5, 11, 15))):
        h = rows[first : first + 2][:, list(members)]
        rates = GHOST_RATES[first - 10 : first - 8]
        odd.append(np.diag([W_AXIS, W_EDGE, W_EDGE]) @ h.T @ np.diag(rates) @ h)
    even = rows[16:19][:, [0, 1, 3, 5, 7, 11, 15]]
    return odd, even, GHOST_RATES[6:9]


ODD, EVEN, EVEN_RATES = ghost_tables()
CLASS_W = [W_REST] + [W_AXIS] * 3 + [W_EDGE] * 3


def combine(coefs, values):
    total = None
    for coef, value in zip(coefs, values):
        coef = float(coef)
        if abs(coef) < 1e-12:
            continue
        term = value if coef == 1.0 else value * coef
        total = term if total is None else total + term
    return total


def split_parity(s):
    e = [s[i] + s[i + 1] for i in range(1, 19, 2)]
    o = [s[i] - s[i + 1] for i in range(1, 19, 2)]
    even = [s[0], e[0], e[1], e[2], e[3] + e[4], e[5] + e[6], e[7] + e[8]]
    cross = [e[3] - e[4], e[5] - e[6], e[7] - e[8]]
    odd_x = [o[0], o[3] + o[4], o[5] + o[6]]
    odd_y = [o[1], o[3] - o[4], o[7] + o[8]]
    odd_z = [o[2], o[5] - o[6], o[7] - o[8]]
    return even, cross, odd_x, odd_y, odd_z


def merge_parity(s, even, cross, odd_x, odd_y, odd_z):
    out = [s[0] + even[0]]
    for axis, odd in enumerate((odd_x, odd_y, odd_z)):
        out += [s[1 + 2 * axis] + (even[1 + axis] + odd[0])]
        out += [s[2 + 2 * axis] + (even[1 + axis] - odd[0])]
    pairs = ((odd_x[1], odd_y[1]), (odd_x[2], odd_z[1]), (odd_y[2], odd_z[2]))
    for family in range(3):
        first, second = pairs[family]
        base = 7 + 4 * family
        for sign, offset in ((1, 0), (-1, 2)):
            level = even[4 + family] + cross[family] if sign > 0 else even[4 + family] - cross[family]
            swing = first + second if sign > 0 else first - second
            out += [s[base + offset] + (level + swing), s[base + offset + 1] + (level - swing)]
    return out


def ghost_even(even, transpose):
    if transpose:
        even = [value * w for value, w in zip(even, CLASS_W)]
    m = [combine(EVEN[k], even) * float(EVEN_RATES[k]) for k in range(3)]
    out = [combine(EVEN[:, j], m) for j in range(7)]
    if not transpose:
        out = [value * w for value, w in zip(out, CLASS_W)]
    return out


def ghost_odd(index, odd, transpose):
    matrix = ODD[index].T if transpose else ODD[index]
    return [combine(matrix[j], odd) for j in range(3)]


def local_state(even, cross, odds):
    rho = ((even[0] + even[1]) + (even[2] + even[3])) + ((even[4] + even[5]) + even[6])
    inverse = 1.0 / rho
    mom = [(odd[0] + odd[1]) + odd[2] for odd in odds]
    u = [m * inverse for m in mom]
    third = rho * (1.0 / 3.0)
    edges = ((even[4], even[5]), (even[4], even[6]), (even[5], even[6]))
    stress = [
        ((even[1 + a] + edges[a][0]) + edges[a][1]) - third - mom[a] * u[a] for a in range(3)
    ]
    stress += [cross[0] - mom[0] * u[1], cross[1] - mom[0] * u[2], cross[2] - mom[1] * u[2]]
    square = stress[0] * stress[0] + stress[1] * stress[1] + stress[2] * stress[2]
    square = square + 2.0 * (
        stress[3] * stress[3] + stress[4] * stress[4] + stress[5] * stress[5]
    )
    norm = jnp.sqrt(square + TINY)
    root = jnp.sqrt(TAU_ZERO * TAU_ZERO + (18.0 * SMAGORINSKY) * norm * inverse)
    tau = 0.5 * (TAU_ZERO + root)
    return inverse, u, stress, norm, root, tau


def collide(s, force):
    even, cross, odd_x, odd_y, odd_z = split_parity(s)
    inverse, u, stress, norm, root, tau = local_state(even, cross, (odd_x, odd_y, odd_z))
    scale = 4.5 / tau
    k = [value * scale for value in stress]
    trace = (k[0] + k[1] + k[2]) * (1.0 / 3.0)
    relax = [-trace, k[0] - trace, k[1] - trace, k[2] - trace]
    relax += [k[0] + relax[2], k[0] + relax[3], k[1] + relax[3]]
    ghost = ghost_even(even, False)
    even_out = [-(relax[j] * CLASS_W[j] + ghost[j]) for j in range(7)]
    cross_out = [k[3 + j] * (-2.0 * W_EDGE) for j in range(3)]
    gx = ghost_odd(0, odd_x, False)
    ox = [force * (1.0 / 6.0) - gx[0], force * (1.0 / 12.0) - gx[1], force * (1.0 / 12.0) - gx[2]]
    oy = [-value for value in ghost_odd(1, odd_y, False)]
    oz = [-value for value in ghost_odd(2, odd_z, False)]
    return merge_parity(s, even_out, cross_out, ox, oy, oz)


def collide_adjoint(s, a, speed_bar):
    even, cross, odd_x, odd_y, odd_z = split_parity(s)
    inverse, u, stress, norm, root, tau = local_state(even, cross, (odd_x, odd_y, odd_z))
    ev, cr, ax, ay, az = split_parity(a)
    weighted = [value * w for value, w in zip(ev, CLASS_W)]
    total = ((weighted[0] + weighted[1]) + (weighted[2] + weighted[3])) + (
        (weighted[4] + weighted[5]) + weighted[6]
    )
    third = total * (1.0 / 3.0)
    edges = ((4, 5), (4, 6), (5, 6))
    beta = [
        (weighted[1 + i] + weighted[edges[i][0]] + weighted[edges[i][1]] - third) * -4.5
        for i in range(3)
    ]
    beta += [value * (-9.0 * W_EDGE) for value in cr]
    inv_tau = 1.0 / tau
    dot = (beta[0] * stress[0] + beta[1] * stress[1] + beta[2] * stress[2]) + (
        beta[3] * stress[3] + beta[4] * stress[4] + beta[5] * stress[5]
    )
    tau_bar = -dot * inv_tau * inv_tau
    common = tau_bar * (4.5 * SMAGORINSKY) * inverse / root
    factor = common / norm
    p_bar = [beta[i] * inv_tau + stress[i] * factor for i in range(3)]
    twice = factor + factor
    p_bar += [beta[i] * inv_tau + stress[i] * twice for i in range(3, 6)]
    sp = speed_bar * inverse
    px, py, pz, pxy, pxz, pyz = p_bar
    tx = pxy * u[1] + pxz * u[2]
    ty = pyz * u[2]
    mx = sp - (2.0 * px * u[0] + tx)
    my = -(2.0 * py * u[1] + pxy * u[0] + ty)
    mz = -(2.0 * pz * u[2] + pxz * u[0] + pyz * u[1])
    rho_bar = -common * norm * inverse - (px + py + pz) * (1.0 / 3.0)
    rho_bar = rho_bar + (px * u[0] + tx) * u[0] + (py * u[1] + ty) * u[1] + pz * u[2] * u[2]
    rho_bar = rho_bar - sp * u[0]
    ghost = ghost_even(ev, True)
    level = [rho_bar, rho_bar + px, rho_bar + py, rho_bar + pz]
    level += [level[1] + py, level[1] + pz, level[2] + pz]
    even_out = [level[j] - ghost[j] for j in range(7)]
    gx, gy, gz = (ghost_odd(i, odd, True) for i, odd in enumerate((ax, ay, az)))
    ox = [mx - value for value in gx]
    oy = [my - value for value in gy]
    oz = [mz - value for value in gz]
    return merge_parity(a, even_out, p_bar[3:], ox, oy, oz)


def chunks(body):
    def step(index, carry):
        lane = pl.multiple_of(index * 128, 128)
        for row in range(0, RX, 8):
            body(pl.ds(row, 8), pl.ds(lane, 128))
        return carry

    lax.fori_loop(0, LANES // 128, step, 0)


def shifted(value, cx, cy, cz):
    lane = (NZ * cy + cz) % LANES
    if lane:
        value = pltpu.roll(value, lane, 1)
    if cx % RX:
        value = pltpu.roll(value, cx % RX, 0)
    return value


def height():
    return lax.broadcasted_iota(jnp.int32, (RX, LANES), 1) & (NZ - 1)


def stream(field, out):
    z = height()
    for i in range(19):
        cx, cy, cz = (int(v) for v in VECTORS[i])
        value = shifted(field[i], cx, cy, cz)
        if cz:
            value = jnp.where(z == (0 if cz > 0 else NZ - 1), field[OPPOSITE[i]], value)
        out[i] = value


def stream_adjoint(field, out):
    z = height()
    for i in range(19):
        cx, cy, cz = (int(v) for v in VECTORS[i])
        value = field[i]
        if cz:
            value = jnp.where(z == (0 if cz > 0 else NZ - 1), 0.0, value)
        value = shifted(value, -cx, -cy, -cz)
        if cz:
            value = value + jnp.where(z == (NZ - 1 if cz > 0 else 0), field[OPPOSITE[i]], 0.0)
        out[i] = value


def speeds(s_ref, v_ref):
    def one(rows, lanes):
        s = [s_ref[i, rows, lanes] for i in range(19)]
        even, cross, odd_x, odd_y, odd_z = split_parity(s)
        rho = ((even[0] + even[1]) + (even[2] + even[3])) + ((even[4] + even[5]) + even[6])
        v_ref[rows, lanes] = ((odd_x[0] + odd_x[1]) + odd_x[2]) / rho

    chunks(one)


def push_back(a):
    odd = (a[7] - a[8]) + (a[9] - a[10]) + (a[11] - a[12]) + (a[13] - a[14])
    return (a[1] - a[2]) * (1.0 / 6.0) + odd * (1.0 / 12.0)


def turbine_sums(area_ref, field_ref, sums_ref, base):
    parts = [field_ref[OWN_ROWS, OWN_LANE + j : OWN_LANE + j + 128] for j in range(0, OWN_SPAN, 128)]
    for t in range(NTURB):
        total = None
        for j, part in enumerate(parts):
            lane = OWN_LANE + 128 * j
            term = area_ref[t, OWN_ROWS, lane : lane + 128] * part
            total = term if total is None else total + term
        sums_ref[base + t : base + t + 1, :] = jnp.sum(total, axis=0, keepdims=True)


def publish(sums_ref, out_ref):
    ones = jnp.ones((8, 128), jnp.bfloat16)
    row = None
    for part in split_three(sums_ref[...]):
        term = lax.dot_general(
            ones, part, (((1,), (1,)), ((), ())), preferred_element_type=jnp.float32
        )
        row = term if row is None else row + term
    for j in range(0, out_ref.shape[0], 8):
        out_ref[j : j + 8, :] = row


def totals(got_ref, base):
    row = jnp.sum(got_ref[...], axis=0, keepdims=True)
    index = lax.broadcasted_iota(jnp.int32, (NTURB, 128), 0) + base
    lane = lax.broadcasted_iota(jnp.int32, (NTURB, 128), 1)
    picked = jnp.where(index == lane, jnp.broadcast_to(row, (NTURB, 128)), 0.0)
    return jnp.broadcast_to(jnp.sum(picked, axis=1, keepdims=True), (NTURB, 128))


def weighted_area(area_ref, weight_ref, rows, lanes):
    total = None
    for t in range(NTURB):
        term = area_ref[t, rows, lanes] * weight_ref[t : t + 1, :]
        total = term if total is None else total + term
    return total


def split_three(value):
    high = value.astype(jnp.bfloat16)
    rest = value - high.astype(jnp.float32)
    middle = rest.astype(jnp.bfloat16)
    return high, middle, (rest - middle.astype(jnp.float32)).astype(jnp.bfloat16)


def area_kernel(x_ref, yz_ref, area_ref, out_ref):
    rows = lax.broadcasted_iota(jnp.int32, (RX, PTS), 0)
    columns = lax.broadcasted_iota(jnp.int32, (LANES, PTS), 0)

    def one(t, carry):
        point = pl.ds(t, 1)
        spots = jnp.where(rows == x_ref[point, :], area_ref[point, :], 0.0)
        left = jnp.concatenate(split_three(spots), axis=0)
        hot = jnp.where(columns == yz_ref[point, :], 1.0, 0.0).astype(jnp.bfloat16)
        product = lax.dot_general(
            left, hot, (((1,), (1,)), ((), ())), preferred_element_type=jnp.float32
        )
        out_ref[t] = product[:RX] + product[RX : 2 * RX] + product[2 * RX :]
        return carry

    lax.fori_loop(0, NTURB, one, 0)


def pack_x_kernel(field_hbm, cot_hbm, next_ref, prev_ref, field_ref, cot_ref, sems):
    first = pltpu.make_async_copy(field_hbm, field_ref, sems.at[0])
    second = pltpu.make_async_copy(cot_hbm, cot_ref, sems.at[1])
    first.start()
    second.start()
    first.wait()
    second.wait()
    half = OWN_SPAN // 2
    top = lax.broadcasted_iota(jnp.int32, (CX, half), 0) < CX // 2
    for i in range(19):
        low, high = cot_ref[i, :, :half], cot_ref[i, :, half:]
        next_ref[i, :, :OWN_SPAN] = field_ref[i]
        prev_ref[i, :, :OWN_SPAN] = field_ref[i]
        next_ref[i, :, OWN_SPAN:] = jnp.where(top, pltpu.roll(low, CX // 2, 0), high)
        prev_ref[i, :, OWN_SPAN:] = jnp.where(top, low, pltpu.roll(high, CX // 2, 0))


def pack_y_kernel(field_ref, cot_ref, before_ref, after_ref, fields_ref, cots_ref, next_ref, prev_ref):
    half = OWN_SPAN // 2
    top = lax.broadcasted_iota(jnp.int32, (CX, half), 0) < CX // 2
    left = lax.broadcasted_iota(jnp.int32, (CX, half), 1) < half // 2
    for i in range(19):
        for j, part in enumerate((before_ref[i, :, :OWN_SPAN], field_ref[i], after_ref[i, :, :OWN_SPAN])):
            rows = slice(CX * j, CX * (j + 1))
            fields_ref[i, rows] = part
            prev_ref[i, rows] = part[:, :half]
            next_ref[i, rows] = part[:, half:]
        before, after = before_ref[i, :, OWN_SPAN:], after_ref[i, :, OWN_SPAN:]
        low = (pltpu.roll(before, CX // 2, 0), cot_ref[i, :, :half], after)
        high = (before, cot_ref[i, :, half:], pltpu.roll(after, CX // 2, 0))
        for j in range(3):
            rows = slice(CX * j, CX * (j + 1))
            cots_ref[i, rows, :half] = low[j]
            cots_ref[i, rows, half:] = high[j]
        outer = jnp.where(top, low[2], low[0])
        prev_ref[i, RX:] = jnp.where(left, low[1], pltpu.roll(outer, half // 2, 1))
        outer = jnp.where(top, high[2], high[0])
        next_ref[i, RX:] = jnp.where(left, pltpu.roll(high[1], half // 2, 1), outer)


class Joined:
    def __init__(self, before, here, after):
        self.parts = before, here, after

    def __getitem__(self, index):
        before, here, after = self.parts
        return jnp.concatenate([before[index, :RX], here[index], after[index, :RX]], axis=1)


def first_kernel(before_ref, fields_ref, after_ref, cots_ref, area_ref, s_ref, v_ref, cot_ref, out_ref, sums):
    stream(Joined(before_ref, fields_ref, after_ref), s_ref)
    speeds(s_ref, v_ref)
    sums[...] = jnp.zeros_like(sums)
    turbine_sums(area_ref, v_ref, sums, 0)
    publish(sums, out_ref)
    half = OWN_SPAN // 2
    for i in range(19):
        before, after = before_ref[i, RX:], after_ref[i, RX:]
        turned = pltpu.roll(before, half // 2, 1), pltpu.roll(after, half // 2, 1)
        for j in range(3):
            rows = slice(CX * j, CX * (j + 1))
            cot_ref[i, rows, :OWN_LANE] = turned[0] if j == 1 else before
            cot_ref[i, rows, OWN_LANE + OWN_SPAN :] = after if j == 1 else turned[1]
        cot_ref[i, :, OWN_LANE : OWN_LANE + OWN_SPAN] = cots_ref[i]


def forward_kernel(last, s_ref, v_ref, area_ref, inv_ref, got_ref, *rest):
    if last:
        cot_ref, next_ref, vn_ref, rotor_ref, out_ref, field, sums, drag = rest
    else:
        next_ref, vn_ref, rotor_ref, out_ref, field, sums = rest
    rotor_ref[...] = totals(got_ref, 0) * inv_ref[...]

    def one(rows, lanes):
        s = [s_ref[i, rows, lanes] for i in range(19)]
        force = weighted_area(area_ref, rotor_ref, rows, lanes) * v_ref[rows, lanes] * -THRUST
        for i, value in enumerate(collide(s, force)):
            field[i, rows, lanes] = value

    chunks(one)
    stream(field, next_ref)
    speeds(next_ref, vn_ref)
    sums[...] = jnp.zeros_like(sums)
    turbine_sums(area_ref, vn_ref, sums, 0)
    if last:

        def other(rows, lanes):
            a = [cot_ref[i, rows, lanes] for i in range(19)]
            drag[rows, lanes] = push_back(a) * vn_ref[rows, lanes] * -THRUST

        chunks(other)
        turbine_sums(area_ref, drag, sums, NTURB)
    publish(sums, out_ref)


def adjoint_field(s_ref, a_ref, area_ref, rotor_ref, bar_ref, field):
    def one(rows, lanes):
        s = [s_ref[i, rows, lanes] for i in range(19)]
        a = [a_ref[i, rows, lanes] for i in range(19)]
        speed_bar = weighted_area(area_ref, rotor_ref, rows, lanes) * push_back(a) * -THRUST
        speed_bar = speed_bar + weighted_area(area_ref, bar_ref, rows, lanes)
        for i, value in enumerate(collide_adjoint(s, a, speed_bar)):
            field[i, rows, lanes] = value

    chunks(one)


def backward_kernel(first, sends, s_ref, a_ref, area_ref, inv_ref, got_ref, v_ref, *rest):
    rest = list(rest)
    rotor_ref = None if first else rest.pop(0)
    out_ref, drag_ref, bar_ref = rest[:3]
    field, sums = rest[-2:]
    if first:
        rotor_ref = rest[-3]
        rotor_ref[...] = totals(got_ref, 0) * inv_ref[...]
    bar_ref[...] = totals(got_ref, NTURB if first else 0) * inv_ref[...]
    adjoint_field(s_ref, a_ref, area_ref, rotor_ref, bar_ref, field)
    stream_adjoint(field, out_ref)

    def other(rows, lanes):
        a = [out_ref[i, rows, lanes] for i in range(19)]
        drag_ref[rows, lanes] = push_back(a) * v_ref[rows, lanes] * -THRUST

    chunks(other)
    if sends:
        sums[...] = jnp.zeros_like(sums)
        turbine_sums(area_ref, drag_ref, sums, 0)
        publish(sums, rest[3])


def last_kernel(s_ref, a_ref, area_ref, rotor_ref, point_ref, size_ref, inv_ref, out_ref, grad_ref, field, result, bar):
    known, swing, slope = (
        point_ref[NTURB * j : NTURB * (j + 1), :PTS] for j in range(3)
    )
    total = jnp.sum(size_ref[...] * swing, axis=1, keepdims=True)
    grad_ref[...] = known + total * slope
    bar[...] = jnp.broadcast_to(total, (NTURB, 128)) * inv_ref[...]
    adjoint_field(s_ref, a_ref, area_ref, rotor_ref, bar, field)
    stream_adjoint(field, result)
    for i in range(19):
        out_ref[i] = result[i, OWN_ROWS, OWN_LANE : OWN_LANE + OWN_SPAN]


def gather_kernel(x_ref, yz_ref, cot_ref, q1, q2, q3, v1, v2, v3, v4, u1, u2, u3, u4, n2, n3, n4, inv, out_ref):
    own = (OWN_ROWS, slice(OWN_LANE, OWN_LANE + OWN_SPAN))
    v = [ref[own] for ref in (v1, v2, v3, v4)]
    q = [ref[own] for ref in (q1, q2, q3)]
    a = [cot_ref[(i,) + own] for i in range(19)]
    q.append(push_back(a) * v[3] * -THRUST)
    rows = lax.broadcasted_iota(jnp.int32, (CX, PTS), 0) + MARGIN
    columns = lax.broadcasted_iota(jnp.int32, (OWN_SPAN, PTS), 0) + OWN_LANE

    def wide(ref, t):
        return jnp.concatenate([ref[pl.ds(t, 1), :]] * (OWN_SPAN // 128), axis=1)

    out_ref[...] = jnp.zeros_like(out_ref)

    def one(t, carry):
        u = [wide(ref, t) for ref in (u1, u2, u3, u4)]
        n = [None] + [wide(ref, t) for ref in (n2, n3, n4)]
        known = u[0] * q[0]
        for k in range(1, 4):
            known = known + u[k] * q[k] + n[k] * (v[k] - u[k])
        fields = [known, q[0], (v[0] - u[0]) * wide(inv, t)]
        left = jnp.concatenate(split_three(jnp.concatenate(fields, axis=0)), axis=0)
        hot = jnp.where(columns == yz_ref[pl.ds(t, 1), :], 1.0, 0.0).astype(jnp.bfloat16)
        product = jnp.dot(left, hot, preferred_element_type=jnp.float32)
        size = 3 * CX
        product = product[:size] + product[size : 2 * size] + product[2 * size :]
        mine = rows == x_ref[pl.ds(t, 1), :]
        for j in range(3):
            picked = jnp.where(mine, product[CX * j : CX * (j + 1)], 0.0)
            out_ref[pl.ds(j * NTURB + t, 1), 0:PTS] = jnp.sum(picked, axis=0, keepdims=True)
        return carry

    lax.fori_loop(0, NTURB, one, 0, unroll=4)


def call(kernel, outs, scratch, *args):
    vmem = pl.BlockSpec(memory_space=pltpu.VMEM)
    return pl.pallas_call(
        kernel,
        out_shape=[jax.ShapeDtypeStruct(shape, jnp.float32) for shape in outs],
        in_specs=[vmem] * len(args),
        out_specs=[vmem] * len(outs),
        scratch_shapes=[pltpu.VMEM(shape, jnp.float32) for shape in scratch],
        compiler_params=pltpu.CompilerParams(vmem_limit_bytes=VMEM_LIMIT),
    )(*args)


def route(value, target):
    size_x, size_y = lax.axis_size("gx"), lax.axis_size("gy")
    pairs = []
    for i in range(size_x):
        for j in range(size_y):
            to = target(i, j)
            if to is not None:
                pairs.append((i * size_y + j, to[0] % size_x * size_y + to[1] % size_y))
    return lax.ppermute(value, ("gx", "gy"), pairs)


def swap(value):
    return route(value, lambda i, j: (i ^ 1, j))


def exchange(rows):
    return lax.all_to_all(rows, ("gx", "gy"), 0, 0, tiled=True)


def merge_kernel(*refs):
    value = refs[0][...]
    for ref in refs[1:-1]:
        value = jnp.where(value != 0.0, value, ref[...])
    refs[-1][...] = value


def merge(value, parts):
    (value,) = call(merge_kernel, [value.shape], [], value, *parts)
    return value


def spread(value):
    size_x, size_y = lax.axis_size("gx"), lax.axis_size("gy")
    half = size_y // 2

    def across(first, second):
        def target(i, j):
            dy, dz = second if i % 2 else first
            return i, (j // half + dz) % 2 * half + (j % half + dy) % half

        return target

    def along(block, step, first, second):
        def target(i, j):
            move = second if i % 2 else first
            if move is None:
                return None
            return i // block * block + (i % block + move * step) % block, j

        return target

    value = merge(value, [swap(value)])
    turns = [((1, 0), (1, 1)), ((3, 0), (3, 1)), ((2, 0), (2, 1)), ((0, 1), (0, 1))]
    value = merge(value, [route(value, across(*turn)) for turn in turns])
    value = merge(value, [swap(value)])
    for block, step in ((8, 2), (size_x, 8)):
        turns = [(1, 2), (3, None)]
        value = merge(value, [route(value, along(block, step, *turn)) for turn in turns])
        value = merge(value, [swap(value)])
    return value


def shift(value, axis, step):
    size = lax.axis_size(axis)
    return lax.ppermute(value, axis, [(i, (i + step) % size) for i in range(size)])


def region(checkpoint, cotangent, ready):
    wide = (19, CX, OWN_SPAN + OWN_SPAN // 2)
    right, left = pl.pallas_call(
        pack_x_kernel,
        out_shape=[jax.ShapeDtypeStruct(wide, jnp.float32)] * 2,
        in_specs=[pl.BlockSpec(memory_space=pltpu.HBM)] * 2,
        out_specs=[pl.BlockSpec(memory_space=pltpu.VMEM)] * 2,
        scratch_shapes=[pltpu.VMEM(checkpoint.shape, jnp.float32)] * 2 + [pltpu.SemaphoreType.DMA((2,))],
        compiler_params=pltpu.CompilerParams(vmem_limit_bytes=VMEM_LIMIT),
    )(checkpoint, cotangent)
    before, after = shift(right, "gx", 1), shift(left, "gx", -1)
    before, after, *ready = lax.optimization_barrier((before, after) + ready)
    stack, edge = (19, RX, OWN_SPAN), (19, RX + CX, OWN_SPAN // 2)
    fields, cots, right, left = call(
        pack_y_kernel, [stack, stack, edge, edge], [], checkpoint, cotangent, before, after
    )
    return (shift(right, "gy", 1), fields, shift(left, "gy", -1), cots), ready


def body(checkpoint, cotangent, blade_area, hub_tile, point_side, point_local):
    count_x, count_y = lax.axis_size("gx"), lax.axis_size("gy")
    index_x, index_y = lax.axis_index("gx"), lax.axis_index("gy")
    area = blade_area.reshape(NTURB, PTS)
    side = point_side.reshape(NTURB, PTS)
    local = point_local.reshape(NTURB, PTS)
    hub = hub_tile.reshape(NTURB, 1)
    cell_x = (hub // count_y + side // 3 - 1 - index_x) * CX + local // (CY * NZ) + MARGIN
    cell_y = (hub % count_y + side % 3 - 1 - index_y) * CY + local // NZ % CY + MARGIN
    cell_x = cell_x % (count_x * CX)
    cell_y = cell_y % (count_y * CY)
    inside = (cell_x < RX) & (cell_y < RY)
    cell_x = jnp.where(inside, cell_x, -1)
    cell_yz = jnp.where(inside, cell_y * NZ + local % NZ, -1)
    mine_y = (cell_y >= MARGIN) & (cell_y < MARGIN + CY)
    inverse = jnp.broadcast_to(1.0 / jnp.sum(area, 1, keepdims=True), (NTURB, 128))

    full = (19, RX, LANES)
    flat = (RX, LANES)
    row = (NTURB, 128)
    (spots,) = call(area_kernel, [(NTURB,) + flat], [], cell_x, cell_yz, area)
    own_yz = jnp.where(mine_y, cell_yz, -1)
    parts, ready = region(checkpoint, cotangent, (spots, cell_x, own_yz, area, inverse))
    spots, cell_x, own_yz, area, inverse = ready

    s, v, rotor = [None] * 5, [None] * 5, [None] * 5
    table = (128, 128)
    every = (count_x * count_y, 128)
    s[1], v[1], cot, sums = call(first_kernel, [full, flat, full, every], [table], *parts, spots)
    for k in (1, 2, 3):
        last = k == 3
        s[k + 1], v[k + 1], rotor[k], sums = call(
            functools.partial(forward_kernel, last),
            [full, flat, row, every],
            [full, table] + ([flat] if last else []),
            *([s[k], v[k], spots, inverse, exchange(sums)] + ([cot] if last else [])),
        )
    adjoint = cot
    bar, drag = [None] * 5, [None] * 5
    for k in (4, 3, 2):
        first, sends = k == 4, k > 2
        args = [s[k], adjoint, spots, inverse, exchange(sums), v[k - 1]]
        outs = call(
            functools.partial(backward_kernel, first, sends),
            [full, flat, row] + ([every] if sends else []) + ([row] if first else []),
            [full, table],
            *(args + ([] if first else [rotor[k]])),
        )
        adjoint, drag[k - 1], bar[k] = outs[:3]
        sums = outs[3] if sends else None
        if first:
            rotor[4] = outs[4]
    (points,) = call(
        gather_kernel,
        [(3 * NTURB, 128)],
        [],
        *([cell_x, own_yz, cot] + drag[1:4] + v[1:] + rotor[1:] + bar[2:] + [inverse]),
    )
    grad, grad_area = call(
        last_kernel,
        [(19, CX, CY * NZ), (NTURB, PTS)],
        [full, full, row],
        *(s[1], adjoint, spots, rotor[1], spread(points), area, inverse),
    )
    return grad, grad_area.reshape(-1)


def solution(mesh):
    return jax.shard_map(
        body,
        mesh=mesh,
        in_specs=(P(None, "gx", "gy"), P(None, "gx", "gy"), P(), P(), P(), P()),
        out_specs=(P(None, "gx", "gy"), P()),
        check_vma=False,
    )
```

```python
import functools

import jax
import jax.numpy as jnp
import numpy as np
from jax import lax
from jax.experimental import pallas as pl
from jax.experimental.pallas import tpu as pltpu
from jax.sharding import PartitionSpec as P

NZ = 16
CX = 8
CY = 16
STEPS = 4
NTURB = 16
PTS = 96
MARGIN = 8
RX = CX + 2 * MARGIN
RY = CY + 2 * MARGIN
LANES = RY * NZ
OWN_ROWS = slice(MARGIN, MARGIN + CX)
OWN_LANE = MARGIN * NZ
OWN_SPAN = CY * NZ

VMEM_LIMIT = 8 * 1024 * 1024

TAU_ZERO = 0.52
SMAGORINSKY = 0.17 * 0.17
TINY = 1e-10
THRUST = 4.0
GHOST_RATES = np.array([1.05, 1.15, 1.25, 1.35, 1.45, 1.55, 1.65, 1.75, 1.85])
W_REST, W_AXIS, W_EDGE = 1.0 / 3.0, 1.0 / 18.0, 1.0 / 36.0

VECTORS = np.array(
    [(0, 0, 0), (1, 0, 0), (-1, 0, 0), (0, 1, 0), (0, -1, 0), (0, 0, 1), (0, 0, -1)]
    + [(1, 1, 0), (-1, -1, 0), (1, -1, 0), (-1, 1, 0), (1, 0, 1), (-1, 0, -1)]
    + [(1, 0, -1), (-1, 0, 1), (0, 1, 1), (0, -1, -1), (0, 1, -1), (0, -1, 1)]
)
OPPOSITE = [0] + [i + 1 if i % 2 else i - 1 for i in range(1, 19)]


def basis():
    c = VECTORS * 1.0
    weights = np.array([W_REST] + [W_AXIS] * 6 + [W_EDGE] * 12)
    x, y, z = c[:, 0], c[:, 1], c[:, 2]
    monomials = [np.ones(19), x, y, z, x * x, y * y, z * z, x * y, x * z, y * z]
    monomials += [x * y * y, x * z * z, y * x * x, y * z * z, z * x * x, z * y * y]
    monomials += [x * x * y * y, x * x * z * z, y * y * z * z]
    rows = []
    for entry in monomials:
        vector = entry * 1.0
        for sweep in range(2):
            for other in rows:
                vector = vector - np.sum(weights * vector * other) * other
        rows.append(vector / np.sqrt(np.sum(weights * vector * vector)))
    return np.stack(rows, 0)


def ghost_tables():
    rows = basis()
    odd = []
    for first, members in ((10, (1, 7, 11)), (12, (3, 7, 15)), (14, (5, 11, 15))):
        h = rows[first : first + 2][:, list(members)]
        rates = GHOST_RATES[first - 10 : first - 8]
        odd.append(np.diag([W_AXIS, W_EDGE, W_EDGE]) @ h.T @ np.diag(rates) @ h)
    even = rows[16:19][:, [0, 1, 3, 5, 7, 11, 15]]
    return odd, even, GHOST_RATES[6:9]


ODD, EVEN, EVEN_RATES = ghost_tables()
CLASS_W = [W_REST] + [W_AXIS] * 3 + [W_EDGE] * 3


def combine(coefs, values):
    total = None
    for coef, value in zip(coefs, values):
        coef = float(coef)
        if abs(coef) < 1e-12:
            continue
        term = value if coef == 1.0 else value * coef
        total = term if total is None else total + term
    return total


def split_parity(s):
    e = [s[i] + s[i + 1] for i in range(1, 19, 2)]
    o = [s[i] - s[i + 1] for i in range(1, 19, 2)]
    even = [s[0], e[0], e[1], e[2], e[3] + e[4], e[5] + e[6], e[7] + e[8]]
    cross = [e[3] - e[4], e[5] - e[6], e[7] - e[8]]
    odd_x = [o[0], o[3] + o[4], o[5] + o[6]]
    odd_y = [o[1], o[3] - o[4], o[7] + o[8]]
    odd_z = [o[2], o[5] - o[6], o[7] - o[8]]
    return even, cross, odd_x, odd_y, odd_z


def merge_parity(s, even, cross, odd_x, odd_y, odd_z):
    out = [s[0] + even[0]]
    for axis, odd in enumerate((odd_x, odd_y, odd_z)):
        out += [s[1 + 2 * axis] + (even[1 + axis] + odd[0])]
        out += [s[2 + 2 * axis] + (even[1 + axis] - odd[0])]
    pairs = ((odd_x[1], odd_y[1]), (odd_x[2], odd_z[1]), (odd_y[2], odd_z[2]))
    for family in range(3):
        first, second = pairs[family]
        base = 7 + 4 * family
        for sign, offset in ((1, 0), (-1, 2)):
            level = even[4 + family] + cross[family] if sign > 0 else even[4 + family] - cross[family]
            swing = first + second if sign > 0 else first - second
            out += [s[base + offset] + (level + swing), s[base + offset + 1] + (level - swing)]
    return out


def ghost_even(even, transpose):
    if transpose:
        even = [value * w for value, w in zip(even, CLASS_W)]
    m = [combine(EVEN[k], even) * float(EVEN_RATES[k]) for k in range(3)]
    out = [combine(EVEN[:, j], m) for j in range(7)]
    if not transpose:
        out = [value * w for value, w in zip(out, CLASS_W)]
    return out


def ghost_odd(index, odd, transpose):
    matrix = ODD[index].T if transpose else ODD[index]
    return [combine(matrix[j], odd) for j in range(3)]


def local_state(even, cross, odds):
    rho = ((even[0] + even[1]) + (even[2] + even[3])) + ((even[4] + even[5]) + even[6])
    inverse = 1.0 / rho
    mom = [(odd[0] + odd[1]) + odd[2] for odd in odds]
    u = [m * inverse for m in mom]
    third = rho * (1.0 / 3.0)
    edges = ((even[4], even[5]), (even[4], even[6]), (even[5], even[6]))
    stress = [
        ((even[1 + a] + edges[a][0]) + edges[a][1]) - third - mom[a] * u[a] for a in range(3)
    ]
    stress += [cross[0] - mom[0] * u[1], cross[1] - mom[0] * u[2], cross[2] - mom[1] * u[2]]
    square = stress[0] * stress[0] + stress[1] * stress[1] + stress[2] * stress[2]
    square = square + 2.0 * (
        stress[3] * stress[3] + stress[4] * stress[4] + stress[5] * stress[5]
    )
    norm = jnp.sqrt(square + TINY)
    root = jnp.sqrt(TAU_ZERO * TAU_ZERO + (18.0 * SMAGORINSKY) * norm * inverse)
    tau = 0.5 * (TAU_ZERO + root)
    return inverse, u, stress, norm, root, tau


def collide(s, force):
    even, cross, odd_x, odd_y, odd_z = split_parity(s)
    inverse, u, stress, norm, root, tau = local_state(even, cross, (odd_x, odd_y, odd_z))
    scale = 4.5 / tau
    k = [value * scale for value in stress]
    trace = (k[0] + k[1] + k[2]) * (1.0 / 3.0)
    relax = [-trace, k[0] - trace, k[1] - trace, k[2] - trace]
    relax += [k[0] + relax[2], k[0] + relax[3], k[1] + relax[3]]
    ghost = ghost_even(even, False)
    even_out = [-(relax[j] * CLASS_W[j] + ghost[j]) for j in range(7)]
    cross_out = [k[3 + j] * (-2.0 * W_EDGE) for j in range(3)]
    gx = ghost_odd(0, odd_x, False)
    ox = [force * (1.0 / 6.0) - gx[0], force * (1.0 / 12.0) - gx[1], force * (1.0 / 12.0) - gx[2]]
    oy = [-value for value in ghost_odd(1, odd_y, False)]
    oz = [-value for value in ghost_odd(2, odd_z, False)]
    return merge_parity(s, even_out, cross_out, ox, oy, oz)


def collide_adjoint(s, a, speed_bar):
    even, cross, odd_x, odd_y, odd_z = split_parity(s)
    inverse, u, stress, norm, root, tau = local_state(even, cross, (odd_x, odd_y, odd_z))
    ev, cr, ax, ay, az = split_parity(a)
    weighted = [value * w for value, w in zip(ev, CLASS_W)]
    total = ((weighted[0] + weighted[1]) + (weighted[2] + weighted[3])) + (
        (weighted[4] + weighted[5]) + weighted[6]
    )
    third = total * (1.0 / 3.0)
    edges = ((4, 5), (4, 6), (5, 6))
    beta = [
        (weighted[1 + i] + weighted[edges[i][0]] + weighted[edges[i][1]] - third) * -4.5
        for i in range(3)
    ]
    beta += [value * (-9.0 * W_EDGE) for value in cr]
    inv_tau = 1.0 / tau
    dot = (beta[0] * stress[0] + beta[1] * stress[1] + beta[2] * stress[2]) + (
        beta[3] * stress[3] + beta[4] * stress[4] + beta[5] * stress[5]
    )
    tau_bar = -dot * inv_tau * inv_tau
    common = tau_bar * (4.5 * SMAGORINSKY) * inverse / root
    factor = common / norm
    p_bar = [beta[i] * inv_tau + stress[i] * factor for i in range(3)]
    twice = factor + factor
    p_bar += [beta[i] * inv_tau + stress[i] * twice for i in range(3, 6)]
    sp = speed_bar * inverse
    px, py, pz, pxy, pxz, pyz = p_bar
    tx = pxy * u[1] + pxz * u[2]
    ty = pyz * u[2]
    mx = sp - (2.0 * px * u[0] + tx)
    my = -(2.0 * py * u[1] + pxy * u[0] + ty)
    mz = -(2.0 * pz * u[2] + pxz * u[0] + pyz * u[1])
    rho_bar = -common * norm * inverse - (px + py + pz) * (1.0 / 3.0)
    rho_bar = rho_bar + (px * u[0] + tx) * u[0] + (py * u[1] + ty) * u[1] + pz * u[2] * u[2]
    rho_bar = rho_bar - sp * u[0]
    ghost = ghost_even(ev, True)
    level = [rho_bar, rho_bar + px, rho_bar + py, rho_bar + pz]
    level += [level[1] + py, level[1] + pz, level[2] + pz]
    even_out = [level[j] - ghost[j] for j in range(7)]
    gx, gy, gz = (ghost_odd(i, odd, True) for i, odd in enumerate((ax, ay, az)))
    ox = [mx - value for value in gx]
    oy = [my - value for value in gy]
    oz = [mz - value for value in gz]
    return merge_parity(a, even_out, p_bar[3:], ox, oy, oz)


def chunks(body):
    def step(index, carry):
        lane = pl.multiple_of(index * 128, 128)
        for row in range(0, RX, 8):
            body(pl.ds(row, 8), pl.ds(lane, 128))
        return carry

    lax.fori_loop(0, LANES // 128, step, 0, unroll=True)


def shifted(value, cx, cy, cz):
    lane = (NZ * cy + cz) % LANES
    if lane:
        value = pltpu.roll(value, lane, 1)
    if cx % RX:
        value = pltpu.roll(value, cx % RX, 0)
    return value


def height():
    return lax.broadcasted_iota(jnp.int32, (RX, LANES), 1) & (NZ - 1)


def stream(field, out):
    z = height()
    for i in range(19):
        cx, cy, cz = (int(v) for v in VECTORS[i])
        value = shifted(field[i], cx, cy, cz)
        if cz:
            value = jnp.where(z == (0 if cz > 0 else NZ - 1), field[OPPOSITE[i]], value)
        out[i] = value


def stream_adjoint(field, out):
    z = height()
    for i in range(19):
        cx, cy, cz = (int(v) for v in VECTORS[i])
        value = field[i]
        if cz:
            value = jnp.where(z == (0 if cz > 0 else NZ - 1), 0.0, value)
        value = shifted(value, -cx, -cy, -cz)
        if cz:
            value = value + jnp.where(z == (NZ - 1 if cz > 0 else 0), field[OPPOSITE[i]], 0.0)
        out[i] = value


def speeds(s_ref, v_ref):
    def one(rows, lanes):
        s = [s_ref[i, rows, lanes] for i in range(19)]
        even, cross, odd_x, odd_y, odd_z = split_parity(s)
        rho = ((even[0] + even[1]) + (even[2] + even[3])) + ((even[4] + even[5]) + even[6])
        v_ref[rows, lanes] = ((odd_x[0] + odd_x[1]) + odd_x[2]) / rho

    chunks(one)


def push_back(a):
    odd = (a[7] - a[8]) + (a[9] - a[10]) + (a[11] - a[12]) + (a[13] - a[14])
    return (a[1] - a[2]) * (1.0 / 6.0) + odd * (1.0 / 12.0)


def turbine_sums(area_ref, field_ref, sums_ref, base):
    parts = [field_ref[OWN_ROWS, OWN_LANE + j : OWN_LANE + j + 128] for j in range(0, OWN_SPAN, 128)]
    for t in range(NTURB):
        total = None
        for j, part in enumerate(parts):
            lane = OWN_LANE + 128 * j
            term = area_ref[t, OWN_ROWS, lane : lane + 128] * part
            total = term if total is None else total + term
        sums_ref[base + t : base + t + 1, :] = jnp.sum(total, axis=0, keepdims=True)


def publish(sums_ref, out_ref):
    ones = jnp.ones((8, 128), jnp.bfloat16)
    row = None
    for part in split_three(sums_ref[...]):
        term = lax.dot_general(
            ones, part, (((1,), (1,)), ((), ())), preferred_element_type=jnp.float32
        )
        row = term if row is None else row + term
    for j in range(0, out_ref.shape[0], 8):
        out_ref[j : j + 8, :] = row


def totals(got_ref, base):
    row = jnp.sum(got_ref[...], axis=0, keepdims=True)
    index = lax.broadcasted_iota(jnp.int32, (NTURB, 128), 0) + base
    lane = lax.broadcasted_iota(jnp.int32, (NTURB, 128), 1)
    picked = jnp.where(index == lane, jnp.broadcast_to(row, (NTURB, 128)), 0.0)
    return jnp.broadcast_to(jnp.sum(picked, axis=1, keepdims=True), (NTURB, 128))


def weighted_area(area_ref, weight_ref, rows, lanes):
    total = None
    for t in range(NTURB):
        term = area_ref[t, rows, lanes] * weight_ref[t : t + 1, :]
        total = term if total is None else total + term
    return total


def split_three(value):
    high = value.astype(jnp.bfloat16)
    rest = value - high.astype(jnp.float32)
    middle = rest.astype(jnp.bfloat16)
    return high, middle, (rest - middle.astype(jnp.float32)).astype(jnp.bfloat16)


def area_kernel(x_ref, yz_ref, area_ref, out_ref):
    rows = lax.broadcasted_iota(jnp.int32, (RX, PTS), 0)
    columns = lax.broadcasted_iota(jnp.int32, (LANES, PTS), 0)

    def one(t, carry):
        point = pl.ds(t, 1)
        spots = jnp.where(rows == x_ref[point, :], area_ref[point, :], 0.0)
        left = jnp.concatenate(split_three(spots), axis=0)
        hot = jnp.where(columns == yz_ref[point, :], 1.0, 0.0).astype(jnp.bfloat16)
        product = lax.dot_general(
            left, hot, (((1,), (1,)), ((), ())), preferred_element_type=jnp.float32
        )
        out_ref[t] = product[:RX] + product[RX : 2 * RX] + product[2 * RX :]
        return carry

    lax.fori_loop(0, NTURB, one, 0)


def pack_x_kernel(field_hbm, cot_hbm, next_ref, prev_ref, field_ref, cot_ref, sems):
    first = pltpu.make_async_copy(field_hbm, field_ref, sems.at[0])
    second = pltpu.make_async_copy(cot_hbm, cot_ref, sems.at[1])
    first.start()
    second.start()
    first.wait()
    second.wait()
    half = OWN_SPAN // 2
    top = lax.broadcasted_iota(jnp.int32, (CX, half), 0) < CX // 2
    for i in range(19):
        low, high = cot_ref[i, :, :half], cot_ref[i, :, half:]
        next_ref[i, :, :OWN_SPAN] = field_ref[i]
        prev_ref[i, :, :OWN_SPAN] = field_ref[i]
        next_ref[i, :, OWN_SPAN:] = jnp.where(top, pltpu.roll(low, CX // 2, 0), high)
        prev_ref[i, :, OWN_SPAN:] = jnp.where(top, low, pltpu.roll(high, CX // 2, 0))


def pack_y_kernel(field_ref, cot_ref, before_ref, after_ref, fields_ref, cots_ref, next_ref, prev_ref):
    half = OWN_SPAN // 2
    top = lax.broadcasted_iota(jnp.int32, (CX, half), 0) < CX // 2
    left = lax.broadcasted_iota(jnp.int32, (CX, half), 1) < half // 2
    for i in range(19):
        for j, part in enumerate((before_ref[i, :, :OWN_SPAN], field_ref[i], after_ref[i, :, :OWN_SPAN])):
            rows = slice(CX * j, CX * (j + 1))
            fields_ref[i, rows] = part
            prev_ref[i, rows] = part[:, :half]
            next_ref[i, rows] = part[:, half:]
        before, after = before_ref[i, :, OWN_SPAN:], after_ref[i, :, OWN_SPAN:]
        low = (pltpu.roll(before, CX // 2, 0), cot_ref[i, :, :half], after)
        high = (before, cot_ref[i, :, half:], pltpu.roll(after, CX // 2, 0))
        for j in range(3):
            rows = slice(CX * j, CX * (j + 1))
            cots_ref[i, rows, :half] = low[j]
            cots_ref[i, rows, half:] = high[j]
        outer = jnp.where(top, low[2], low[0])
        prev_ref[i, RX:] = jnp.where(left, low[1], pltpu.roll(outer, half // 2, 1))
        outer = jnp.where(top, high[2], high[0])
        next_ref[i, RX:] = jnp.where(left, pltpu.roll(high[1], half // 2, 1), outer)


class Joined:
    def __init__(self, before, here, after):
        self.parts = before, here, after

    def __getitem__(self, index):
        before, here, after = self.parts
        return jnp.concatenate([before[index, :RX], here[index], after[index, :RX]], axis=1)


def first_kernel(before_ref, fields_ref, after_ref, cots_ref, area_ref, s_ref, v_ref, cot_ref, out_ref, sums):
    stream(Joined(before_ref, fields_ref, after_ref), s_ref)
    speeds(s_ref, v_ref)
    sums[...] = jnp.zeros_like(sums)
    turbine_sums(area_ref, v_ref, sums, 0)
    publish(sums, out_ref)
    half = OWN_SPAN // 2
    for i in range(19):
        before, after = before_ref[i, RX:], after_ref[i, RX:]
        turned = pltpu.roll(before, half // 2, 1), pltpu.roll(after, half // 2, 1)
        for j in range(3):
            rows = slice(CX * j, CX * (j + 1))
            cot_ref[i, rows, :OWN_LANE] = turned[0] if j == 1 else before
            cot_ref[i, rows, OWN_LANE + OWN_SPAN :] = after if j == 1 else turned[1]
        cot_ref[i, :, OWN_LANE : OWN_LANE + OWN_SPAN] = cots_ref[i]


def forward_kernel(last, s_ref, v_ref, area_ref, inv_ref, got_ref, *rest):
    if last:
        cot_ref, next_ref, vn_ref, rotor_ref, out_ref, field, sums, drag = rest
    else:
        next_ref, vn_ref, rotor_ref, out_ref, field, sums = rest
    rotor_ref[...] = totals(got_ref, 0) * inv_ref[...]

    def one(rows, lanes):
        s = [s_ref[i, rows, lanes] for i in range(19)]
        force = weighted_area(area_ref, rotor_ref, rows, lanes) * v_ref[rows, lanes] * -THRUST
        for i, value in enumerate(collide(s, force)):
            field[i, rows, lanes] = value

    chunks(one)
    stream(field, next_ref)
    speeds(next_ref, vn_ref)
    sums[...] = jnp.zeros_like(sums)
    turbine_sums(area_ref, vn_ref, sums, 0)
    if last:

        def other(rows, lanes):
            a = [cot_ref[i, rows, lanes] for i in range(19)]
            drag[rows, lanes] = push_back(a) * vn_ref[rows, lanes] * -THRUST

        chunks(other)
        turbine_sums(area_ref, drag, sums, NTURB)
    publish(sums, out_ref)


def adjoint_field(s_ref, a_ref, area_ref, rotor_ref, bar_ref, field):
    def one(rows, lanes):
        s = [s_ref[i, rows, lanes] for i in range(19)]
        a = [a_ref[i, rows, lanes] for i in range(19)]
        speed_bar = weighted_area(area_ref, rotor_ref, rows, lanes) * push_back(a) * -THRUST
        speed_bar = speed_bar + weighted_area(area_ref, bar_ref, rows, lanes)
        for i, value in enumerate(collide_adjoint(s, a, speed_bar)):
            field[i, rows, lanes] = value

    chunks(one)


def backward_kernel(first, sends, s_ref, a_ref, area_ref, inv_ref, got_ref, v_ref, *rest):
    rest = list(rest)
    rotor_ref = None if first else rest.pop(0)
    out_ref, drag_ref, bar_ref = rest[:3]
    field, sums = rest[-2:]
    if first:
        rotor_ref = rest[-3]
        rotor_ref[...] = totals(got_ref, 0) * inv_ref[...]
    bar_ref[...] = totals(got_ref, NTURB if first else 0) * inv_ref[...]
    adjoint_field(s_ref, a_ref, area_ref, rotor_ref, bar_ref, field)
    stream_adjoint(field, out_ref)

    def other(rows, lanes):
        a = [out_ref[i, rows, lanes] for i in range(19)]
        drag_ref[rows, lanes] = push_back(a) * v_ref[rows, lanes] * -THRUST

    chunks(other)
    if sends:
        sums[...] = jnp.zeros_like(sums)
        turbine_sums(area_ref, drag_ref, sums, 0)
        publish(sums, rest[3])


def last_kernel(s_ref, a_ref, area_ref, rotor_ref, point_ref, size_ref, inv_ref, out_ref, grad_ref, field, result, bar):
    known, swing, slope = (
        point_ref[NTURB * j : NTURB * (j + 1), :PTS] for j in range(3)
    )
    total = jnp.sum(size_ref[...] * swing, axis=1, keepdims=True)
    grad_ref[...] = known + total * slope
    bar[...] = jnp.broadcast_to(total, (NTURB, 128)) * inv_ref[...]
    adjoint_field(s_ref, a_ref, area_ref, rotor_ref, bar, field)
    stream_adjoint(field, result)
    for i in range(19):
        out_ref[i] = result[i, OWN_ROWS, OWN_LANE : OWN_LANE + OWN_SPAN]


def gather_kernel(x_ref, yz_ref, cot_ref, q1, q2, q3, v1, v2, v3, v4, u1, u2, u3, u4, n2, n3, n4, inv, out_ref):
    own = (OWN_ROWS, slice(OWN_LANE, OWN_LANE + OWN_SPAN))
    v = [ref[own] for ref in (v1, v2, v3, v4)]
    q = [ref[own] for ref in (q1, q2, q3)]
    a = [cot_ref[(i,) + own] for i in range(19)]
    q.append(push_back(a) * v[3] * -THRUST)
    rows = lax.broadcasted_iota(jnp.int32, (CX, PTS), 0) + MARGIN
    columns = lax.broadcasted_iota(jnp.int32, (OWN_SPAN, PTS), 0) + OWN_LANE

    def wide(ref, t):
        return jnp.concatenate([ref[pl.ds(t, 1), :]] * (OWN_SPAN // 128), axis=1)

    out_ref[...] = jnp.zeros_like(out_ref)

    def one(t, carry):
        u = [wide(ref, t) for ref in (u1, u2, u3, u4)]
        n = [None] + [wide(ref, t) for ref in (n2, n3, n4)]
        known = u[0] * q[0]
        for k in range(1, 4):
            known = known + u[k] * q[k] + n[k] * (v[k] - u[k])
        fields = [known, q[0], (v[0] - u[0]) * wide(inv, t)]
        left = jnp.concatenate(split_three(jnp.concatenate(fields, axis=0)), axis=0)
        hot = jnp.where(columns == yz_ref[pl.ds(t, 1), :], 1.0, 0.0).astype(jnp.bfloat16)
        product = jnp.dot(left, hot, preferred_element_type=jnp.float32)
        size = 3 * CX
        product = product[:size] + product[size : 2 * size] + product[2 * size :]
        mine = rows == x_ref[pl.ds(t, 1), :]
        for j in range(3):
            picked = jnp.where(mine, product[CX * j : CX * (j + 1)], 0.0)
            out_ref[pl.ds(j * NTURB + t, 1), 0:PTS] = jnp.sum(picked, axis=0, keepdims=True)
        return carry

    lax.fori_loop(0, NTURB, one, 0, unroll=True)


def call(kernel, outs, scratch, *args):
    vmem = pl.BlockSpec(memory_space=pltpu.VMEM)
    return pl.pallas_call(
        kernel,
        out_shape=[jax.ShapeDtypeStruct(shape, jnp.float32) for shape in outs],
        in_specs=[vmem] * len(args),
        out_specs=[vmem] * len(outs),
        scratch_shapes=[pltpu.VMEM(shape, jnp.float32) for shape in scratch],
        compiler_params=pltpu.CompilerParams(vmem_limit_bytes=VMEM_LIMIT),
    )(*args)


def route(value, target):
    size_x, size_y = lax.axis_size("gx"), lax.axis_size("gy")
    pairs = []
    for i in range(size_x):
        for j in range(size_y):
            to = target(i, j)
            if to is not None:
                pairs.append((i * size_y + j, to[0] % size_x * size_y + to[1] % size_y))
    return lax.ppermute(value, ("gx", "gy"), pairs)


def swap(value):
    return route(value, lambda i, j: (i ^ 1, j))


def exchange(rows):
    return lax.all_to_all(rows, ("gx", "gy"), 0, 0, tiled=True)


def merge_kernel(*refs):
    value = refs[0][...]
    for ref in refs[1:-1]:
        value = jnp.where(value != 0.0, value, ref[...])
    refs[-1][...] = value


def merge(value, parts):
    (value,) = call(merge_kernel, [value.shape], [], value, *parts)
    return value


def spread(value):
    size_x, size_y = lax.axis_size("gx"), lax.axis_size("gy")
    half = size_y // 2

    def across(first, second):
        def target(i, j):
            dy, dz = second if i % 2 else first
            return i, (j // half + dz) % 2 * half + (j % half + dy) % half

        return target

    def along(block, step, first, second):
        def target(i, j):
            move = second if i % 2 else first
            if move is None:
                return None
            return i // block * block + (i % block + move * step) % block, j

        return target

    value = merge(value, [swap(value)])
    turns = [((1, 0), (1, 1)), ((3, 0), (3, 1)), ((2, 0), (2, 1)), ((0, 1), (0, 1))]
    value = merge(value, [route(value, across(*turn)) for turn in turns])
    value = merge(value, [swap(value)])
    for block, step in ((8, 2), (size_x, 8)):
        turns = [(1, 2), (3, None)]
        value = merge(value, [route(value, along(block, step, *turn)) for turn in turns])
        value = merge(value, [swap(value)])
    return value


def shift(value, axis, step):
    size = lax.axis_size(axis)
    return lax.ppermute(value, axis, [(i, (i + step) % size) for i in range(size)])


def region(checkpoint, cotangent, ready):
    wide = (19, CX, OWN_SPAN + OWN_SPAN // 2)
    right, left = pl.pallas_call(
        pack_x_kernel,
        out_shape=[jax.ShapeDtypeStruct(wide, jnp.float32)] * 2,
        in_specs=[pl.BlockSpec(memory_space=pltpu.HBM)] * 2,
        out_specs=[pl.BlockSpec(memory_space=pltpu.VMEM)] * 2,
        scratch_shapes=[pltpu.VMEM(checkpoint.shape, jnp.float32)] * 2 + [pltpu.SemaphoreType.DMA((2,))],
        compiler_params=pltpu.CompilerParams(vmem_limit_bytes=VMEM_LIMIT),
    )(checkpoint, cotangent)
    before, after = shift(right, "gx", 1), shift(left, "gx", -1)
    before, after, *ready = lax.optimization_barrier((before, after) + ready)
    stack, edge = (19, RX, OWN_SPAN), (19, RX + CX, OWN_SPAN // 2)
    fields, cots, right, left = call(
        pack_y_kernel, [stack, stack, edge, edge], [], checkpoint, cotangent, before, after
    )
    return (shift(right, "gy", 1), fields, shift(left, "gy", -1), cots), ready


def body(checkpoint, cotangent, blade_area, hub_tile, point_side, point_local):
    count_x, count_y = lax.axis_size("gx"), lax.axis_size("gy")
    index_x, index_y = lax.axis_index("gx"), lax.axis_index("gy")
    area = blade_area.reshape(NTURB, PTS)
    side = point_side.reshape(NTURB, PTS)
    local = point_local.reshape(NTURB, PTS)
    hub = hub_tile.reshape(NTURB, 1)
    cell_x = (hub // count_y + side // 3 - 1 - index_x) * CX + local // (CY * NZ) + MARGIN
    cell_y = (hub % count_y + side % 3 - 1 - index_y) * CY + local // NZ % CY + MARGIN
    cell_x = cell_x % (count_x * CX)
    cell_y = cell_y % (count_y * CY)
    inside = (cell_x < RX) & (cell_y < RY)
    cell_x = jnp.where(inside, cell_x, -1)
    cell_yz = jnp.where(inside, cell_y * NZ + local % NZ, -1)
    mine_y = (cell_y >= MARGIN) & (cell_y < MARGIN + CY)
    inverse = jnp.broadcast_to(1.0 / jnp.sum(area, 1, keepdims=True), (NTURB, 128))

    full = (19, RX, LANES)
    flat = (RX, LANES)
    row = (NTURB, 128)
    (spots,) = call(area_kernel, [(NTURB,) + flat], [], cell_x, cell_yz, area)
    own_yz = jnp.where(mine_y, cell_yz, -1)
    parts, ready = region(checkpoint, cotangent, (spots, cell_x, own_yz, area, inverse))
    spots, cell_x, own_yz, area, inverse = ready

    s, v, rotor = [None] * 5, [None] * 5, [None] * 5
    table = (128, 128)
    every = (count_x * count_y, 128)
    s[1], v[1], cot, sums = call(first_kernel, [full, flat, full, every], [table], *parts, spots)
    for k in (1, 2, 3):
        last = k == 3
        s[k + 1], v[k + 1], rotor[k], sums = call(
            functools.partial(forward_kernel, last),
            [full, flat, row, every],
            [full, table] + ([flat] if last else []),
            *([s[k], v[k], spots, inverse, exchange(sums)] + ([cot] if last else [])),
        )
    adjoint = cot
    bar, drag = [None] * 5, [None] * 5
    for k in (4, 3, 2):
        first, sends = k == 4, k > 2
        args = [s[k], adjoint, spots, inverse, exchange(sums), v[k - 1]]
        outs = call(
            functools.partial(backward_kernel, first, sends),
            [full, flat, row] + ([every] if sends else []) + ([row] if first else []),
            [full, table],
            *(args + ([] if first else [rotor[k]])),
        )
        adjoint, drag[k - 1], bar[k] = outs[:3]
        sums = outs[3] if sends else None
        if first:
            rotor[4] = outs[4]
    (points,) = call(
        gather_kernel,
        [(3 * NTURB, 128)],
        [],
        *([cell_x, own_yz, cot] + drag[1:4] + v[1:] + rotor[1:] + bar[2:] + [inverse]),
    )
    grad, grad_area = call(
        last_kernel,
        [(19, CX, CY * NZ), (NTURB, PTS)],
        [full, full, row],
        *(s[1], adjoint, spots, rotor[1], spread(points), area, inverse),
    )
    return grad, grad_area.reshape(-1)


def solution(mesh):
    return jax.shard_map(
        body,
        mesh=mesh,
        in_specs=(P(None, "gx", "gy"), P(None, "gx", "gy"), P(), P(), P(), P()),
        out_specs=(P(None, "gx", "gy"), P()),
        check_vma=False,
    )
```

```python
import functools

import jax
import jax.numpy as jnp
import numpy as np
from jax import lax
from jax.experimental import pallas as pl
from jax.experimental.pallas import tpu as pltpu
from jax.sharding import PartitionSpec as P

NZ = 16
CX = 8
CY = 16
STEPS = 4
NTURB = 16
PTS = 96
MARGIN = 8
RX = CX + 2 * MARGIN
RY = CY + 2 * MARGIN
LANES = RY * NZ
OWN_ROWS = slice(MARGIN, MARGIN + CX)
OWN_LANE = MARGIN * NZ
OWN_SPAN = CY * NZ

VMEM_LIMIT = 8 * 1024 * 1024

TAU_ZERO = 0.52
SMAGORINSKY = 0.17 * 0.17
TINY = 1e-10
THRUST = 4.0
GHOST_RATES = np.array([1.05, 1.15, 1.25, 1.35, 1.45, 1.55, 1.65, 1.75, 1.85])
W_REST, W_AXIS, W_EDGE = 1.0 / 3.0, 1.0 / 18.0, 1.0 / 36.0

VECTORS = np.array(
    [(0, 0, 0), (1, 0, 0), (-1, 0, 0), (0, 1, 0), (0, -1, 0), (0, 0, 1), (0, 0, -1)]
    + [(1, 1, 0), (-1, -1, 0), (1, -1, 0), (-1, 1, 0), (1, 0, 1), (-1, 0, -1)]
    + [(1, 0, -1), (-1, 0, 1), (0, 1, 1), (0, -1, -1), (0, 1, -1), (0, -1, 1)]
)
OPPOSITE = [0] + [i + 1 if i % 2 else i - 1 for i in range(1, 19)]


def basis():
    c = VECTORS * 1.0
    weights = np.array([W_REST] + [W_AXIS] * 6 + [W_EDGE] * 12)
    x, y, z = c[:, 0], c[:, 1], c[:, 2]
    monomials = [np.ones(19), x, y, z, x * x, y * y, z * z, x * y, x * z, y * z]
    monomials += [x * y * y, x * z * z, y * x * x, y * z * z, z * x * x, z * y * y]
    monomials += [x * x * y * y, x * x * z * z, y * y * z * z]
    rows = []
    for entry in monomials:
        vector = entry * 1.0
        for sweep in range(2):
            for other in rows:
                vector = vector - np.sum(weights * vector * other) * other
        rows.append(vector / np.sqrt(np.sum(weights * vector * vector)))
    return np.stack(rows, 0)


def ghost_tables():
    rows = basis()
    odd = []
    for first, members in ((10, (1, 7, 11)), (12, (3, 7, 15)), (14, (5, 11, 15))):
        h = rows[first : first + 2][:, list(members)]
        rates = GHOST_RATES[first - 10 : first - 8]
        odd.append(np.diag([W_AXIS, W_EDGE, W_EDGE]) @ h.T @ np.diag(rates) @ h)
    even = rows[16:19][:, [0, 1, 3, 5, 7, 11, 15]]
    return odd, even, GHOST_RATES[6:9]


ODD, EVEN, EVEN_RATES = ghost_tables()
CLASS_W = [W_REST] + [W_AXIS] * 3 + [W_EDGE] * 3


def combine(coefs, values):
    total = None
    for coef, value in zip(coefs, values):
        coef = float(coef)
        if abs(coef) < 1e-12:
            continue
        term = value if coef == 1.0 else value * coef
        total = term if total is None else total + term
    return total


def split_parity(s):
    e = [s[i] + s[i + 1] for i in range(1, 19, 2)]
    o = [s[i] - s[i + 1] for i in range(1, 19, 2)]
    even = [s[0], e[0], e[1], e[2], e[3] + e[4], e[5] + e[6], e[7] + e[8]]
    cross = [e[3] - e[4], e[5] - e[6], e[7] - e[8]]
    odd_x = [o[0], o[3] + o[4], o[5] + o[6]]
    odd_y = [o[1], o[3] - o[4], o[7] + o[8]]
    odd_z = [o[2], o[5] - o[6], o[7] - o[8]]
    return even, cross, odd_x, odd_y, odd_z


def merge_parity(s, even, cross, odd_x, odd_y, odd_z):
    out = [s[0] + even[0]]
    for axis, odd in enumerate((odd_x, odd_y, odd_z)):
        out += [s[1 + 2 * axis] + (even[1 + axis] + odd[0])]
        out += [s[2 + 2 * axis] + (even[1 + axis] - odd[0])]
    pairs = ((odd_x[1], odd_y[1]), (odd_x[2], odd_z[1]), (odd_y[2], odd_z[2]))
    for family in range(3):
        first, second = pairs[family]
        base = 7 + 4 * family
        for sign, offset in ((1, 0), (-1, 2)):
            level = even[4 + family] + cross[family] if sign > 0 else even[4 + family] - cross[family]
            swing = first + second if sign > 0 else first - second
            out += [s[base + offset] + (level + swing), s[base + offset + 1] + (level - swing)]
    return out


def ghost_even(even, transpose):
    if transpose:
        even = [value * w for value, w in zip(even, CLASS_W)]
    m = [combine(EVEN[k], even) * float(EVEN_RATES[k]) for k in range(3)]
    out = [combine(EVEN[:, j], m) for j in range(7)]
    if not transpose:
        out = [value * w for value, w in zip(out, CLASS_W)]
    return out


def ghost_odd(index, odd, transpose):
    matrix = ODD[index].T if transpose else ODD[index]
    return [combine(matrix[j], odd) for j in range(3)]


def local_state(even, cross, odds):
    rho = ((even[0] + even[1]) + (even[2] + even[3])) + ((even[4] + even[5]) + even[6])
    inverse = 1.0 / rho
    mom = [(odd[0] + odd[1]) + odd[2] for odd in odds]
    u = [m * inverse for m in mom]
    third = rho * (1.0 / 3.0)
    edges = ((even[4], even[5]), (even[4], even[6]), (even[5], even[6]))
    stress = [
        ((even[1 + a] + edges[a][0]) + edges[a][1]) - third - mom[a] * u[a] for a in range(3)
    ]
    stress += [cross[0] - mom[0] * u[1], cross[1] - mom[0] * u[2], cross[2] - mom[1] * u[2]]
    square = stress[0] * stress[0] + stress[1] * stress[1] + stress[2] * stress[2]
    square = square + 2.0 * (
        stress[3] * stress[3] + stress[4] * stress[4] + stress[5] * stress[5]
    )
    norm = jnp.sqrt(square + TINY)
    root = jnp.sqrt(TAU_ZERO * TAU_ZERO + (18.0 * SMAGORINSKY) * norm * inverse)
    tau = 0.5 * (TAU_ZERO + root)
    return inverse, u, stress, norm, root, tau


def collide(s, force):
    even, cross, odd_x, odd_y, odd_z = split_parity(s)
    inverse, u, stress, norm, root, tau = local_state(even, cross, (odd_x, odd_y, odd_z))
    scale = 4.5 / tau
    k = [value * scale for value in stress]
    trace = (k[0] + k[1] + k[2]) * (1.0 / 3.0)
    relax = [-trace, k[0] - trace, k[1] - trace, k[2] - trace]
    relax += [k[0] + relax[2], k[0] + relax[3], k[1] + relax[3]]
    ghost = ghost_even(even, False)
    even_out = [-(relax[j] * CLASS_W[j] + ghost[j]) for j in range(7)]
    cross_out = [k[3 + j] * (-2.0 * W_EDGE) for j in range(3)]
    gx = ghost_odd(0, odd_x, False)
    ox = [force * (1.0 / 6.0) - gx[0], force * (1.0 / 12.0) - gx[1], force * (1.0 / 12.0) - gx[2]]
    oy = [-value for value in ghost_odd(1, odd_y, False)]
    oz = [-value for value in ghost_odd(2, odd_z, False)]
    return merge_parity(s, even_out, cross_out, ox, oy, oz)


def collide_adjoint(s, a, speed_bar):
    even, cross, odd_x, odd_y, odd_z = split_parity(s)
    inverse, u, stress, norm, root, tau = local_state(even, cross, (odd_x, odd_y, odd_z))
    ev, cr, ax, ay, az = split_parity(a)
    weighted = [value * w for value, w in zip(ev, CLASS_W)]
    total = ((weighted[0] + weighted[1]) + (weighted[2] + weighted[3])) + (
        (weighted[4] + weighted[5]) + weighted[6]
    )
    third = total * (1.0 / 3.0)
    edges = ((4, 5), (4, 6), (5, 6))
    beta = [
        (weighted[1 + i] + weighted[edges[i][0]] + weighted[edges[i][1]] - third) * -4.5
        for i in range(3)
    ]
    beta += [value * (-9.0 * W_EDGE) for value in cr]
    inv_tau = 1.0 / tau
    dot = (beta[0] * stress[0] + beta[1] * stress[1] + beta[2] * stress[2]) + (
        beta[3] * stress[3] + beta[4] * stress[4] + beta[5] * stress[5]
    )
    tau_bar = -dot * inv_tau * inv_tau
    common = tau_bar * (4.5 * SMAGORINSKY) * inverse / root
    factor = common / norm
    p_bar = [beta[i] * inv_tau + stress[i] * factor for i in range(3)]
    twice = factor + factor
    p_bar += [beta[i] * inv_tau + stress[i] * twice for i in range(3, 6)]
    sp = speed_bar * inverse
    px, py, pz, pxy, pxz, pyz = p_bar
    tx = pxy * u[1] + pxz * u[2]
    ty = pyz * u[2]
    mx = sp - (2.0 * px * u[0] + tx)
    my = -(2.0 * py * u[1] + pxy * u[0] + ty)
    mz = -(2.0 * pz * u[2] + pxz * u[0] + pyz * u[1])
    rho_bar = -common * norm * inverse - (px + py + pz) * (1.0 / 3.0)
    rho_bar = rho_bar + (px * u[0] + tx) * u[0] + (py * u[1] + ty) * u[1] + pz * u[2] * u[2]
    rho_bar = rho_bar - sp * u[0]
    ghost = ghost_even(ev, True)
    level = [rho_bar, rho_bar + px, rho_bar + py, rho_bar + pz]
    level += [level[1] + py, level[1] + pz, level[2] + pz]
    even_out = [level[j] - ghost[j] for j in range(7)]
    gx, gy, gz = (ghost_odd(i, odd, True) for i, odd in enumerate((ax, ay, az)))
    ox = [mx - value for value in gx]
    oy = [my - value for value in gy]
    oz = [mz - value for value in gz]
    return merge_parity(a, even_out, p_bar[3:], ox, oy, oz)


def chunks(body):
    def step(index, carry):
        lane = pl.multiple_of(index * 128, 128)
        for row in range(0, RX, 8):
            body(pl.ds(row, 8), pl.ds(lane, 128))
        return carry

    lax.fori_loop(0, LANES // 128, step, 0, unroll=True)


def shifted(value, cx, cy, cz):
    lane = (NZ * cy + cz) % LANES
    if lane:
        value = pltpu.roll(value, lane, 1)
    if cx % RX:
        value = pltpu.roll(value, cx % RX, 0)
    return value


def height():
    return lax.broadcasted_iota(jnp.int32, (RX, LANES), 1) & (NZ - 1)


def stream(field, out):
    z = height()
    for i in range(19):
        cx, cy, cz = (int(v) for v in VECTORS[i])
        value = shifted(field[i], cx, cy, cz)
        if cz:
            value = jnp.where(z == (0 if cz > 0 else NZ - 1), field[OPPOSITE[i]], value)
        out[i] = value


def stream_adjoint(field, out):
    z = height()
    for i in range(19):
        cx, cy, cz = (int(v) for v in VECTORS[i])
        value = field[i]
        if cz:
            value = jnp.where(z == (0 if cz > 0 else NZ - 1), 0.0, value)
        value = shifted(value, -cx, -cy, -cz)
        if cz:
            value = value + jnp.where(z == (NZ - 1 if cz > 0 else 0), field[OPPOSITE[i]], 0.0)
        out[i] = value


def speeds(s_ref, v_ref):
    def one(rows, lanes):
        s = [s_ref[i, rows, lanes] for i in range(19)]
        even, cross, odd_x, odd_y, odd_z = split_parity(s)
        rho = ((even[0] + even[1]) + (even[2] + even[3])) + ((even[4] + even[5]) + even[6])
        v_ref[rows, lanes] = ((odd_x[0] + odd_x[1]) + odd_x[2]) / rho

    chunks(one)


def push_back(a):
    odd = (a[7] - a[8]) + (a[9] - a[10]) + (a[11] - a[12]) + (a[13] - a[14])
    return (a[1] - a[2]) * (1.0 / 6.0) + odd * (1.0 / 12.0)


def turbine_sums(area_ref, field_ref, sums_ref, base):
    parts = [field_ref[OWN_ROWS, OWN_LANE + j : OWN_LANE + j + 128] for j in range(0, OWN_SPAN, 128)]
    for t in range(NTURB):
        total = None
        for j, part in enumerate(parts):
            lane = OWN_LANE + 128 * j
            term = area_ref[t, OWN_ROWS, lane : lane + 128] * part
            total = term if total is None else total + term
        sums_ref[base + t : base + t + 1, :] = jnp.sum(total, axis=0, keepdims=True)


def publish(sums_ref, out_ref):
    shape = sums_ref.shape
    total = jnp.broadcast_to(jnp.sum(sums_ref[...], axis=1, keepdims=True), shape)
    index = lax.broadcasted_iota(jnp.int32, shape, 0)
    picked = jnp.where(index == lax.broadcasted_iota(jnp.int32, shape, 1), total, 0.0)
    row = jnp.broadcast_to(jnp.sum(picked, axis=0, keepdims=True), (8, 128))
    for j in range(0, out_ref.shape[0], 8):
        out_ref[j : j + 8, :] = row


def totals(got_ref, base):
    row = jnp.sum(got_ref[...], axis=0, keepdims=True)
    index = lax.broadcasted_iota(jnp.int32, (NTURB, 128), 0) + base
    lane = lax.broadcasted_iota(jnp.int32, (NTURB, 128), 1)
    picked = jnp.where(index == lane, jnp.broadcast_to(row, (NTURB, 128)), 0.0)
    return jnp.broadcast_to(jnp.sum(picked, axis=1, keepdims=True), (NTURB, 128))


def weighted_area(area_ref, weight_ref, rows, lanes):
    total = None
    for t in range(NTURB):
        term = area_ref[t, rows, lanes] * weight_ref[t : t + 1, :]
        total = term if total is None else total + term
    return total


def split_three(value):
    high = value.astype(jnp.bfloat16)
    rest = value - high.astype(jnp.float32)
    middle = rest.astype(jnp.bfloat16)
    return high, middle, (rest - middle.astype(jnp.float32)).astype(jnp.bfloat16)


def area_kernel(x_ref, yz_ref, area_ref, out_ref):
    rows = lax.broadcasted_iota(jnp.int32, (RX, PTS), 0)
    columns = lax.broadcasted_iota(jnp.int32, (LANES, PTS), 0)

    def one(t, carry):
        point = pl.ds(t, 1)
        spots = jnp.where(rows == x_ref[point, :], area_ref[point, :], 0.0)
        left = jnp.concatenate(split_three(spots), axis=0)
        hot = jnp.where(columns == yz_ref[point, :], 1.0, 0.0).astype(jnp.bfloat16)
        product = lax.dot_general(
            left, hot, (((1,), (1,)), ((), ())), preferred_element_type=jnp.float32
        )
        out_ref[t] = product[:RX] + product[RX : 2 * RX] + product[2 * RX :]
        return carry

    lax.fori_loop(0, NTURB, one, 0)


def pack_x_kernel(field_hbm, cot_hbm, next_ref, prev_ref, field_ref, cot_ref, sems):
    first = pltpu.make_async_copy(field_hbm, field_ref, sems.at[0])
    second = pltpu.make_async_copy(cot_hbm, cot_ref, sems.at[1])
    first.start()
    second.start()
    first.wait()
    second.wait()
    half = OWN_SPAN // 2
    top = lax.broadcasted_iota(jnp.int32, (CX, half), 0) < CX // 2
    for i in range(19):
        low, high = cot_ref[i, :, :half], cot_ref[i, :, half:]
        next_ref[i, :, :OWN_SPAN] = field_ref[i]
        prev_ref[i, :, :OWN_SPAN] = field_ref[i]
        next_ref[i, :, OWN_SPAN:] = jnp.where(top, pltpu.roll(low, CX // 2, 0), high)
        prev_ref[i, :, OWN_SPAN:] = jnp.where(top, low, pltpu.roll(high, CX // 2, 0))


def pack_y_kernel(field_ref, cot_ref, before_ref, after_ref, fields_ref, cots_ref, next_ref, prev_ref):
    half = OWN_SPAN // 2
    top = lax.broadcasted_iota(jnp.int32, (CX, half), 0) < CX // 2
    left = lax.broadcasted_iota(jnp.int32, (CX, half), 1) < half // 2
    for i in range(19):
        for j, part in enumerate((before_ref[i, :, :OWN_SPAN], field_ref[i], after_ref[i, :, :OWN_SPAN])):
            rows = slice(CX * j, CX * (j + 1))
            fields_ref[i, rows] = part
            prev_ref[i, rows] = part[:, :half]
            next_ref[i, rows] = part[:, half:]
        before, after = before_ref[i, :, OWN_SPAN:], after_ref[i, :, OWN_SPAN:]
        low = (pltpu.roll(before, CX // 2, 0), cot_ref[i, :, :half], after)
        high = (before, cot_ref[i, :, half:], pltpu.roll(after, CX // 2, 0))
        for j in range(3):
            rows = slice(CX * j, CX * (j + 1))
            cots_ref[i, rows, :half] = low[j]
            cots_ref[i, rows, half:] = high[j]
        outer = jnp.where(top, low[2], low[0])
        prev_ref[i, RX:] = jnp.where(left, low[1], pltpu.roll(outer, half // 2, 1))
        outer = jnp.where(top, high[2], high[0])
        next_ref[i, RX:] = jnp.where(left, pltpu.roll(high[1], half // 2, 1), outer)


class Joined:
    def __init__(self, before, here, after):
        self.parts = before, here, after

    def __getitem__(self, index):
        before, here, after = self.parts
        return jnp.concatenate([before[index, :RX], here[index], after[index, :RX]], axis=1)


def first_kernel(before_ref, fields_ref, after_ref, cots_ref, area_ref, s_ref, v_ref, cot_ref, out_ref, sums):
    stream(Joined(before_ref, fields_ref, after_ref), s_ref)
    speeds(s_ref, v_ref)
    turbine_sums(area_ref, v_ref, sums, 0)
    publish(sums, out_ref)
    half = OWN_SPAN // 2
    for i in range(19):
        before, after = before_ref[i, RX:], after_ref[i, RX:]
        turned = pltpu.roll(before, half // 2, 1), pltpu.roll(after, half // 2, 1)
        for j in range(3):
            rows = slice(CX * j, CX * (j + 1))
            cot_ref[i, rows, :OWN_LANE] = turned[0] if j == 1 else before
            cot_ref[i, rows, OWN_LANE + OWN_SPAN :] = after if j == 1 else turned[1]
        cot_ref[i, :, OWN_LANE : OWN_LANE + OWN_SPAN] = cots_ref[i]


def forward_kernel(last, s_ref, v_ref, area_ref, inv_ref, got_ref, *rest):
    if last:
        cot_ref, next_ref, vn_ref, rotor_ref, out_ref, field, sums, drag = rest
    else:
        next_ref, vn_ref, rotor_ref, out_ref, field, sums = rest
    rotor_ref[...] = totals(got_ref, 0) * inv_ref[...]

    def one(rows, lanes):
        s = [s_ref[i, rows, lanes] for i in range(19)]
        force = weighted_area(area_ref, rotor_ref, rows, lanes) * v_ref[rows, lanes] * -THRUST
        for i, value in enumerate(collide(s, force)):
            field[i, rows, lanes] = value

    chunks(one)
    stream(field, next_ref)
    speeds(next_ref, vn_ref)
    turbine_sums(area_ref, vn_ref, sums, 0)
    if last:

        def other(rows, lanes):
            a = [cot_ref[i, rows, lanes] for i in range(19)]
            drag[rows, lanes] = push_back(a) * vn_ref[rows, lanes] * -THRUST

        chunks(other)
        turbine_sums(area_ref, drag, sums, NTURB)
    publish(sums, out_ref)


def adjoint_field(s_ref, a_ref, area_ref, rotor_ref, bar_ref, field):
    def one(rows, lanes):
        s = [s_ref[i, rows, lanes] for i in range(19)]
        a = [a_ref[i, rows, lanes] for i in range(19)]
        speed_bar = weighted_area(area_ref, rotor_ref, rows, lanes) * push_back(a) * -THRUST
        speed_bar = speed_bar + weighted_area(area_ref, bar_ref, rows, lanes)
        for i, value in enumerate(collide_adjoint(s, a, speed_bar)):
            field[i, rows, lanes] = value

    chunks(one)


def backward_kernel(first, sends, s_ref, a_ref, area_ref, inv_ref, got_ref, v_ref, *rest):
    rest = list(rest)
    rotor_ref = None if first else rest.pop(0)
    out_ref, drag_ref, bar_ref = rest[:3]
    field, sums = rest[-2:]
    if first:
        rotor_ref = rest[-3]
        rotor_ref[...] = totals(got_ref, 0) * inv_ref[...]
    bar_ref[...] = totals(got_ref, NTURB if first else 0) * inv_ref[...]
    adjoint_field(s_ref, a_ref, area_ref, rotor_ref, bar_ref, field)
    stream_adjoint(field, out_ref)

    def other(rows, lanes):
        a = [out_ref[i, rows, lanes] for i in range(19)]
        drag_ref[rows, lanes] = push_back(a) * v_ref[rows, lanes] * -THRUST

    chunks(other)
    if sends:
        turbine_sums(area_ref, drag_ref, sums, 0)
        publish(sums, rest[3])


def last_kernel(s_ref, a_ref, area_ref, rotor_ref, point_ref, size_ref, inv_ref, out_ref, grad_ref, field, result, bar):
    known, swing, slope = (point_ref[NTURB * j : NTURB * (j + 1), :] for j in range(3))
    total = jnp.sum(size_ref[...] * swing[:, :PTS], axis=1, keepdims=True)
    grad = known + total * slope
    turned = [grad] + [pltpu.roll(grad, 128 - PTS // 3 * j, 1) for j in (1, 2, 3)]
    lane = lax.broadcasted_iota(jnp.int32, (1, 128), 1)
    for m in range(NTURB // 4):
        for j in range(3):
            row = 4 * m + j
            first, second = turned[j][row : row + 1], turned[j + 1][row + 1 : row + 2]
            grad_ref[3 * m + j : 3 * m + j + 1, :] = jnp.where(lane < 128 - 32 * (j + 1), first, second)
    bar[...] = jnp.broadcast_to(total, (NTURB, 128)) * inv_ref[...]
    adjoint_field(s_ref, a_ref, area_ref, rotor_ref, bar, field)
    stream_adjoint(field, result)
    for i in range(19):
        out_ref[i] = result[i, OWN_ROWS, OWN_LANE : OWN_LANE + OWN_SPAN]


def gather_kernel(x_ref, yz_ref, cot_ref, q1, q2, q3, v1, v2, v3, v4, u1, u2, u3, u4, n2, n3, n4, inv, out_ref):
    own = (OWN_ROWS, slice(OWN_LANE, OWN_LANE + OWN_SPAN))
    v = [ref[own] for ref in (v1, v2, v3, v4)]
    q = [ref[own] for ref in (q1, q2, q3)]
    a = [cot_ref[(i,) + own] for i in range(19)]
    q.append(push_back(a) * v[3] * -THRUST)
    rows = lax.broadcasted_iota(jnp.int32, (CX, PTS), 0) + MARGIN
    columns = lax.broadcasted_iota(jnp.int32, (OWN_SPAN, PTS), 0) + OWN_LANE

    def wide(ref, t):
        return jnp.concatenate([ref[pl.ds(t, 1), :]] * (OWN_SPAN // 128), axis=1)

    out_ref[...] = jnp.zeros_like(out_ref)

    def one(t, carry):
        u = [wide(ref, t) for ref in (u1, u2, u3, u4)]
        n = [None] + [wide(ref, t) for ref in (n2, n3, n4)]
        known = u[0] * q[0]
        for k in range(1, 4):
            known = known + u[k] * q[k] + n[k] * (v[k] - u[k])
        fields = [known, q[0], (v[0] - u[0]) * wide(inv, t)]
        left = jnp.concatenate(split_three(jnp.concatenate(fields, axis=0)), axis=0)
        hot = jnp.where(columns == yz_ref[pl.ds(t, 1), :], 1.0, 0.0).astype(jnp.bfloat16)
        product = jnp.dot(left, hot, preferred_element_type=jnp.float32)
        size = 3 * CX
        product = product[:size] + product[size : 2 * size] + product[2 * size :]
        mine = rows == x_ref[pl.ds(t, 1), :]
        for j in range(3):
            picked = jnp.where(mine, product[CX * j : CX * (j + 1)], 0.0)
            out_ref[pl.ds(j * NTURB + t, 1), 0:PTS] = jnp.sum(picked, axis=0, keepdims=True)
        return carry

    lax.fori_loop(0, NTURB, one, 0, unroll=True)


def call(kernel, outs, scratch, *args):
    vmem = pl.BlockSpec(memory_space=pltpu.VMEM)
    return pl.pallas_call(
        kernel,
        out_shape=[jax.ShapeDtypeStruct(shape, jnp.float32) for shape in outs],
        in_specs=[vmem] * len(args),
        out_specs=[vmem] * len(outs),
        scratch_shapes=[pltpu.VMEM(shape, jnp.float32) for shape in scratch],
        compiler_params=pltpu.CompilerParams(vmem_limit_bytes=VMEM_LIMIT),
    )(*args)


def route(value, target):
    size_x, size_y = lax.axis_size("gx"), lax.axis_size("gy")
    pairs = []
    for i in range(size_x):
        for j in range(size_y):
            to = target(i, j)
            if to is not None:
                pairs.append((i * size_y + j, to[0] % size_x * size_y + to[1] % size_y))
    return lax.ppermute(value, ("gx", "gy"), pairs)


def swap(value):
    return route(value, lambda i, j: (i ^ 1, j))


def exchange(rows):
    return lax.all_to_all(rows, ("gx", "gy"), 0, 0, tiled=True)


def merge_kernel(*refs):
    value = refs[0][...]
    for ref in refs[1:-1]:
        value = jnp.where(value != 0.0, value, ref[...])
    refs[-1][...] = value


def merge(value, parts):
    (value,) = call(merge_kernel, [value.shape], [], value, *parts)
    return value


def spread(value):
    size_x, size_y = lax.axis_size("gx"), lax.axis_size("gy")
    half = size_y // 2

    def across(first, second):
        def target(i, j):
            dy, dz = second if i % 2 else first
            return i, (j // half + dz) % 2 * half + (j % half + dy) % half

        return target

    def along(block, step, first, second):
        def target(i, j):
            move = second if i % 2 else first
            if move is None:
                return None
            return i // block * block + (i % block + move * step) % block, j

        return target

    value = merge(value, [swap(value)])
    turns = [((1, 0), (1, 1)), ((3, 0), (3, 1)), ((2, 0), (2, 1)), ((0, 1), (0, 1))]
    value = merge(value, [route(value, across(*turn)) for turn in turns])
    value = merge(value, [swap(value)])
    for block, step in ((8, 2), (size_x, 8)):
        turns = [(1, 2), (3, None)]
        value = merge(value, [route(value, along(block, step, *turn)) for turn in turns])
        value = merge(value, [swap(value)])
    return value


def shift(value, axis, step):
    size = lax.axis_size(axis)
    return lax.ppermute(value, axis, [(i, (i + step) % size) for i in range(size)])


def region(checkpoint, cotangent, ready):
    wide = (19, CX, OWN_SPAN + OWN_SPAN // 2)
    right, left = pl.pallas_call(
        pack_x_kernel,
        out_shape=[jax.ShapeDtypeStruct(wide, jnp.float32)] * 2,
        in_specs=[pl.BlockSpec(memory_space=pltpu.HBM)] * 2,
        out_specs=[pl.BlockSpec(memory_space=pltpu.VMEM)] * 2,
        scratch_shapes=[pltpu.VMEM(checkpoint.shape, jnp.float32)] * 2 + [pltpu.SemaphoreType.DMA((2,))],
        compiler_params=pltpu.CompilerParams(vmem_limit_bytes=VMEM_LIMIT),
    )(checkpoint, cotangent)
    before, after = shift(right, "gx", 1), shift(left, "gx", -1)
    before, after, *ready = lax.optimization_barrier((before, after) + ready)
    stack, edge = (19, RX, OWN_SPAN), (19, RX + CX, OWN_SPAN // 2)
    fields, cots, right, left = call(
        pack_y_kernel, [stack, stack, edge, edge], [], checkpoint, cotangent, before, after
    )
    return (shift(right, "gy", 1), fields, shift(left, "gy", -1), cots), ready


def body(checkpoint, cotangent, blade_area, hub_tile, point_side, point_local):
    count_x, count_y = lax.axis_size("gx"), lax.axis_size("gy")
    index_x, index_y = lax.axis_index("gx"), lax.axis_index("gy")
    area = blade_area.reshape(NTURB, PTS)
    side = point_side.reshape(NTURB, PTS)
    local = point_local.reshape(NTURB, PTS)
    hub = hub_tile.reshape(NTURB, 1)
    cell_x = (hub // count_y + side // 3 - 1 - index_x) * CX + local // (CY * NZ) + MARGIN
    cell_y = (hub % count_y + side % 3 - 1 - index_y) * CY + local // NZ % CY + MARGIN
    cell_x = cell_x % (count_x * CX)
    cell_y = cell_y % (count_y * CY)
    inside = (cell_x < RX) & (cell_y < RY)
    cell_x = jnp.where(inside, cell_x, -1)
    cell_yz = jnp.where(inside, cell_y * NZ + local % NZ, -1)
    mine_y = (cell_y >= MARGIN) & (cell_y < MARGIN + CY)
    inverse = jnp.broadcast_to(1.0 / jnp.sum(area, 1, keepdims=True), (NTURB, 128))

    full = (19, RX, LANES)
    flat = (RX, LANES)
    row = (NTURB, 128)
    (spots,) = call(area_kernel, [(NTURB,) + flat], [], cell_x, cell_yz, area)
    own_yz = jnp.where(mine_y, cell_yz, -1)
    parts, ready = region(checkpoint, cotangent, (spots, cell_x, own_yz, area, inverse))
    spots, cell_x, own_yz, area, inverse = ready

    s, v, rotor = [None] * 5, [None] * 5, [None] * 5
    every = (count_x * count_y, 128)
    s[1], v[1], cot, sums = call(first_kernel, [full, flat, full, every], [row], *parts, spots)
    for k in (1, 2, 3):
        last = k == 3
        s[k + 1], v[k + 1], rotor[k], sums = call(
            functools.partial(forward_kernel, last),
            [full, flat, row, every],
            [full, (2 * NTURB, 128) if last else row] + ([flat] if last else []),
            *([s[k], v[k], spots, inverse, exchange(sums)] + ([cot] if last else [])),
        )
    adjoint = cot
    bar, drag = [None] * 5, [None] * 5
    for k in (4, 3, 2):
        first, sends = k == 4, k > 2
        args = [s[k], adjoint, spots, inverse, exchange(sums), v[k - 1]]
        outs = call(
            functools.partial(backward_kernel, first, sends),
            [full, flat, row] + ([every] if sends else []) + ([row] if first else []),
            [full, row],
            *(args + ([] if first else [rotor[k]])),
        )
        adjoint, drag[k - 1], bar[k] = outs[:3]
        sums = outs[3] if sends else None
        if first:
            rotor[4] = outs[4]
    (points,) = call(
        gather_kernel,
        [(3 * NTURB, 128)],
        [],
        *([cell_x, own_yz, cot] + drag[1:4] + v[1:] + rotor[1:] + bar[2:] + [inverse]),
    )
    grad, grad_area = call(
        last_kernel,
        [(19, CX, CY * NZ), (NTURB * PTS // 128, 128)],
        [full, full, row],
        *(s[1], adjoint, spots, rotor[1], spread(points), area, inverse),
    )
    return grad, grad_area.reshape(-1)


def solution(mesh):
    return jax.shard_map(
        body,
        mesh=mesh,
        in_specs=(P(None, "gx", "gy"), P(None, "gx", "gy"), P(), P(), P(), P()),
        out_specs=(P(None, "gx", "gy"), P()),
        check_vma=False,
    )
```

```python
import functools

import jax
import jax.numpy as jnp
import numpy as np
from jax import lax
from jax.experimental import pallas as pl
from jax.experimental.pallas import tpu as pltpu
from jax.sharding import PartitionSpec as P

NZ = 16
CX = 8
CY = 16
STEPS = 4
NTURB = 16
PTS = 96
MARGIN = 8
RX = CX + 2 * MARGIN
RY = CY + 2 * MARGIN
LANES = RY * NZ
OWN_ROWS = slice(MARGIN, MARGIN + CX)
OWN_LANE = MARGIN * NZ
OWN_SPAN = CY * NZ

VMEM_LIMIT = 8 * 1024 * 1024

TAU_ZERO = 0.52
SMAGORINSKY = 0.17 * 0.17
TINY = 1e-10
THRUST = 4.0
GHOST_RATES = np.array([1.05, 1.15, 1.25, 1.35, 1.45, 1.55, 1.65, 1.75, 1.85])
W_REST, W_AXIS, W_EDGE = 1.0 / 3.0, 1.0 / 18.0, 1.0 / 36.0

VECTORS = np.array(
    [(0, 0, 0), (1, 0, 0), (-1, 0, 0), (0, 1, 0), (0, -1, 0), (0, 0, 1), (0, 0, -1)]
    + [(1, 1, 0), (-1, -1, 0), (1, -1, 0), (-1, 1, 0), (1, 0, 1), (-1, 0, -1)]
    + [(1, 0, -1), (-1, 0, 1), (0, 1, 1), (0, -1, -1), (0, 1, -1), (0, -1, 1)]
)
OPPOSITE = [0] + [i + 1 if i % 2 else i - 1 for i in range(1, 19)]


def basis():
    c = VECTORS * 1.0
    weights = np.array([W_REST] + [W_AXIS] * 6 + [W_EDGE] * 12)
    x, y, z = c[:, 0], c[:, 1], c[:, 2]
    monomials = [np.ones(19), x, y, z, x * x, y * y, z * z, x * y, x * z, y * z]
    monomials += [x * y * y, x * z * z, y * x * x, y * z * z, z * x * x, z * y * y]
    monomials += [x * x * y * y, x * x * z * z, y * y * z * z]
    rows = []
    for entry in monomials:
        vector = entry * 1.0
        for sweep in range(2):
            for other in rows:
                vector = vector - np.sum(weights * vector * other) * other
        rows.append(vector / np.sqrt(np.sum(weights * vector * vector)))
    return np.stack(rows, 0)


def ghost_tables():
    rows = basis()
    odd = []
    for first, members in ((10, (1, 7, 11)), (12, (3, 7, 15)), (14, (5, 11, 15))):
        h = rows[first : first + 2][:, list(members)]
        rates = GHOST_RATES[first - 10 : first - 8]
        odd.append(np.diag([W_AXIS, W_EDGE, W_EDGE]) @ h.T @ np.diag(rates) @ h)
    even = rows[16:19][:, [0, 1, 3, 5, 7, 11, 15]]
    return odd, even, GHOST_RATES[6:9]


ODD, EVEN, EVEN_RATES = ghost_tables()
CLASS_W = [W_REST] + [W_AXIS] * 3 + [W_EDGE] * 3


def combine(coefs, values):
    total = None
    for coef, value in zip(coefs, values):
        coef = float(coef)
        if abs(coef) < 1e-12:
            continue
        term = value if coef == 1.0 else value * coef
        total = term if total is None else total + term
    return total


def split_parity(s):
    e = [s[i] + s[i + 1] for i in range(1, 19, 2)]
    o = [s[i] - s[i + 1] for i in range(1, 19, 2)]
    even = [s[0], e[0], e[1], e[2], e[3] + e[4], e[5] + e[6], e[7] + e[8]]
    cross = [e[3] - e[4], e[5] - e[6], e[7] - e[8]]
    odd_x = [o[0], o[3] + o[4], o[5] + o[6]]
    odd_y = [o[1], o[3] - o[4], o[7] + o[8]]
    odd_z = [o[2], o[5] - o[6], o[7] - o[8]]
    return even, cross, odd_x, odd_y, odd_z


def merge_parity(s, even, cross, odd_x, odd_y, odd_z):
    out = [s[0] + even[0]]
    for axis, odd in enumerate((odd_x, odd_y, odd_z)):
        out += [s[1 + 2 * axis] + (even[1 + axis] + odd[0])]
        out += [s[2 + 2 * axis] + (even[1 + axis] - odd[0])]
    pairs = ((odd_x[1], odd_y[1]), (odd_x[2], odd_z[1]), (odd_y[2], odd_z[2]))
    for family in range(3):
        first, second = pairs[family]
        base = 7 + 4 * family
        for sign, offset in ((1, 0), (-1, 2)):
            level = even[4 + family] + cross[family] if sign > 0 else even[4 + family] - cross[family]
            swing = first + second if sign > 0 else first - second
            out += [s[base + offset] + (level + swing), s[base + offset + 1] + (level - swing)]
    return out


def ghost_even(even, transpose):
    if transpose:
        even = [value * w for value, w in zip(even, CLASS_W)]
    m = [combine(EVEN[k], even) * float(EVEN_RATES[k]) for k in range(3)]
    out = [combine(EVEN[:, j], m) for j in range(7)]
    if not transpose:
        out = [value * w for value, w in zip(out, CLASS_W)]
    return out


def ghost_odd(index, odd, transpose):
    matrix = ODD[index].T if transpose else ODD[index]
    return [combine(matrix[j], odd) for j in range(3)]


def local_state(even, cross, odds):
    rho = ((even[0] + even[1]) + (even[2] + even[3])) + ((even[4] + even[5]) + even[6])
    inverse = 1.0 / rho
    mom = [(odd[0] + odd[1]) + odd[2] for odd in odds]
    u = [m * inverse for m in mom]
    third = rho * (1.0 / 3.0)
    edges = ((even[4], even[5]), (even[4], even[6]), (even[5], even[6]))
    stress = [
        ((even[1 + a] + edges[a][0]) + edges[a][1]) - third - mom[a] * u[a] for a in range(3)
    ]
    stress += [cross[0] - mom[0] * u[1], cross[1] - mom[0] * u[2], cross[2] - mom[1] * u[2]]
    square = stress[0] * stress[0] + stress[1] * stress[1] + stress[2] * stress[2]
    square = square + 2.0 * (
        stress[3] * stress[3] + stress[4] * stress[4] + stress[5] * stress[5]
    )
    norm = jnp.sqrt(square + TINY)
    root = jnp.sqrt(TAU_ZERO * TAU_ZERO + (18.0 * SMAGORINSKY) * norm * inverse)
    tau = 0.5 * (TAU_ZERO + root)
    return inverse, u, stress, norm, root, tau


def collide(s, force):
    even, cross, odd_x, odd_y, odd_z = split_parity(s)
    inverse, u, stress, norm, root, tau = local_state(even, cross, (odd_x, odd_y, odd_z))
    scale = 4.5 / tau
    k = [value * scale for value in stress]
    trace = (k[0] + k[1] + k[2]) * (1.0 / 3.0)
    relax = [-trace, k[0] - trace, k[1] - trace, k[2] - trace]
    relax += [k[0] + relax[2], k[0] + relax[3], k[1] + relax[3]]
    ghost = ghost_even(even, False)
    even_out = [-(relax[j] * CLASS_W[j] + ghost[j]) for j in range(7)]
    cross_out = [k[3 + j] * (-2.0 * W_EDGE) for j in range(3)]
    gx = ghost_odd(0, odd_x, False)
    ox = [force * (1.0 / 6.0) - gx[0], force * (1.0 / 12.0) - gx[1], force * (1.0 / 12.0) - gx[2]]
    oy = [-value for value in ghost_odd(1, odd_y, False)]
    oz = [-value for value in ghost_odd(2, odd_z, False)]
    return merge_parity(s, even_out, cross_out, ox, oy, oz)


def collide_adjoint(s, a, speed_bar):
    even, cross, odd_x, odd_y, odd_z = split_parity(s)
    inverse, u, stress, norm, root, tau = local_state(even, cross, (odd_x, odd_y, odd_z))
    ev, cr, ax, ay, az = split_parity(a)
    weighted = [value * w for value, w in zip(ev, CLASS_W)]
    total = ((weighted[0] + weighted[1]) + (weighted[2] + weighted[3])) + (
        (weighted[4] + weighted[5]) + weighted[6]
    )
    third = total * (1.0 / 3.0)
    edges = ((4, 5), (4, 6), (5, 6))
    beta = [
        (weighted[1 + i] + weighted[edges[i][0]] + weighted[edges[i][1]] - third) * -4.5
        for i in range(3)
    ]
    beta += [value * (-9.0 * W_EDGE) for value in cr]
    inv_tau = 1.0 / tau
    dot = (beta[0] * stress[0] + beta[1] * stress[1] + beta[2] * stress[2]) + (
        beta[3] * stress[3] + beta[4] * stress[4] + beta[5] * stress[5]
    )
    tau_bar = -dot * inv_tau * inv_tau
    common = tau_bar * (4.5 * SMAGORINSKY) * inverse / root
    factor = common / norm
    p_bar = [beta[i] * inv_tau + stress[i] * factor for i in range(3)]
    twice = factor + factor
    p_bar += [beta[i] * inv_tau + stress[i] * twice for i in range(3, 6)]
    sp = speed_bar * inverse
    px, py, pz, pxy, pxz, pyz = p_bar
    tx = pxy * u[1] + pxz * u[2]
    ty = pyz * u[2]
    mx = sp - (2.0 * px * u[0] + tx)
    my = -(2.0 * py * u[1] + pxy * u[0] + ty)
    mz = -(2.0 * pz * u[2] + pxz * u[0] + pyz * u[1])
    rho_bar = -common * norm * inverse - (px + py + pz) * (1.0 / 3.0)
    rho_bar = rho_bar + (px * u[0] + tx) * u[0] + (py * u[1] + ty) * u[1] + pz * u[2] * u[2]
    rho_bar = rho_bar - sp * u[0]
    ghost = ghost_even(ev, True)
    level = [rho_bar, rho_bar + px, rho_bar + py, rho_bar + pz]
    level += [level[1] + py, level[1] + pz, level[2] + pz]
    even_out = [level[j] - ghost[j] for j in range(7)]
    gx, gy, gz = (ghost_odd(i, odd, True) for i, odd in enumerate((ax, ay, az)))
    ox = [mx - value for value in gx]
    oy = [my - value for value in gy]
    oz = [mz - value for value in gz]
    return merge_parity(a, even_out, p_bar[3:], ox, oy, oz)


def chunks(body):
    def step(index, carry):
        lane = pl.multiple_of(index * 128, 128)
        for row in range(0, RX, 8):
            body(pl.ds(row, 8), pl.ds(lane, 128))
        return carry

    lax.fori_loop(0, LANES // 128, step, 0, unroll=True)


def shifted(value, cx, cy, cz):
    lane = (NZ * cy + cz) % LANES
    if lane:
        value = pltpu.roll(value, lane, 1)
    if cx % RX:
        value = pltpu.roll(value, cx % RX, 0)
    return value


def height():
    return lax.broadcasted_iota(jnp.int32, (RX, LANES), 1) & (NZ - 1)


def stream(field, out):
    z = height()
    for i in range(19):
        cx, cy, cz = (int(v) for v in VECTORS[i])
        value = shifted(field[i], cx, cy, cz)
        if cz:
            value = jnp.where(z == (0 if cz > 0 else NZ - 1), field[OPPOSITE[i]], value)
        out[i] = value


def stream_adjoint(field, out):
    z = height()
    for i in range(19):
        cx, cy, cz = (int(v) for v in VECTORS[i])
        value = field[i]
        if cz:
            value = jnp.where(z == (0 if cz > 0 else NZ - 1), 0.0, value)
        value = shifted(value, -cx, -cy, -cz)
        if cz:
            value = value + jnp.where(z == (NZ - 1 if cz > 0 else 0), field[OPPOSITE[i]], 0.0)
        out[i] = value


def speeds(s_ref, v_ref):
    def one(rows, lanes):
        s = [s_ref[i, rows, lanes] for i in range(19)]
        even, cross, odd_x, odd_y, odd_z = split_parity(s)
        rho = ((even[0] + even[1]) + (even[2] + even[3])) + ((even[4] + even[5]) + even[6])
        v_ref[rows, lanes] = ((odd_x[0] + odd_x[1]) + odd_x[2]) / rho

    chunks(one)


def push_back(a):
    odd = (a[7] - a[8]) + (a[9] - a[10]) + (a[11] - a[12]) + (a[13] - a[14])
    return (a[1] - a[2]) * (1.0 / 6.0) + odd * (1.0 / 12.0)


def turbine_sums(area_ref, field_ref, sums_ref, base):
    parts = [field_ref[OWN_ROWS, OWN_LANE + j : OWN_LANE + j + 128] for j in range(0, OWN_SPAN, 128)]
    for t in range(NTURB):
        total = None
        for j, part in enumerate(parts):
            lane = OWN_LANE + 128 * j
            term = area_ref[t, OWN_ROWS, lane : lane + 128] * part
            total = term if total is None else total + term
        sums_ref[base + t : base + t + 1, :] = jnp.sum(total, axis=0, keepdims=True)


def publish(sums_ref, out_ref):
    shape = sums_ref.shape
    total = jnp.broadcast_to(jnp.sum(sums_ref[...], axis=1, keepdims=True), shape)
    index = lax.broadcasted_iota(jnp.int32, shape, 0)
    picked = jnp.where(index == lax.broadcasted_iota(jnp.int32, shape, 1), total, 0.0)
    row = jnp.broadcast_to(jnp.sum(picked, axis=0, keepdims=True), (8, 128))
    for j in range(0, out_ref.shape[0], 8):
        out_ref[j : j + 8, :] = row


def totals(got_ref, base):
    row = jnp.sum(got_ref[...], axis=0, keepdims=True)
    index = lax.broadcasted_iota(jnp.int32, (NTURB, 128), 0) + base
    lane = lax.broadcasted_iota(jnp.int32, (NTURB, 128), 1)
    picked = jnp.where(index == lane, jnp.broadcast_to(row, (NTURB, 128)), 0.0)
    return jnp.broadcast_to(jnp.sum(picked, axis=1, keepdims=True), (NTURB, 128))


def weighted_area(area_ref, weight_ref, rows, lanes):
    total = None
    for t in range(NTURB):
        term = area_ref[t, rows, lanes] * weight_ref[t : t + 1, :]
        total = term if total is None else total + term
    return total


def split_three(value):
    high = value.astype(jnp.bfloat16)
    rest = value - high.astype(jnp.float32)
    middle = rest.astype(jnp.bfloat16)
    return high, middle, (rest - middle.astype(jnp.float32)).astype(jnp.bfloat16)


def area_kernel(x_ref, yz_ref, area_ref, out_ref):
    rows = lax.broadcasted_iota(jnp.int32, (RX, PTS), 0)
    columns = lax.broadcasted_iota(jnp.int32, (LANES, PTS), 0)

    def one(t, carry):
        point = pl.ds(t, 1)
        spots = jnp.where(rows == x_ref[point, :], area_ref[point, :], 0.0)
        left = jnp.concatenate(split_three(spots), axis=0)
        hot = jnp.where(columns == yz_ref[point, :], 1.0, 0.0).astype(jnp.bfloat16)
        product = lax.dot_general(
            left, hot, (((1,), (1,)), ((), ())), preferred_element_type=jnp.float32
        )
        out_ref[t] = product[:RX] + product[RX : 2 * RX] + product[2 * RX :]
        return carry

    lax.fori_loop(0, NTURB, one, 0)


def pack_x_kernel(field_hbm, cot_hbm, next_ref, prev_ref, field_ref, cot_ref, sems):
    first = pltpu.make_async_copy(field_hbm, field_ref, sems.at[0])
    second = pltpu.make_async_copy(cot_hbm, cot_ref, sems.at[1])
    first.start()
    second.start()
    first.wait()
    second.wait()
    half = OWN_SPAN // 2
    top = lax.broadcasted_iota(jnp.int32, (CX, half), 0) < CX // 2
    for i in range(19):
        low, high = cot_ref[i, :, :half], cot_ref[i, :, half:]
        next_ref[i, :, :OWN_SPAN] = field_ref[i]
        prev_ref[i, :, :OWN_SPAN] = field_ref[i]
        next_ref[i, :, OWN_SPAN:] = jnp.where(top, pltpu.roll(low, CX // 2, 0), high)
        prev_ref[i, :, OWN_SPAN:] = jnp.where(top, low, pltpu.roll(high, CX // 2, 0))


def pack_y_kernel(field_ref, cot_ref, before_ref, after_ref, fields_ref, cots_ref, next_ref, prev_ref):
    half = OWN_SPAN // 2
    top = lax.broadcasted_iota(jnp.int32, (CX, half), 0) < CX // 2
    left = lax.broadcasted_iota(jnp.int32, (CX, half), 1) < half // 2
    for i in range(19):
        for j, part in enumerate((before_ref[i, :, :OWN_SPAN], field_ref[i], after_ref[i, :, :OWN_SPAN])):
            rows = slice(CX * j, CX * (j + 1))
            fields_ref[i, rows] = part
            prev_ref[i, rows] = part[:, :half]
            next_ref[i, rows] = part[:, half:]
        before, after = before_ref[i, :, OWN_SPAN:], after_ref[i, :, OWN_SPAN:]
        low = (pltpu.roll(before, CX // 2, 0), cot_ref[i, :, :half], after)
        high = (before, cot_ref[i, :, half:], pltpu.roll(after, CX // 2, 0))
        for j in range(3):
            rows = slice(CX * j, CX * (j + 1))
            cots_ref[i, rows, :half] = low[j]
            cots_ref[i, rows, half:] = high[j]
        outer = jnp.where(top, low[2], low[0])
        prev_ref[i, RX:] = jnp.where(left, low[1], pltpu.roll(outer, half // 2, 1))
        outer = jnp.where(top, high[2], high[0])
        next_ref[i, RX:] = jnp.where(left, pltpu.roll(high[1], half // 2, 1), outer)


class Joined:
    def __init__(self, before, here, after):
        self.parts = before, here, after

    def __getitem__(self, index):
        before, here, after = self.parts
        return jnp.concatenate([before[index, :RX], here[index], after[index, :RX]], axis=1)


def first_kernel(before_ref, fields_ref, after_ref, cots_ref, area_ref, s_ref, v_ref, cot_ref, out_ref, sums):
    stream(Joined(before_ref, fields_ref, after_ref), s_ref)
    speeds(s_ref, v_ref)
    turbine_sums(area_ref, v_ref, sums, 0)
    publish(sums, out_ref)
    half = OWN_SPAN // 2
    for i in range(19):
        before, after = before_ref[i, RX:], after_ref[i, RX:]
        turned = pltpu.roll(before, half // 2, 1), pltpu.roll(after, half // 2, 1)
        for j in range(3):
            rows = slice(CX * j, CX * (j + 1))
            cot_ref[i, rows, :OWN_LANE] = turned[0] if j == 1 else before
            cot_ref[i, rows, OWN_LANE + OWN_SPAN :] = after if j == 1 else turned[1]
        cot_ref[i, :, OWN_LANE : OWN_LANE + OWN_SPAN] = cots_ref[i]


def forward_kernel(last, s_ref, v_ref, area_ref, inv_ref, got_ref, *rest):
    if last:
        cot_ref, next_ref, vn_ref, rotor_ref, out_ref, field, sums, drag = rest
    else:
        next_ref, vn_ref, rotor_ref, out_ref, field, sums = rest
    rotor_ref[...] = totals(got_ref, 0) * inv_ref[...]

    def one(rows, lanes):
        s = [s_ref[i, rows, lanes] for i in range(19)]
        force = weighted_area(area_ref, rotor_ref, rows, lanes) * v_ref[rows, lanes] * -THRUST
        for i, value in enumerate(collide(s, force)):
            field[i, rows, lanes] = value

    chunks(one)
    stream(field, next_ref)
    speeds(next_ref, vn_ref)
    turbine_sums(area_ref, vn_ref, sums, 0)
    if last:

        def other(rows, lanes):
            a = [cot_ref[i, rows, lanes] for i in range(19)]
            drag[rows, lanes] = push_back(a) * vn_ref[rows, lanes] * -THRUST

        chunks(other)
        turbine_sums(area_ref, drag, sums, NTURB)
    publish(sums, out_ref)


def adjoint_field(s_ref, a_ref, area_ref, rotor_ref, bar_ref, field):
    def one(rows, lanes):
        s = [s_ref[i, rows, lanes] for i in range(19)]
        a = [a_ref[i, rows, lanes] for i in range(19)]
        speed_bar = weighted_area(area_ref, rotor_ref, rows, lanes) * push_back(a) * -THRUST
        speed_bar = speed_bar + weighted_area(area_ref, bar_ref, rows, lanes)
        for i, value in enumerate(collide_adjoint(s, a, speed_bar)):
            field[i, rows, lanes] = value

    chunks(one)


def backward_kernel(first, sends, s_ref, a_ref, area_ref, inv_ref, got_ref, v_ref, *rest):
    rest = list(rest)
    rotor_ref = None if first else rest.pop(0)
    out_ref, drag_ref, bar_ref = rest[:3]
    field, sums = rest[-2:]
    if first:
        rotor_ref = rest[-3]
        rotor_ref[...] = totals(got_ref, 0) * inv_ref[...]
    bar_ref[...] = totals(got_ref, NTURB if first else 0) * inv_ref[...]
    adjoint_field(s_ref, a_ref, area_ref, rotor_ref, bar_ref, field)
    stream_adjoint(field, out_ref)

    def other(rows, lanes):
        a = [out_ref[i, rows, lanes] for i in range(19)]
        drag_ref[rows, lanes] = push_back(a) * v_ref[rows, lanes] * -THRUST

    chunks(other)
    if sends:
        turbine_sums(area_ref, drag_ref, sums, 0)
        publish(sums, rest[3])


def last_kernel(s_ref, a_ref, area_ref, rotor_ref, point_ref, size_ref, inv_ref, out_ref, grad_ref, field, result, bar):
    known, swing, slope = (point_ref[NTURB * j : NTURB * (j + 1), :] for j in range(3))
    total = jnp.sum(size_ref[...] * swing[:, :PTS], axis=1, keepdims=True)
    grad = known + total * slope
    turned = [grad] + [pltpu.roll(grad, 128 - PTS // 3 * j, 1) for j in (1, 2, 3)]
    lane = lax.broadcasted_iota(jnp.int32, (1, 128), 1)
    for m in range(NTURB // 4):
        for j in range(3):
            row = 4 * m + j
            first, second = turned[j][row : row + 1], turned[j + 1][row + 1 : row + 2]
            grad_ref[3 * m + j : 3 * m + j + 1, :] = jnp.where(lane < 128 - 32 * (j + 1), first, second)
    bar[...] = jnp.broadcast_to(total, (NTURB, 128)) * inv_ref[...]
    adjoint_field(s_ref, a_ref, area_ref, rotor_ref, bar, field)
    stream_adjoint(field, result)
    for i in range(19):
        out_ref[i] = result[i, OWN_ROWS, OWN_LANE : OWN_LANE + OWN_SPAN]


def gather_kernel(x_ref, yz_ref, cot_ref, q1, q2, q3, v1, v2, v3, v4, u1, u2, u3, u4, n2, n3, n4, inv, out_ref):
    own = (OWN_ROWS, slice(OWN_LANE, OWN_LANE + OWN_SPAN))
    v = [ref[own] for ref in (v1, v2, v3, v4)]
    q = [ref[own] for ref in (q1, q2, q3)]
    a = [cot_ref[(i,) + own] for i in range(19)]
    q.append(push_back(a) * v[3] * -THRUST)
    rows = lax.broadcasted_iota(jnp.int32, (CX, PTS), 0) + MARGIN
    columns = lax.broadcasted_iota(jnp.int32, (OWN_SPAN, PTS), 0) + OWN_LANE

    def wide(ref, t):
        return jnp.concatenate([ref[pl.ds(t, 1), :]] * (OWN_SPAN // 128), axis=1)

    out_ref[...] = jnp.zeros_like(out_ref)

    def one(t, carry):
        u = [wide(ref, t) for ref in (u1, u2, u3, u4)]
        n = [None] + [wide(ref, t) for ref in (n2, n3, n4)]
        known = u[0] * q[0]
        for k in range(1, 4):
            known = known + u[k] * q[k] + n[k] * (v[k] - u[k])
        fields = [known, q[0], (v[0] - u[0]) * wide(inv, t)]
        left = jnp.concatenate(split_three(jnp.concatenate(fields, axis=0)), axis=0)
        hot = jnp.where(columns == yz_ref[pl.ds(t, 1), :], 1.0, 0.0).astype(jnp.bfloat16)
        product = jnp.dot(left, hot, preferred_element_type=jnp.float32)
        size = 3 * CX
        product = product[:size] + product[size : 2 * size] + product[2 * size :]
        mine = rows == x_ref[pl.ds(t, 1), :]
        for j in range(3):
            picked = jnp.where(mine, product[CX * j : CX * (j + 1)], 0.0)
            out_ref[pl.ds(j * NTURB + t, 1), 0:PTS] = jnp.sum(picked, axis=0, keepdims=True)
        return carry

    lax.fori_loop(0, NTURB, one, 0, unroll=True)


def call(kernel, outs, scratch, *args):
    vmem = pl.BlockSpec(memory_space=pltpu.VMEM)
    return pl.pallas_call(
        kernel,
        out_shape=[jax.ShapeDtypeStruct(shape, jnp.float32) for shape in outs],
        in_specs=[vmem] * len(args),
        out_specs=[vmem] * len(outs),
        scratch_shapes=[pltpu.VMEM(shape, jnp.float32) for shape in scratch],
        compiler_params=pltpu.CompilerParams(vmem_limit_bytes=VMEM_LIMIT),
    )(*args)


def route(value, target):
    size_x, size_y = lax.axis_size("gx"), lax.axis_size("gy")
    pairs = []
    for i in range(size_x):
        for j in range(size_y):
            to = target(i, j)
            if to is not None:
                pairs.append((i * size_y + j, to[0] % size_x * size_y + to[1] % size_y))
    return lax.ppermute(value, ("gx", "gy"), pairs)


def swap(value):
    return route(value, lambda i, j: (i ^ 1, j))


def exchange(rows):
    return lax.all_to_all(rows, ("gx", "gy"), 0, 0, tiled=True)


def merge_kernel(*refs):
    value = refs[0][...]
    for ref in refs[1:-1]:
        value = jnp.where(value != 0.0, value, ref[...])
    refs[-1][...] = value


def merge(value, parts):
    (value,) = call(merge_kernel, [value.shape], [], value, *parts)
    return value


def spread(value):
    size_x, size_y = lax.axis_size("gx"), lax.axis_size("gy")
    half = size_y // 2

    def across(first, second):
        def target(i, j):
            dy, dz = second if i % 2 else first
            return i, (j // half + dz) % 2 * half + (j % half + dy) % half

        return target

    def along(block, step, first, second):
        def target(i, j):
            move = second if i % 2 else first
            if move is None:
                return None
            return i // block * block + (i % block + move * step) % block, j

        return target

    value = merge(value, [swap(value)])
    turns = [((1, 0), (1, 1)), ((3, 0), (3, 1)), ((2, 0), (2, 1)), ((0, 1), (0, 1))]
    value = merge(value, [route(value, across(*turn)) for turn in turns])
    value = merge(value, [swap(value)])
    for block, step in ((8, 2), (size_x, 8)):
        turns = [(1, 2), (3, None)]
        value = merge(value, [route(value, along(block, step, *turn)) for turn in turns])
        value = merge(value, [swap(value)])
    return value


def shift(value, axis, step):
    size = lax.axis_size(axis)
    return lax.ppermute(value, axis, [(i, (i + step) % size) for i in range(size)])


def region(checkpoint, cotangent, ready):
    wide = (19, CX, OWN_SPAN + OWN_SPAN // 2)
    right, left = pl.pallas_call(
        pack_x_kernel,
        out_shape=[jax.ShapeDtypeStruct(wide, jnp.float32)] * 2,
        in_specs=[pl.BlockSpec(memory_space=pltpu.HBM)] * 2,
        out_specs=[pl.BlockSpec(memory_space=pltpu.VMEM)] * 2,
        scratch_shapes=[pltpu.VMEM(checkpoint.shape, jnp.float32)] * 2 + [pltpu.SemaphoreType.DMA((2,))],
        compiler_params=pltpu.CompilerParams(vmem_limit_bytes=60 * 1024 * 1024),
    )(checkpoint, cotangent)
    before, after = shift(right, "gx", 1), shift(left, "gx", -1)
    before, after, *ready = lax.optimization_barrier((before, after) + ready)
    stack, edge = (19, RX, OWN_SPAN), (19, RX + CX, OWN_SPAN // 2)
    fields, cots, right, left = call(
        pack_y_kernel, [stack, stack, edge, edge], [], checkpoint, cotangent, before, after
    )
    return (shift(right, "gy", 1), fields, shift(left, "gy", -1), cots), ready


def body(checkpoint, cotangent, blade_area, hub_tile, point_side, point_local):
    count_x, count_y = lax.axis_size("gx"), lax.axis_size("gy")
    index_x, index_y = lax.axis_index("gx"), lax.axis_index("gy")
    area = blade_area.reshape(NTURB, PTS)
    side = point_side.reshape(NTURB, PTS)
    local = point_local.reshape(NTURB, PTS)
    hub = hub_tile.reshape(NTURB, 1)
    cell_x = (hub // count_y + side // 3 - 1 - index_x) * CX + local // (CY * NZ) + MARGIN
    cell_y = (hub % count_y + side % 3 - 1 - index_y) * CY + local // NZ % CY + MARGIN
    cell_x = cell_x % (count_x * CX)
    cell_y = cell_y % (count_y * CY)
    inside = (cell_x < RX) & (cell_y < RY)
    cell_x = jnp.where(inside, cell_x, -1)
    cell_yz = jnp.where(inside, cell_y * NZ + local % NZ, -1)
    mine_y = (cell_y >= MARGIN) & (cell_y < MARGIN + CY)
    inverse = jnp.broadcast_to(1.0 / jnp.sum(area, 1, keepdims=True), (NTURB, 128))

    full = (19, RX, LANES)
    flat = (RX, LANES)
    row = (NTURB, 128)
    (spots,) = call(area_kernel, [(NTURB,) + flat], [], cell_x, cell_yz, area)
    own_yz = jnp.where(mine_y, cell_yz, -1)
    parts, ready = region(checkpoint, cotangent, (spots, cell_x, own_yz, area, inverse))
    spots, cell_x, own_yz, area, inverse = ready

    s, v, rotor = [None] * 5, [None] * 5, [None] * 5
    every = (count_x * count_y, 128)
    s[1], v[1], cot, sums = call(first_kernel, [full, flat, full, every], [row], *parts, spots)
    for k in (1, 2, 3):
        last = k == 3
        s[k + 1], v[k + 1], rotor[k], sums = call(
            functools.partial(forward_kernel, last),
            [full, flat, row, every],
            [full, (2 * NTURB, 128) if last else row] + ([flat] if last else []),
            *([s[k], v[k], spots, inverse, exchange(sums)] + ([cot] if last else [])),
        )
    adjoint = cot
    bar, drag = [None] * 5, [None] * 5
    for k in (4, 3, 2):
        first, sends = k == 4, k > 2
        args = [s[k], adjoint, spots, inverse, exchange(sums), v[k - 1]]
        outs = call(
            functools.partial(backward_kernel, first, sends),
            [full, flat, row] + ([every] if sends else []) + ([row] if first else []),
            [full, row],
            *(args + ([] if first else [rotor[k]])),
        )
        adjoint, drag[k - 1], bar[k] = outs[:3]
        sums = outs[3] if sends else None
        if first:
            rotor[4] = outs[4]
    (points,) = call(
        gather_kernel,
        [(3 * NTURB, 128)],
        [],
        *([cell_x, own_yz, cot] + drag[1:4] + v[1:] + rotor[1:] + bar[2:] + [inverse]),
    )
    grad, grad_area = call(
        last_kernel,
        [(19, CX, CY * NZ), (NTURB * PTS // 128, 128)],
        [full, full, row],
        *(s[1], adjoint, spots, rotor[1], spread(points), area, inverse),
    )
    return grad, grad_area.reshape(-1)


def solution(mesh):
    return jax.shard_map(
        body,
        mesh=mesh,
        in_specs=(P(None, "gx", "gy"), P(None, "gx", "gy"), P(), P(), P(), P()),
        out_specs=(P(None, "gx", "gy"), P()),
        check_vma=False,
    )
```
